32 devices in a mesh: arc: 8 (over z, x), vec: 4 (over y, core).
Axes of the slice: x: 2, y: 2, z: 4, core: 2. Of those that a mesh axis runs over, the one named last changes fastest.
Arguments:
- right_side: float32 [640, 128, 128], P(('arc', 'vec')), may hold values from -6 to 6
- prior_diag: float32 [640, 128], P(('arc', 'vec')), may hold values from 0.5 to 4
- inv_factor: bfloat16 [512, 256, 256], P(('arc', 'vec'))
- coupling_panel: bfloat16 [512, 256, 1024], P(('arc', 'vec')), may hold values from -0.09375 to 0.09375
- coupling_owner: int32 [512, 8], replicated, may hold values from 0 to 31, all different within a row; in each aligned block of 16 rows (0 to 15, 16 to 31, ...) at most 5 rows name the same one
- coupling_block: int32 [512, 8], replicated, may hold values from 0 to 19
Outputs:
- solution_field: float32 [640, 128, 128], P(('arc', 'vec'))
- residual: float32 [640, 128, 128], P(('arc', 'vec'))
The draws below stay inside these ranges and needn't reach their ends.
Inputs may be any that keep to these rules, and one draw needn't show every extreme that they name: `coupling_owner`: the 8 holders named for one arc are different. Among the 16 arcs of one device (aligned blocks of rows) no holder is named more than 5 times; some holder is named exactly 5 times.
All inputs are finite; a program needn't handle non-finite values.
Results may differ from the reference program's by a relative error of at most 0.006.
The reference program's roundings to bfloat16 on the way count: a program that leaves them out, or rounds other values in their place, can miss the bound.
Values may be sent and summed in bfloat16 or wider, within the bound.
No kernel may reach another device: no remote copies, remote signals or barrier semaphores. Data moves between devices by JAX's collectives and lax.ppermute only.
A program may use at most 128 MiB of HBM per device.

```python
import math
import jax
import jax.numpy as jnp
import numpy as np
from jax import lax

BR = 128
GBLK = 640
AP = 256
RHS = 128
K = 8
ITERS = 2
ARC_DEV = 16
ARCS = 512
BLK_DEV = 20
CAP = 5
DEVICES = 32


def draw_inv_factor(key, part):
    key_diag, key_below = jax.random.split(key)
    diagonal_part = jax.random.uniform(key_diag, (ARCS, AP), jnp.float32, 0.7, 1.3)
    below_part = jax.random.normal(key_below, (ARCS, AP, AP), jnp.float32) * (0.5 / math.sqrt(AP))
    strict_lower = jnp.tril(jnp.ones((AP, AP), jnp.float32), -1)
    identity = jnp.eye(AP, dtype=jnp.float32)
    full_factor = below_part * strict_lower[None] + diagonal_part[:, :, None] * identity[None]
    return full_factor.astype(jnp.bfloat16)


def place_ends(array, stream_key, low, largest):
    longest = array.shape.index(max(array.shape))
    spots = []
    for shift in (0, 1):
        where = [jax.random.randint(jax.random.fold_in(stream_key, axis), (), 0, length) for axis, length in enumerate(array.shape)]
        where[longest] = (where[longest] + shift) % array.shape[longest]
        spots.append(tuple(where))
    return array.at[spots[0]].set(low).at[spots[1]].set(largest)


def block_scale(rng, dims, cuts, least, top_value):
    level = 1.0
    for dim, parts in cuts:
        draws = jax.random.uniform(jax.random.fold_in(jax.random.fold_in(rng, 6), dim), (parts,), jnp.float32, least / len(cuts), top_value / len(cuts))
        level = level * jnp.repeat(jnp.exp(draws), dims[dim] // parts).reshape((-1,) + (1,) * (len(dims) - 1 - dim))
    return level


def routed_block(rng, own, number, rows, count, top, reach, skew):
    ranking = jax.random.permutation(rng, count)
    heavy_load, usual = shares(count, rows * top, reach, skew, True), shares(count, rows * top, reach, skew, False)
    places = jnp.arange(count)

    def named(lengths, turn):
        used = int((lengths > 0).sum())
        fixed = max(1, used // 4)
        passed = fixed + (places - fixed + turn * (used - fixed)) % max(1, count - fixed)
        return jnp.zeros((count,), jnp.int32).at[ranking[jnp.where(places < fixed, places, passed)]].set(jnp.asarray(lengths, jnp.int32))

    lengths = jnp.where(number % 4 == 0, named(heavy_load, number // 4), named(usual, number - number // 4 - 1))
    mixed = jax.random.permutation(jax.random.fold_in(own, 3), count)
    giver, taker = mixed[0:count // 2 * 2:2], mixed[1:count // 2 * 2:2]
    slack = jnp.minimum(lengths[giver] - 1, reach - lengths[taker]) // 2
    slack = jnp.where((giver == ranking[0]) | (taker == ranking[0]) | (lengths[taker] == 0), 0, jnp.maximum(slack, 0))
    passed = jax.random.randint(jax.random.fold_in(own, 4), (count // 2,), 0, 1 << 20) % (slack + 1)
    lengths = lengths.at[giver].add(-passed).at[taker].add(passed)
    labels = jnp.searchsorted(jnp.cumsum(lengths), jnp.arange(rows * top), side="right").astype(jnp.int32)
    listing = labels.reshape(top, rows).T
    listing = listing[jax.random.permutation(jax.random.fold_in(own, 1), rows)]
    turn = jax.random.randint(jax.random.fold_in(own, 2), (rows, 1), 0, top)
    return jnp.take_along_axis(listing, (jnp.arange(top)[None, :] + turn) % top, axis=1)


def shares(amount, total, reach, skew, full):
    weights = [(1 << 20) // math.isqrt(grade ** skew) + 1 for grade in range(1, amount + 1)]
    largest = reach if full else min(reach, max(-(-total // amount), total * weights[0] // sum(weights)))
    least = 1 if total - largest >= amount - 1 else 0
    holding, surplus = [largest] + [least] * (amount - 1), total - largest - least * (amount - 1)
    while surplus > 0:
        candidates = [i for i in range(1, amount) if holding[i] < largest] or [i for i in range(1, amount) if holding[i] < reach]
        whole, left = sum([weights[i] for i in candidates]), surplus
        for i in candidates:
            extra = min(reach - holding[i], max(1, left * weights[i] // whole), surplus)
            holding[i] = holding[i] + extra
            surplus = surplus - extra
    return np.array(holding)


def bell_draw(key, shape, width, reach, cuts=(), kind=jnp.bfloat16):
    level = block_scale(key, shape, cuts, -0.22, 0.18) if cuts else 1.0
    array = jax.random.normal(key, shape, jnp.float32) * width * level
    return jnp.minimum(jnp.maximum(array, -reach), reach).astype(kind)


def setup_inputs(seed: int = 0) -> dict:
    seeds = jax.random.split(jax.random.key(seed), 7)
    right_side = bell_draw(seeds[0], (GBLK, BR, RHS), 1.0, 6.0, ((0, 32),), jnp.float32)
    prior_diag = jnp.clip(jnp.exp(math.log(4.0) - 2.0794415 * jax.random.uniform(seeds[1], (GBLK, BR), jnp.float32) ** block_scale(seeds[1], (GBLK, BR), ((0, 32),), -0.2, 0.2)), 0.5, 4.0)
    inv_factor = draw_inv_factor(jax.random.fold_in(seeds[6], 71), 0)
    coupling_panel = bell_draw(seeds[3], (ARCS, AP, K * BR), (K * BR * 4) ** -0.5, 0.09375, ((0, 32),))
    coupling_owner_keys = jax.random.split(jax.random.fold_in(seeds[4], 1), ARCS // ARC_DEV)
    coupling_owner_turns = jax.random.permutation(jax.random.fold_in(seeds[4], 3), ARCS // ARC_DEV)
    coupling_owner = jax.vmap(lambda own, number: routed_block(jax.random.fold_in(seeds[4], 2), own, number, ARC_DEV, DEVICES, K, CAP, 2))(coupling_owner_keys, coupling_owner_turns).reshape((ARCS, K))
    coupling_block = place_ends(jax.random.randint(seeds[5], (ARCS, K), 0, BLK_DEV), jax.random.fold_in(seeds[5], 1), 0, BLK_DEV - 1).astype(jnp.int32)
    return {"right_side": right_side, "prior_diag": prior_diag, "inv_factor": inv_factor, "coupling_panel": coupling_panel, "coupling_owner": coupling_owner, "coupling_block": coupling_block}


def round_bf16(values):
    return lax.optimization_barrier(values.astype(jnp.bfloat16)).astype(jnp.float32)

def inner_gram(left, right):
    return jnp.einsum('grc,grd->cd', left, right, precision=lax.Precision.HIGHEST)

def combine_cols(field, weights):
    return jnp.einsum('grc,cd->grd', field, weights, precision=lax.Precision.HIGHEST)

def apply_schur(field, prior_diag, inv_factor, coupling_panel, global_index):
    rounded = round_bf16(field)
    factor_groups = inv_factor.reshape(DEVICES, ARC_DEV, AP, AP)
    panel_groups = coupling_panel.reshape(DEVICES, ARC_DEV, AP, K * BR)
    index_groups = global_index.reshape(DEVICES, ARC_DEV * K)

    def arc_group(summed, group_data):
        factor_part, panel_part, group_index = group_data
        factor_f32 = factor_part.astype(jnp.float32)
        panel_f32 = panel_part.astype(jnp.float32)
        fetched = rounded[group_index].reshape(ARC_DEV, K * BR, RHS)
        coupled = round_bf16(jnp.einsum('apk,akc->apc', panel_f32, fetched, precision=lax.Precision.HIGHEST))
        whitened = round_bf16(jnp.einsum('apq,aqc->apc', factor_f32, coupled, precision=lax.Precision.HIGHEST))
        smoothed = round_bf16(jnp.einsum('aqp,aqc->apc', factor_f32, whitened, precision=lax.Precision.HIGHEST))
        projected = round_bf16(jnp.einsum('apk,apc->akc', panel_f32, smoothed, precision=lax.Precision.HIGHEST))
        summed = summed.at[group_index].add(projected.reshape(ARC_DEV * K, BR, RHS))
        return (summed, None)
    start = jnp.zeros((GBLK, BR, RHS), jnp.float32)
    summed, _ = lax.scan(arc_group, start, (factor_groups, panel_groups, index_groups))
    return prior_diag[:, :, None] * field + summed

def reference(right_side, prior_diag, inv_factor, coupling_panel, coupling_owner, coupling_block):
    global_index = (coupling_owner * BLK_DEV + coupling_block).astype(jnp.int32)
    solution_field = jnp.zeros_like(right_side)
    residual = right_side
    direction = right_side
    res_gram = inner_gram(residual, residual)
    for sweep_index in range(ITERS):
        image_vec = apply_schur(direction, prior_diag, inv_factor, coupling_panel, global_index)
        curv_gram = inner_gram(direction, image_vec)
        factor_low = jnp.linalg.cholesky(curv_gram)
        step_mat = jax.scipy.linalg.cho_solve((factor_low, True), res_gram)
        solution_field = solution_field + combine_cols(direction, step_mat)
        residual = residual - combine_cols(image_vec, step_mat)
        if sweep_index + 1 < ITERS:
            new_gram = inner_gram(residual, residual)
            beta_mat = jax.scipy.linalg.cho_solve((jnp.linalg.cholesky(res_gram), True), new_gram)
            direction = residual + combine_cols(direction, beta_mat)
            res_gram = new_gram
    return (solution_field, residual)
```

```python
import jax
import jax.numpy as jnp
from jax import lax
from jax.sharding import PartitionSpec as P

ITERS = 2


def inner_gram(left, right):
    return jnp.einsum("grc,grd->cd", left, right, precision=lax.Precision.HIGHEST)


def combine_cols(field, weights):
    return jnp.einsum("grc,cd->grd", field, weights, precision=lax.Precision.HIGHEST)


def times_high(left, right):
    return jnp.dot(left, right, precision=lax.Precision.HIGHEST)


def trade_out(buffer):
    return lax.all_to_all(buffer, ("arc", "vec"), split_axis=0, concat_axis=0, tiled=True)


def trade_back(buffer):
    return lax.all_to_all(buffer, ("arc", "vec"), split_axis=0, concat_axis=0, tiled=True)


def sum_all(grams):
    device_count = lax.axis_size(("arc", "vec"))
    stacked = jnp.concatenate(grams, axis=0)
    rows, cols = stacked.shape
    pieces = stacked.reshape(device_count, rows // device_count, cols)
    mine = jnp.sum(trade_out(pieces), axis=0)
    shared = jnp.broadcast_to(mine[None], pieces.shape)
    total = trade_out(shared).reshape(len(grams), rows // len(grams), cols)
    return [total[i] for i in range(len(grams))]


def per_device(right_side, prior_diag, inv_factor, coupling_panel, coupling_owner, coupling_block):
    device_count = lax.axis_size(("arc", "vec"))
    my_index = lax.axis_index(("arc", "vec"))
    arcs_here = coupling_panel.shape[0]
    links = coupling_owner.shape[1]
    blocks_here = right_side.shape[0]
    block_rows = right_side.shape[1]
    rhs_count = right_side.shape[2]
    entries = arcs_here * links
    slot_count = (entries + device_count - 1) // device_count + 1
    owner_all = coupling_owner.reshape(device_count, entries)
    block_all = coupling_block.reshape(device_count, entries)
    position = jnp.arange(entries, dtype=jnp.int32)
    earlier = (owner_all[:, :, None] == owner_all[:, None, :]) & (
        position[None, None, :] < position[None, :, None]
    )
    rank_all = jnp.sum(earlier.astype(jnp.int32), axis=2)
    owner_mine = lax.dynamic_index_in_dim(owner_all, my_index, 0, keepdims=False)
    rank_mine = lax.dynamic_index_in_dim(rank_all, my_index, 0, keepdims=False)
    slot_mine = owner_mine * slot_count + rank_mine
    slot_ids = jnp.arange(slot_count, dtype=jnp.int32)
    matches = (owner_all[:, None, :] == my_index) & (
        rank_all[:, None, :] == slot_ids[None, :, None]
    )
    filled = jnp.any(matches, axis=2).reshape(-1)
    source_block = jnp.sum(jnp.where(matches, block_all[:, None, :], 0), axis=2).reshape(-1)
    block_ids = jnp.arange(blocks_here, dtype=jnp.int32)
    selector = ((source_block[:, None] == block_ids[None, :]) & filled[:, None]).astype(
        jnp.bfloat16
    )
    solution_field = jnp.zeros_like(right_side)
    residual = right_side
    direction = right_side
    (res_gram,) = sum_all([inner_gram(residual, residual)])
    for sweep_index in range(ITERS):
        local_rounded = direction.astype(jnp.bfloat16)
        outgoing = jnp.where(
            filled[:, None, None], local_rounded[source_block], jnp.zeros((), jnp.bfloat16)
        )
        arrived = trade_out(outgoing)
        fetched = arrived[slot_mine].reshape(arcs_here, links * block_rows, rhs_count)
        coupled = jnp.einsum(
            "apk,akc->apc", coupling_panel, fetched, preferred_element_type=jnp.float32
        ).astype(jnp.bfloat16)
        whitened = jnp.einsum(
            "apq,aqc->apc", inv_factor, coupled, preferred_element_type=jnp.float32
        ).astype(jnp.bfloat16)
        smoothed = jnp.einsum(
            "aqp,aqc->apc", inv_factor, whitened, preferred_element_type=jnp.float32
        ).astype(jnp.bfloat16)
        projected = jnp.einsum(
            "apk,apc->akc", coupling_panel, smoothed, preferred_element_type=jnp.float32
        ).astype(jnp.bfloat16)
        projected = projected.reshape(entries, block_rows, rhs_count)
        returning = (
            jnp.zeros((device_count * slot_count, block_rows, rhs_count), jnp.bfloat16)
            .at[slot_mine]
            .set(projected)
        )
        came_back = trade_back(returning)
        summed = jnp.einsum("sb,src->brc", selector, came_back, preferred_element_type=jnp.float32)
        image_vec = prior_diag[:, :, None] * direction + summed
        last = sweep_index + 1 == ITERS
        if last:
            (curv_gram,) = sum_all([inner_gram(direction, image_vec)])
        else:
            curv_gram, image_gram, cross_gram = sum_all(
                [
                    inner_gram(direction, image_vec),
                    inner_gram(image_vec, image_vec),
                    inner_gram(residual, image_vec),
                ]
            )
        factor_low = jnp.linalg.cholesky(curv_gram)
        step_mat = jax.scipy.linalg.cho_solve((factor_low, True), res_gram)
        solution_field = solution_field + combine_cols(direction, step_mat)
        residual = residual - combine_cols(image_vec, step_mat)
        if sweep_index + 1 < ITERS:
            new_gram = (
                res_gram - times_high(step_mat.T, cross_gram.T) - times_high(cross_gram, step_mat)
            )
            new_gram = new_gram + times_high(step_mat.T, times_high(image_gram, step_mat))
            beta_mat = jax.scipy.linalg.cho_solve((jnp.linalg.cholesky(res_gram), True), new_gram)
            direction = residual + combine_cols(direction, beta_mat)
            res_gram = new_gram
    return (solution_field, residual)


def solution(mesh):
    in_specs = (
        P(("arc", "vec"), None, None),
        P(("arc", "vec"), None),
        P(("arc", "vec"), None, None),
        P(("arc", "vec"), None, None),
        P(),
        P(),
    )
    out_specs = (P(("arc", "vec"), None, None), P(("arc", "vec"), None, None))
    return jax.shard_map(
        per_device, mesh=mesh, in_specs=in_specs, out_specs=out_specs, check_vma=False
    )
```

```python
import functools

import jax
import jax.numpy as jnp
from jax import lax
from jax.experimental import pallas as pl
from jax.experimental.pallas import tpu as pltpu
from jax.sharding import PartitionSpec as P

ITERS = 2
AXES = ("arc", "vec")
SMEM = pltpu.MemorySpace.SMEM
VMEM = pltpu.MemorySpace.VMEM


def inner_gram(left, right):
    return jnp.einsum("grc,grd->cd", left, right, precision=lax.Precision.HIGHEST)


def combine_cols(field, weights):
    return jnp.einsum("grc,cd->grd", field, weights, precision=lax.Precision.HIGHEST)


def times_high(left, right):
    return jnp.dot(left, right, precision=lax.Precision.HIGHEST)


def trade(buffer):
    return lax.all_to_all(buffer, AXES, split_axis=0, concat_axis=0, tiled=True)


def sum_all(grams):
    device_count = lax.axis_size(AXES)
    stacked = jnp.concatenate(grams, axis=0)
    rows, cols = stacked.shape
    pieces = stacked.reshape(device_count, rows // device_count, cols)
    mine = jnp.sum(trade(pieces), axis=0)
    shared = jnp.broadcast_to(mine[None], pieces.shape)
    total = trade(shared).reshape(len(grams), rows // len(grams), cols)
    return [total[i] for i in range(len(grams))]


class Plan:
    def __init__(self, mesh, arcs_here, links, blocks_here):
        arc, vec = mesh.shape["arc"], mesh.shape["vec"]
        half = max(1, vec // 2)
        self.rings = arc // half if arc % half == 0 else arc
        self.devices = arc * vec
        self.plane = self.devices // self.rings
        self.arcs, self.links, self.blocks = arcs_here, links, blocks_here
        entries = arcs_here * links
        self.cap = (entries + self.devices - 1) // self.devices + 1
        self.slots = self.plane * self.cap
        self.pos_row = self.slots
        self.own_row = self.slots + arcs_here
        self.rows = self.slots + 2 * arcs_here
        self.order = [self.plane_at(i) for i in range(self.rings)]
        self.ring = [
            (self.order[i] * self.plane + p, self.order[(i + 1) % self.rings] * self.plane + p)
            for i in range(self.rings)
            for p in range(self.plane)
        ]
        self.groups = [
            [z * self.plane + p for p in range(self.plane)] for z in range(self.rings)
        ]

    def plane_at(self, place):
        return 2 * place if 2 * place < self.rings else 2 * self.rings - 1 - 2 * place

    def place_of(self, z):
        half = lax.div(z, 2)
        return jnp.where(lax.rem(z, 2) == 0, half, self.rings - 1 - half)

    def source_plane(self, me, step):
        place = self.place_of(lax.div(me, self.plane))
        place = lax.rem(place - step + self.rings, self.rings)
        doubled = 2 * place
        return jnp.where(doubled < self.rings, doubled, 2 * self.rings - 1 - doubled)


def tables_kernel(plan, me_ref, owner_ref, block_ref, tab_ref):
    me = me_ref[0]
    arcs, links, lanes = plan.arcs, plan.links, tab_ref.shape[1]
    z = lax.div(me, plan.plane)
    owners = lax.broadcasted_iota(jnp.int32, (arcs, lanes), 1)
    low = lax.broadcasted_iota(jnp.int32, (arcs, arcs), 0)
    high = lax.broadcasted_iota(jnp.int32, (arcs, arcs), 1)
    before = (high < low).astype(jnp.float32)

    def incidence(row):
        owner = owner_ref[pl.ds(row, arcs), :]
        block = block_ref[pl.ds(row, arcs), :]
        named = jnp.zeros((arcs, lanes), jnp.float32)
        held = jnp.zeros((arcs, lanes), jnp.int32)
        for k in range(links):
            same = owner[:, k : k + 1] == owners
            named = jnp.where(same, 1.0, named)
            held = jnp.where(same, block[:, k : k + 1] + 1, held)
        rank = jnp.dot(before, named, preferred_element_type=jnp.float32).astype(jnp.int32)
        return held, rank

    for q in range(plan.plane):
        row = pl.multiple_of((z * plan.plane + q) * arcs, arcs)
        held, rank = incidence(row)
        for r in range(plan.cap):
            at_rank = jnp.where(rank == r, held, 0)
            tab_ref[r * plan.plane + q : r * plan.plane + q + 1, :] = jnp.sum(
                at_rank, axis=0, keepdims=True
            )
    row = pl.multiple_of(me * arcs, arcs)
    held, rank = incidence(row)
    place = plan.place_of(z)
    other = plan.place_of(lax.div(owners, plan.plane))
    step = lax.rem(place - other + plan.rings, plan.rings)
    slot = step * plan.slots + lax.rem(owners, plan.plane) * plan.cap + rank
    tab_ref[plan.pos_row : plan.pos_row + arcs, :] = slot
    mine = jnp.zeros((arcs, lanes), jnp.int32)
    owner = owner_ref[pl.ds(row, arcs), :]
    for k in range(links):
        mine = jnp.where(owners == k, owner[:, k : k + 1], mine)
    tab_ref[plan.own_row : plan.own_row + arcs, :] = mine


def make_tables(plan, me, coupling_owner, coupling_block):
    lanes = -(-plan.devices // 128) * 128
    return pl.pallas_call(
        functools.partial(tables_kernel, plan),
        out_shape=jax.ShapeDtypeStruct((plan.rows, lanes), jnp.int32),
        in_specs=[
            pl.BlockSpec(memory_space=SMEM),
            pl.BlockSpec(memory_space=VMEM),
            pl.BlockSpec(memory_space=VMEM),
        ],
        out_specs=pl.BlockSpec(memory_space=VMEM),
        name="tables",
    )(me, coupling_owner, coupling_block)


def pick_kernel(plan, step, me_ref, tab_ref, chunk_ref, out_ref):
    me = me_ref[0]
    column = plan.source_plane(me, step) * plan.plane + lax.rem(me, plan.plane)

    @pl.loop(0, plan.plane)
    def _(q):
        for r in range(plan.cap):
            block = jnp.maximum(tab_ref[r * plan.plane + q, column] - 1, 0)
            out_ref[q * plan.cap + r] = chunk_ref[block]


def pick(plan, step, me, tab, chunk):
    shape = (plan.slots,) + chunk.shape[1:]
    return pl.pallas_call(
        functools.partial(pick_kernel, plan, step),
        out_shape=jax.ShapeDtypeStruct(shape, chunk.dtype),
        in_specs=[
            pl.BlockSpec(memory_space=SMEM),
            pl.BlockSpec(memory_space=SMEM),
            pl.BlockSpec(memory_space=VMEM),
        ],
        out_specs=pl.BlockSpec(memory_space=VMEM),
        name="pick",
    )(me, tab, chunk)


def arcs_kernel(plan, tab_ref, *refs):
    rings, slots = plan.rings, plan.slots
    arrived_refs = refs[:rings]
    panel_ref, factor_ref = refs[rings], refs[rings + 1]
    out_refs = refs[rings + 2 : 2 * rings + 2]
    arrived, leaving, fetched, sems = refs[2 * rings + 2 :]
    arc = pl.program_id(0)
    rows = arrived.shape[1]

    def inward(s):
        return pltpu.make_async_copy(
            arrived_refs[s], arrived.at[pl.ds(s * slots, slots)], sems.at[s]
        )

    def outward(s):
        return pltpu.make_async_copy(
            leaving.at[pl.ds(s * slots, slots)], out_refs[s], sems.at[s]
        )

    @pl.when(arc == 0)
    def _():
        for s in range(rings):
            inward(s).start()
        for s in range(rings):
            inward(s).wait()

    spots = []
    for k in range(plan.links):
        spot = tab_ref[plan.pos_row + arc, tab_ref[plan.own_row + arc, k]]
        spots.append(spot)
        fetched[k * rows : (k + 1) * rows, :] = arrived[spot]
    panel, factor = panel_ref[0], factor_ref[0]
    coupled = jnp.dot(panel, fetched[...], preferred_element_type=jnp.float32)
    coupled = coupled.astype(jnp.bfloat16)
    whitened = jnp.dot(factor, coupled, preferred_element_type=jnp.float32)
    whitened = whitened.astype(jnp.bfloat16)
    smoothed = lax.dot_general(
        whitened, factor, (((0,), (0,)), ((), ())), preferred_element_type=jnp.float32
    ).astype(jnp.bfloat16)
    projected = jnp.dot(smoothed, panel, preferred_element_type=jnp.float32)
    projected = projected.astype(jnp.bfloat16)
    for k in range(plan.links):
        leaving[spots[k]] = projected[:, k * rows : (k + 1) * rows]

    @pl.when(arc == pl.num_programs(0) - 1)
    def _():
        for s in range(rings):
            outward(s).start()
        for s in range(rings):
            outward(s).wait()


def run_arcs(plan, tab, arrived, coupling_panel, inv_factor):
    arcs, arc_rows, width = coupling_panel.shape
    block = arrived[0].shape[1:]
    total = plan.rings * plan.slots
    anywhere = pl.BlockSpec(memory_space=pl.ANY)
    return pl.pallas_call(
        functools.partial(arcs_kernel, plan),
        grid_spec=pltpu.PrefetchScalarGridSpec(
            num_scalar_prefetch=1,
            grid=(arcs,),
            in_specs=[anywhere] * plan.rings
            + [
                pl.BlockSpec((1, arc_rows, width), lambda i, t: (i, 0, 0)),
                pl.BlockSpec((1, arc_rows, arc_rows), lambda i, t: (i, 0, 0)),
            ],
            out_specs=[anywhere] * plan.rings,
            scratch_shapes=[
                pltpu.VMEM((total,) + block, jnp.bfloat16),
                pltpu.VMEM((total,) + block, jnp.bfloat16),
                pltpu.VMEM((width, block[1]), jnp.bfloat16),
                pltpu.SemaphoreType.DMA((plan.rings,)),
            ],
        ),
        out_shape=[jax.ShapeDtypeStruct((plan.slots,) + block, jnp.bfloat16)] * plan.rings,
        name="arcs",
    )(tab, *arrived, coupling_panel, inv_factor)


def fold_kernel(plan, step, has_prev, last, me_ref, tab_ref, got_ref, *refs):
    me = me_ref[0]
    prev_ref = refs[0] if has_prev else None
    out_ref, acc = refs[-2], refs[-1]
    column = plan.source_plane(me, step) * plan.plane + lax.rem(me, plan.plane)
    if has_prev:
        acc[...] = prev_ref[...].astype(jnp.float32)
    else:
        acc[...] = jnp.zeros_like(acc)

    @pl.loop(0, plan.plane)
    def _(q):
        for r in range(plan.cap):
            held = tab_ref[r * plan.plane + q, column]

            @pl.when(held > 0)
            def _():
                acc[held - 1] += got_ref[q * plan.cap + r].astype(jnp.float32)

    if last:

        @pl.loop(0, plan.blocks)
        def _(b):
            out_ref[b] = acc[b].T
    else:
        out_ref[...] = acc[...].astype(out_ref.dtype)


def fold(plan, step, me, tab, got, prev, last):
    shape = (plan.blocks,) + got.shape[1:]
    args = (me, tab, got) + (() if prev is None else (prev,))
    specs = [pl.BlockSpec(memory_space=SMEM)] * 2 + [pl.BlockSpec(memory_space=VMEM)] * (
        len(args) - 2
    )
    return pl.pallas_call(
        functools.partial(fold_kernel, plan, step, prev is not None, last),
        out_shape=jax.ShapeDtypeStruct(shape, jnp.float32 if last else jnp.bfloat16),
        in_specs=specs,
        out_specs=pl.BlockSpec(memory_space=VMEM),
        scratch_shapes=[pltpu.VMEM(shape, jnp.float32)],
        name="fold",
    )(*args)


def trade_plane(plan, buffer):
    return lax.all_to_all(
        buffer, AXES, split_axis=0, concat_axis=0, tiled=True, axis_index_groups=plan.groups
    )


def coupled_sum(plan, me, tab, rounded, coupling_panel, inv_factor):
    chunk, arrived = rounded, []
    for s in range(plan.rings):
        following = None
        if s + 1 < plan.rings:
            following = lax.ppermute(chunk, AXES, plan.ring)
        chosen = pick(plan, s, me, tab, chunk)
        arrived.append(trade_plane(plan, chosen))
        chunk = following
    leaving = run_arcs(plan, tab, arrived, coupling_panel, inv_factor)
    carried = None
    for j in range(plan.rings):
        s = (j + 1) % plan.rings
        last = j + 1 == plan.rings
        got = trade_plane(plan, leaving[s])
        carried = fold(plan, s, me, tab, got, carried, last)
        if not last:
            carried = lax.ppermute(carried, AXES, plan.ring)
    return carried


def per_device(
    mesh, right_side, prior_diag, inv_factor, coupling_panel, coupling_owner, coupling_block
):
    plan = Plan(mesh, coupling_panel.shape[0], coupling_owner.shape[1], right_side.shape[0])
    me = lax.axis_index(AXES).astype(jnp.int32).reshape(1)
    tab = make_tables(plan, me, coupling_owner, coupling_block)
    solution_field = jnp.zeros_like(right_side)
    residual = right_side
    direction = right_side
    (res_gram,) = sum_all([inner_gram(residual, residual)])
    for sweep_index in range(ITERS):
        summed = coupled_sum(
            plan, me, tab, direction.astype(jnp.bfloat16), coupling_panel, inv_factor
        )
        image_vec = prior_diag[:, :, None] * direction + summed
        last = sweep_index + 1 == ITERS
        if last:
            (curv_gram,) = sum_all([inner_gram(direction, image_vec)])
        else:
            curv_gram, image_gram, cross_gram = sum_all(
                [
                    inner_gram(direction, image_vec),
                    inner_gram(image_vec, image_vec),
                    inner_gram(residual, image_vec),
                ]
            )
        factor_low = jnp.linalg.cholesky(curv_gram)
        step_mat = jax.scipy.linalg.cho_solve((factor_low, True), res_gram)
        solution_field = solution_field + combine_cols(direction, step_mat)
        residual = residual - combine_cols(image_vec, step_mat)
        if not last:
            new_gram = (
                res_gram - times_high(step_mat.T, cross_gram.T) - times_high(cross_gram, step_mat)
            )
            new_gram = new_gram + times_high(step_mat.T, times_high(image_gram, step_mat))
            beta_mat = jax.scipy.linalg.cho_solve((jnp.linalg.cholesky(res_gram), True), new_gram)
            direction = residual + combine_cols(direction, beta_mat)
            res_gram = new_gram
    return (solution_field, residual)


def solution(mesh):
    in_specs = (
        P(AXES, None, None),
        P(AXES, None),
        P(AXES, None, None),
        P(AXES, None, None),
        P(),
        P(),
    )
    out_specs = (P(AXES, None, None), P(AXES, None, None))
    return jax.shard_map(
        functools.partial(per_device, mesh),
        mesh=mesh,
        in_specs=in_specs,
        out_specs=out_specs,
        check_vma=False,
    )
```

```python
import functools

import jax
import jax.numpy as jnp
from jax import lax
from jax.experimental import pallas as pl
from jax.experimental.pallas import tpu as pltpu
from jax.sharding import PartitionSpec as P


ITERS = 2
GROUP = 2
AXES = ("arc", "vec")
SMEM = pltpu.MemorySpace.SMEM
VMEM = pltpu.MemorySpace.VMEM


def inner_gram(left, right):
    return jnp.einsum("grc,grd->cd", left, right, precision=lax.Precision.HIGHEST)


def combine_cols(field, weights):
    return jnp.einsum("grc,cd->grd", field, weights, precision=lax.Precision.HIGHEST)


def times_high(left, right):
    return jnp.dot(left, right, precision=lax.Precision.HIGHEST)


def trade(buffer):
    return lax.all_to_all(buffer, AXES, split_axis=0, concat_axis=0, tiled=True)


def sum_all(grams):
    device_count = lax.axis_size(AXES)
    stacked = jnp.concatenate(grams, axis=0)
    rows, cols = stacked.shape
    pieces = stacked.reshape(device_count, rows // device_count, cols)
    mine = jnp.sum(trade(pieces), axis=0)
    shared = jnp.broadcast_to(mine[None], pieces.shape)
    total = trade(shared).reshape(len(grams), rows // len(grams), cols)
    return total


class Plan:
    def __init__(self, mesh, arcs_here, links, blocks_here):
        arc, vec = mesh.shape["arc"], mesh.shape["vec"]
        half = max(1, vec // 2)
        self.rings = arc // half if arc % half == 0 else arc
        self.devices = arc * vec
        self.plane = self.devices // self.rings
        self.arcs, self.links, self.blocks = arcs_here, links, blocks_here
        entries = arcs_here * links
        self.cap = (entries + self.devices - 1) // self.devices + 1
        self.slots = self.plane * self.cap
        self.pos_row = self.slots
        self.own_row = self.slots + arcs_here
        self.rows = self.slots + 2 * arcs_here
        self.order = [self.plane_at(i) for i in range(self.rings)]
        self.ring = [
            (self.order[i] * self.plane + p, self.order[(i + 1) % self.rings] * self.plane + p)
            for i in range(self.rings)
            for p in range(self.plane)
        ]
        self.paired = self.plane & (self.plane - 1) == 0
        half = self.rings // 2
        onward, reverse = list(range(half, 0, -1)), list(range(half + 1, self.rings))
        self.back = []
        while onward or reverse:
            self.back += onward[:1] + reverse[:1]
            onward, reverse = onward[1:], reverse[1:]
        self.back.append(0)

    def follows(self, step):
        half = self.rings // 2
        sources = [step + 1] if step < half else []
        if step > half + 1 or (step == 0 and self.rings > half + 1):
            sources.append((step - 1) % self.rings)
        return sources

    def shift_back(self, step):
        move = 1 if step <= self.rings // 2 else -1
        return [
            (self.order[i] * self.plane + p, self.order[(i - move) % self.rings] * self.plane + p)
            for i in range(self.rings)
            for p in range(self.plane)
        ]

    def target(self, p, offset):
        return p ^ offset if self.paired else (p + offset) % self.plane

    def target_traced(self, p, offset):
        return p ^ offset if self.paired else lax.rem(p + offset, self.plane)

    def source_traced(self, p, offset):
        return p ^ offset if self.paired else lax.rem(p - offset + self.plane, self.plane)

    def shift_plane(self, offset):
        return [
            (z * self.plane + p, z * self.plane + self.target(p, offset))
            for z in range(self.rings)
            for p in range(self.plane)
        ]

    def plane_at(self, place):
        return 2 * place if 2 * place < self.rings else 2 * self.rings - 1 - 2 * place

    def place_of(self, z):
        half = lax.div(z, 2)
        return jnp.where(lax.rem(z, 2) == 0, half, self.rings - 1 - half)

    def source_plane(self, me, step):
        place = self.place_of(lax.div(me, self.plane))
        place = lax.rem(place - step + self.rings, self.rings)
        doubled = 2 * place
        return jnp.where(doubled < self.rings, doubled, 2 * self.rings - 1 - doubled)


def tables_kernel(plan, me_ref, owner_cols, block_cols, tab_ref, owner_ref, block_ref):
    me = me_ref[0]
    arcs, links, lanes = plan.arcs, plan.links, tab_ref.shape[1]
    z = lax.div(me, plan.plane)
    span = plan.plane * arcs
    first = pl.multiple_of(z * span, span)
    owner_ref[...] = owner_cols[:, pl.ds(first, span)].T
    block_ref[...] = block_cols[:, pl.ds(first, span)].T
    owners = lax.broadcasted_iota(jnp.int32, (arcs, lanes), 1)
    low = lax.broadcasted_iota(jnp.int32, (arcs, arcs), 0)
    high = lax.broadcasted_iota(jnp.int32, (arcs, arcs), 1)
    before = (high < low).astype(jnp.float32)

    def incidence(row):
        owner = owner_ref[pl.ds(row, arcs), :]
        block = block_ref[pl.ds(row, arcs), :]
        named = jnp.zeros((arcs, lanes), jnp.float32)
        held = jnp.zeros((arcs, lanes), jnp.int32)
        for k in range(links):
            same = owner[:, k : k + 1] == owners
            named = jnp.where(same, 1.0, named)
            held = jnp.where(same, block[:, k : k + 1] + 1, held)
        rank = jnp.dot(before, named, preferred_element_type=jnp.float32).astype(jnp.int32)
        return held, rank

    for q in range(plan.plane):
        held, rank = incidence(q * arcs)
        for r in range(plan.cap):
            at_rank = jnp.where(rank == r, held, 0)
            tab_ref[r * plan.plane + q : r * plan.plane + q + 1, :] = jnp.sum(
                at_rank, axis=0, keepdims=True
            )
    row = pl.multiple_of(lax.rem(me, plan.plane) * arcs, arcs)
    held, rank = incidence(row)
    place = plan.place_of(z)
    other = plan.place_of(lax.div(owners, plan.plane))
    step = lax.rem(place - other + plan.rings, plan.rings)
    here, there = lax.rem(me, plan.plane), lax.rem(owners, plan.plane)
    offset = here ^ there if plan.paired else lax.rem(here - there + plan.plane, plan.plane)
    slot = step * plan.slots + offset * plan.cap + rank
    tab_ref[plan.pos_row : plan.pos_row + arcs, :] = slot
    mine = jnp.zeros((arcs, lanes), jnp.int32)
    owner = owner_ref[pl.ds(row, arcs), :]
    for k in range(links):
        mine = jnp.where(owners == k, owner[:, k : k + 1], mine)
    tab_ref[plan.own_row : plan.own_row + arcs, :] = mine


def make_tables(plan, me, coupling_owner, coupling_block):
    lanes = -(-plan.devices // 128) * 128
    return pl.pallas_call(
        functools.partial(tables_kernel, plan),
        out_shape=jax.ShapeDtypeStruct((plan.rows, lanes), jnp.int32),
        in_specs=[
            pl.BlockSpec(memory_space=SMEM),
            pl.BlockSpec(memory_space=VMEM),
            pl.BlockSpec(memory_space=VMEM),
        ],
        out_specs=pl.BlockSpec(memory_space=VMEM),
        scratch_shapes=[pltpu.VMEM((plan.plane * plan.arcs, plan.links), jnp.int32)] * 2,
        name="tables",
    )(me, coupling_owner.T, coupling_block.T)


def pick_kernel(plan, step, me_ref, tab_ref, chunk_ref, *out_refs):
    me = me_ref[0]
    here = lax.rem(me, plan.plane)
    column = plan.source_plane(me, step) * plan.plane + here
    for offset, out_ref in enumerate(out_refs):
        q = plan.target_traced(here, offset)
        for r in range(plan.cap):
            block = jnp.maximum(tab_ref[r * plan.plane + q, column] - 1, 0)
            out_ref[r] = chunk_ref[block]


def pick(plan, step, me, tab, chunk):
    shape = (plan.cap,) + chunk.shape[1:]
    return pl.pallas_call(
        functools.partial(pick_kernel, plan, step),
        out_shape=[jax.ShapeDtypeStruct(shape, chunk.dtype)] * plan.plane,
        in_specs=[
            pl.BlockSpec(memory_space=SMEM),
            pl.BlockSpec(memory_space=SMEM),
            pl.BlockSpec(memory_space=VMEM),
        ],
        out_specs=[pl.BlockSpec(memory_space=VMEM)] * plan.plane,
        name="pick",
    )(me, tab, chunk)


def narrow_dot(left, right, contract=1):
    product = lax.dot_general(
        left, right, (((contract,), (0,)), ((), ())), preferred_element_type=jnp.float32
    )
    return product.astype(jnp.bfloat16)


def arcs_kernel(plan, tab_ref, *refs):
    count, cap = plan.rings * plan.plane, plan.cap
    arrived_refs = refs[:count]
    panel_ref, factor_ref = refs[count], refs[count + 1]
    out_refs = refs[count + 2 : 2 * count + 2]
    arrived, leaving, fetched, sems = refs[2 * count + 2 :]
    arc = pl.program_id(0)
    rows = arrived.shape[1]

    def inward(s):
        return pltpu.make_async_copy(
            arrived_refs[s], arrived.at[pl.ds(s * cap, cap)], sems.at[s]
        )

    def outward(s):
        return pltpu.make_async_copy(
            leaving.at[pl.ds(s * cap, cap)], out_refs[s], sems.at[s]
        )

    @pl.when(arc == 0)
    def _():
        for s in range(count):
            inward(s).start()
        for s in range(count):
            inward(s).wait()

    group = range(panel_ref.shape[0])
    spots = [[] for _ in group]
    for g in group:
        row = arc * len(group) + g
        for k in range(plan.links):
            spot = tab_ref[plan.pos_row + row, tab_ref[plan.own_row + row, k]]
            spots[g].append(spot)
            fetched[g, k * rows : (k + 1) * rows, :] = arrived[spot]
    coupled = [narrow_dot(panel_ref[g], fetched[g]) for g in group]
    whitened = [narrow_dot(factor_ref[g], coupled[g]) for g in group]
    smoothed = [narrow_dot(whitened[g], factor_ref[g], 0) for g in group]
    for g in group:
        projected = narrow_dot(smoothed[g], panel_ref[g])
        for k in range(plan.links):
            leaving[spots[g][k]] = projected[:, k * rows : (k + 1) * rows]

    @pl.when(arc == pl.num_programs(0) - 1)
    def _():
        for s in range(count):
            outward(s).start()
        for s in range(count):
            outward(s).wait()


def run_arcs(plan, tab, arrived, coupling_panel, inv_factor):
    arcs, arc_rows, width = coupling_panel.shape
    block = arrived[0].shape[1:]
    total = plan.rings * plan.slots
    group = GROUP if arcs % GROUP == 0 else 1
    anywhere = pl.BlockSpec(memory_space=pl.ANY)
    return pl.pallas_call(
        functools.partial(arcs_kernel, plan),
        grid_spec=pltpu.PrefetchScalarGridSpec(
            num_scalar_prefetch=1,
            grid=(arcs // group,),
            in_specs=[anywhere] * (plan.rings * plan.plane)
            + [
                pl.BlockSpec((group, arc_rows, width), lambda i, t: (i, 0, 0)),
                pl.BlockSpec((group, arc_rows, arc_rows), lambda i, t: (i, 0, 0)),
            ],
            out_specs=[anywhere] * (plan.rings * plan.plane),
            scratch_shapes=[
                pltpu.VMEM((total,) + block, jnp.bfloat16),
                pltpu.VMEM((total,) + block, jnp.bfloat16),
                pltpu.VMEM((group, width, block[1]), jnp.bfloat16),
                pltpu.SemaphoreType.DMA((plan.rings * plan.plane,)),
            ],
        ),
        out_shape=[jax.ShapeDtypeStruct((plan.cap,) + block, jnp.bfloat16)]
        * (plan.rings * plan.plane),
        name="arcs",
    )(tab, *arrived, coupling_panel, inv_factor)


def fold_kernel(plan, step, me_ref, tab_ref, *refs):
    me = me_ref[0]
    here = lax.rem(me, plan.plane)
    got_refs, part_refs = refs[: plan.plane], refs[plan.plane : -2]
    out_ref, acc = refs[-2], refs[-1]
    column = plan.source_plane(me, step) * plan.plane + here
    start = jnp.zeros(acc.shape, jnp.float32)
    for part_ref in part_refs:
        start = start + part_ref[...].astype(jnp.float32)
    acc[...] = start
    for offset, got_ref in enumerate(got_refs):
        q = plan.source_traced(here, offset)
        for r in range(plan.cap):
            held = tab_ref[r * plan.plane + q, column]

            @pl.when(held > 0)
            def _():
                acc[held - 1] += got_ref[r].astype(jnp.float32)

    if step == 0:

        @pl.loop(0, plan.blocks)
        def _(b):
            out_ref[b] = acc[b].T
    else:
        out_ref[...] = acc[...].astype(out_ref.dtype)


def fold(plan, step, me, tab, got, parts):
    shape = (plan.blocks,) + got[0].shape[1:]
    args = (me, tab, *got, *parts)
    specs = [pl.BlockSpec(memory_space=SMEM)] * 2 + [pl.BlockSpec(memory_space=VMEM)] * (
        len(args) - 2
    )
    return pl.pallas_call(
        functools.partial(fold_kernel, plan, step),
        out_shape=jax.ShapeDtypeStruct(shape, jnp.bfloat16 if step else jnp.float32),
        in_specs=specs,
        out_specs=pl.BlockSpec(memory_space=VMEM),
        scratch_shapes=[pltpu.VMEM(shape, jnp.float32)],
        name="fold",
    )(*args)


def identity(size):
    rows = lax.broadcasted_iota(jnp.int32, (size, size), 0)
    lanes = lax.broadcasted_iota(jnp.int32, (size, size), 1)
    return jnp.where(rows == lanes, 1.0, 0.0)


def eliminate(matrix):
    size = matrix.shape[0]
    rows = lax.broadcasted_iota(jnp.int32, (size, size), 0)
    lanes = lax.broadcasted_iota(jnp.int32, (size, size), 1)

    def pivot(k, matrix):
        on_row, on_lane = rows == k, lanes == k
        column = jnp.sum(jnp.where(on_lane, matrix, 0.0), axis=1, keepdims=True)
        row = jnp.sum(jnp.where(on_row, matrix, 0.0), axis=0, keepdims=True)
        scale = 1.0 / jnp.sum(jnp.where(on_lane[:1], row, 0.0), axis=1, keepdims=True)
        row = jnp.where(on_lane[:1], 1.0, row) * scale
        rest = jnp.where(on_lane, 0.0, matrix) - column * row
        return jnp.where(on_row, row, rest)

    return lax.fori_loop(0, size, pivot, matrix)


def invert_into(out_refs, matrices):
    size = matrices[0].shape[0]
    eye = identity(size)
    scales, scaled = [], []
    for matrix in matrices:
        diagonal = eye * matrix
        down = lax.rsqrt(jnp.sum(diagonal, axis=1, keepdims=True))
        along = lax.rsqrt(jnp.sum(diagonal, axis=0, keepdims=True))
        scales.append((down, along))
        scaled.append(matrix * down * along)
    off = [matrix - eye for matrix in scaled]
    second = [times_high(e, e) for e in off]
    fourth = [times_high(e, e) for e in second]
    third = [times_high(e, f) for e, f in zip(off, second)]
    guess = [eye - e + f - g for e, f, g in zip(off, second, third)]
    guess = [x + times_high(x, e) for x, e in zip(guess, fourth)]
    left = [eye - times_high(a, x) for a, x in zip(scaled, guess)]
    guess = [x + times_high(x, r) for x, r in zip(guess, left)]
    for out_ref, x, r, a, (down, along) in zip(out_refs, guess, left, scaled, scales):
        out_ref[...] = x * down * along
        worst = jnp.max(jnp.sum(jnp.abs(r), axis=1, keepdims=True))

        @pl.when(jnp.logical_not(worst < 1e-3))
        def _():
            y = eliminate(a)
            y = y + times_high(y, eye - times_high(a, y))
            out_ref[...] = y * down * along


def step_kernel(grams_ref, step_ref, beta_ref, new_ref, first_inv, second_inv):
    res, cross, image = grams_ref[0], grams_ref[1], grams_ref[2]
    invert_into([first_inv, second_inv], [0.5 * (cross + cross.T), 0.5 * (res + res.T)])
    step = times_high(first_inv[...], res)
    step_ref[...] = step
    moved = times_high(cross, step)
    new = res - moved.T - moved + times_high(step.T, times_high(image, step))
    new_ref[...] = new
    beta_ref[...] = times_high(second_inv[...], new)


def last_kernel(grams_ref, res_ref, step_ref, first_inv):
    curv = grams_ref[0]
    invert_into([first_inv], [0.5 * (curv + curv.T)])
    step_ref[...] = times_high(first_inv[...], res_ref[...])


def small_solve(kernel, args, outputs, scratch):
    shape = args[0].shape[1:]
    return pl.pallas_call(
        kernel,
        out_shape=[jax.ShapeDtypeStruct(shape, jnp.float32)] * outputs,
        scratch_shapes=[pltpu.VMEM(shape, jnp.float32)] * scratch,
        name="solve",
    )(*args)


def trade_plane(plan, buffers):
    moved = [None] * plan.plane
    moved[0] = buffers[0]
    for offset in range(plan.plane - 1, 0, -1):
        moved[offset] = lax.ppermute(buffers[offset], AXES, plan.shift_plane(offset))
    return moved


def gate_kernel(in_ref, out_ref):
    out_ref[0] = in_ref[0]


def gate(me):
    return pl.pallas_call(
        gate_kernel,
        out_shape=jax.ShapeDtypeStruct(me.shape, me.dtype),
        in_specs=[pl.BlockSpec(memory_space=SMEM)],
        out_specs=pl.BlockSpec(memory_space=SMEM),
        name="gate",
    )(me)


def coupled_sum(plan, me, tab, rounded, coupling_panel, inv_factor):
    chunk, arrived = rounded, []
    for s in range(plan.rings):
        following = None
        if s + 1 < plan.rings:
            following = lax.ppermute(chunk, AXES, plan.ring)
        chosen = pick(plan, s, me, tab, chunk)
        arrived += trade_plane(plan, chosen)
        if s + 1 < plan.rings:
            me = gate(me)
        chunk = following
    leaving = run_arcs(plan, tab, arrived, coupling_panel, inv_factor)
    moved, folded = {}, []
    for j, s in enumerate(plan.back):
        buffers = leaving[s * plan.plane : (s + 1) * plan.plane]
        if j >= 2:
            *buffers, _ = lax.optimization_barrier((*buffers, folded[j - 2]))
        got = trade_plane(plan, buffers)
        sources = [moved[source] for source in plan.follows(s)]
        if s:
            me = gate(me)
        folded.append(fold(plan, s, me, tab, got, sources))
        if s:
            moved[s] = lax.ppermute(folded[j], AXES, plan.shift_back(s))
    return folded[-1], me


def per_device(
    mesh, right_side, prior_diag, inv_factor, coupling_panel, coupling_owner, coupling_block
):
    plan = Plan(mesh, coupling_panel.shape[0], coupling_owner.shape[1], right_side.shape[0])
    me = lax.axis_index(AXES).astype(jnp.int32).reshape(1)
    tab = make_tables(plan, me, coupling_owner, coupling_block)
    solution_field = jnp.zeros_like(right_side)
    residual = right_side
    direction = right_side
    start_gram = inner_gram(residual, residual)
    for sweep_index in range(ITERS):
        summed, me = coupled_sum(
            plan, me, tab, direction.astype(jnp.bfloat16), coupling_panel, inv_factor
        )
        image_vec = prior_diag[:, :, None] * direction + summed
        last = sweep_index + 1 == ITERS
        if last:
            grams = sum_all([inner_gram(direction, image_vec)])
            (step_mat,) = small_solve(last_kernel, (grams, res_gram), 1, 1)
        else:
            grams = sum_all(
                [start_gram, inner_gram(direction, image_vec), inner_gram(image_vec, image_vec)]
            )
            step_mat, beta_mat, res_gram = small_solve(step_kernel, (grams,), 3, 2)
        solution_field = solution_field + combine_cols(direction, step_mat)
        residual = residual - combine_cols(image_vec, step_mat)
        if not last:
            direction = residual + combine_cols(direction, beta_mat)
    return (solution_field, residual)


def solution(mesh):
    in_specs = (
        P(AXES, None, None),
        P(AXES, None),
        P(AXES, None, None),
        P(AXES, None, None),
        P(),
        P(),
    )
    out_specs = (P(AXES, None, None), P(AXES, None, None))
    return jax.shard_map(
        functools.partial(per_device, mesh),
        mesh=mesh,
        in_specs=in_specs,
        out_specs=out_specs,
        check_vma=False,
    )
```

```python
import functools

import jax
import jax.numpy as jnp
from jax import lax
from jax.experimental import pallas as pl
from jax.experimental.pallas import tpu as pltpu
from jax.sharding import PartitionSpec as P


ITERS = 2
GROUP = 4
AXES = ("arc", "vec")
SMEM = pltpu.MemorySpace.SMEM
VMEM = pltpu.MemorySpace.VMEM


def inner_gram(left, right):
    return jnp.einsum("grc,grd->cd", left, right, precision=lax.Precision.HIGHEST)


def combine_cols(field, weights):
    return jnp.einsum("grc,cd->grd", field, weights, precision=lax.Precision.HIGHEST)


def times_high(left, right):
    return jnp.dot(left, right, precision=lax.Precision.HIGHEST)


def trade(buffer):
    return lax.all_to_all(buffer, AXES, split_axis=0, concat_axis=0, tiled=True)


def sum_all(grams):
    device_count = lax.axis_size(AXES)
    count, rows, cols = grams.shape
    pieces = grams.reshape(device_count, count * rows // device_count, cols)
    mine = jnp.sum(trade(pieces), axis=0)
    shared = jnp.broadcast_to(mine[None], pieces.shape)
    return trade(shared).reshape(grams.shape)


class Plan:
    def __init__(self, mesh, arcs_here, links, blocks_here):
        arc, vec = mesh.shape["arc"], mesh.shape["vec"]
        half = max(1, vec // 2)
        self.rings = arc // half if arc % half == 0 else arc
        self.devices = arc * vec
        self.plane = self.devices // self.rings
        self.arcs, self.links, self.blocks = arcs_here, links, blocks_here
        entries = arcs_here * links
        self.cap = (entries + self.devices - 1) // self.devices + 1
        self.slots = self.plane * self.cap
        self.pos_row = self.slots
        self.own_row = self.slots + arcs_here
        self.rows = self.slots + 2 * arcs_here
        self.order = [self.plane_at(i) for i in range(self.rings)]
        self.ring = [
            (self.order[i] * self.plane + p, self.order[(i + 1) % self.rings] * self.plane + p)
            for i in range(self.rings)
            for p in range(self.plane)
        ]
        self.paired = self.plane & (self.plane - 1) == 0
        half = self.rings // 2
        onward, reverse = list(range(half, 0, -1)), list(range(half + 1, self.rings))
        self.back = []
        while onward or reverse:
            self.back += onward[:1] + reverse[:1]
            onward, reverse = onward[1:], reverse[1:]
        self.back.append(0)

    def follows(self, step):
        half = self.rings // 2
        sources = [step + 1] if step < half else []
        if step > half + 1 or (step == 0 and self.rings > half + 1):
            sources.append((step - 1) % self.rings)
        return sources

    def shift_back(self, step):
        move = 1 if step <= self.rings // 2 else -1
        return [
            (self.order[i] * self.plane + p, self.order[(i - move) % self.rings] * self.plane + p)
            for i in range(self.rings)
            for p in range(self.plane)
        ]

    def target(self, p, offset):
        return p ^ offset if self.paired else (p + offset) % self.plane

    def target_traced(self, p, offset):
        return p ^ offset if self.paired else lax.rem(p + offset, self.plane)

    def source_traced(self, p, offset):
        return p ^ offset if self.paired else lax.rem(p - offset + self.plane, self.plane)

    def shift_plane(self, offset):
        return [
            (z * self.plane + p, z * self.plane + self.target(p, offset))
            for z in range(self.rings)
            for p in range(self.plane)
        ]

    def plane_at(self, place):
        return 2 * place if 2 * place < self.rings else 2 * self.rings - 1 - 2 * place

    def place_of(self, z):
        half = lax.div(z, 2)
        return jnp.where(lax.rem(z, 2) == 0, half, self.rings - 1 - half)

    def source_plane(self, me, step):
        place = self.place_of(lax.div(me, self.plane))
        place = lax.rem(place - step + self.rings, self.rings)
        doubled = 2 * place
        return jnp.where(doubled < self.rings, doubled, 2 * self.rings - 1 - doubled)


def tables_kernel(plan, me_ref, owner_cols, block_cols, tab_ref, owner_ref, block_ref):
    me = me_ref[0]
    arcs, links, lanes = plan.arcs, plan.links, tab_ref.shape[1]
    z = lax.div(me, plan.plane)
    span = plan.plane * arcs
    first = pl.multiple_of(z * span, span)
    owner_ref[...] = owner_cols[:, pl.ds(first, span)].T
    block_ref[...] = block_cols[:, pl.ds(first, span)].T
    owners = lax.broadcasted_iota(jnp.int32, (arcs, lanes), 1)
    low = lax.broadcasted_iota(jnp.int32, (arcs, arcs), 0)
    high = lax.broadcasted_iota(jnp.int32, (arcs, arcs), 1)
    before = (high < low).astype(jnp.float32)

    def incidence(row):
        owner = owner_ref[pl.ds(row, arcs), :]
        block = block_ref[pl.ds(row, arcs), :]
        named = jnp.zeros((arcs, lanes), jnp.float32)
        held = jnp.zeros((arcs, lanes), jnp.int32)
        for k in range(links):
            same = owner[:, k : k + 1] == owners
            named = jnp.where(same, 1.0, named)
            held = jnp.where(same, block[:, k : k + 1] + 1, held)
        rank = jnp.dot(before, named, preferred_element_type=jnp.float32).astype(jnp.int32)
        return held, rank

    for q in range(plan.plane):
        held, rank = incidence(q * arcs)
        for r in range(plan.cap):
            at_rank = jnp.where(rank == r, held, 0)
            tab_ref[r * plan.plane + q : r * plan.plane + q + 1, :] = jnp.sum(
                at_rank, axis=0, keepdims=True
            )
    row = pl.multiple_of(lax.rem(me, plan.plane) * arcs, arcs)
    held, rank = incidence(row)
    place = plan.place_of(z)
    other = plan.place_of(lax.div(owners, plan.plane))
    step = lax.rem(place - other + plan.rings, plan.rings)
    here, there = lax.rem(me, plan.plane), lax.rem(owners, plan.plane)
    offset = here ^ there if plan.paired else lax.rem(here - there + plan.plane, plan.plane)
    slot = step * plan.slots + offset * plan.cap + rank
    tab_ref[plan.pos_row : plan.pos_row + arcs, :] = slot
    mine = jnp.zeros((arcs, lanes), jnp.int32)
    owner = owner_ref[pl.ds(row, arcs), :]
    for k in range(links):
        mine = jnp.where(owners == k, owner[:, k : k + 1], mine)
    tab_ref[plan.own_row : plan.own_row + arcs, :] = mine


def make_tables(plan, me, coupling_owner, coupling_block):
    lanes = -(-plan.devices // 128) * 128
    return pl.pallas_call(
        functools.partial(tables_kernel, plan),
        out_shape=jax.ShapeDtypeStruct((plan.rows, lanes), jnp.int32),
        in_specs=[
            pl.BlockSpec(memory_space=SMEM),
            pl.BlockSpec(memory_space=VMEM),
            pl.BlockSpec(memory_space=VMEM),
        ],
        out_specs=pl.BlockSpec(memory_space=VMEM),
        scratch_shapes=[pltpu.VMEM((plan.plane * plan.arcs, plan.links), jnp.int32)] * 2,
        name="tables",
    )(me, coupling_owner.T, coupling_block.T)


def pick_kernel(plan, step, me_ref, tab_ref, chunk_ref, *out_refs):
    me = me_ref[0]
    here = lax.rem(me, plan.plane)
    column = plan.source_plane(me, step) * plan.plane + here
    for offset, out_ref in enumerate(out_refs):
        q = plan.target_traced(here, offset)
        for r in range(plan.cap):
            block = jnp.maximum(tab_ref[r * plan.plane + q, column] - 1, 0)
            out_ref[r] = chunk_ref[block]


def pick(plan, step, me, tab, chunk):
    shape = (plan.cap,) + chunk.shape[1:]
    return pl.pallas_call(
        functools.partial(pick_kernel, plan, step),
        out_shape=[jax.ShapeDtypeStruct(shape, chunk.dtype)] * plan.plane,
        in_specs=[
            pl.BlockSpec(memory_space=SMEM),
            pl.BlockSpec(memory_space=SMEM),
            pl.BlockSpec(memory_space=VMEM),
        ],
        out_specs=[pl.BlockSpec(memory_space=VMEM)] * plan.plane,
        name="pick",
    )(me, tab, chunk)


def narrow_dot(left, right, contract=1):
    product = lax.dot_general(
        left, right, (((contract,), (0,)), ((), ())), preferred_element_type=jnp.float32
    )
    return product.astype(jnp.bfloat16)


def arcs_kernel(plan, tab_ref, *refs):
    count, cap = plan.rings * plan.plane, plan.cap
    arrived_refs = refs[:count]
    panel_ref, factor_ref = refs[count], refs[count + 1]
    out_refs = refs[count + 2 : 2 * count + 2]
    arrived, leaving, fetched, sems = refs[2 * count + 2 :]
    arc = pl.program_id(0)
    rows = arrived.shape[1]

    def inward(s):
        return pltpu.make_async_copy(
            arrived_refs[s], arrived.at[pl.ds(s * cap, cap)], sems.at[s]
        )

    def outward(s):
        return pltpu.make_async_copy(
            leaving.at[pl.ds(s * cap, cap)], out_refs[s], sems.at[s]
        )

    @pl.when(arc == 0)
    def _():
        for s in range(count):
            inward(s).start()
        for s in range(count):
            inward(s).wait()

    group = range(panel_ref.shape[0])
    spots = [[] for _ in group]
    for g in group:
        row = arc * len(group) + g
        for k in range(plan.links):
            spot = tab_ref[plan.pos_row + row, tab_ref[plan.own_row + row, k]]
            spots[g].append(spot)
            fetched[g, k * rows : (k + 1) * rows, :] = arrived[spot]
    coupled = [narrow_dot(panel_ref[g], fetched[g]) for g in group]
    whitened = [narrow_dot(factor_ref[g], coupled[g]) for g in group]
    smoothed = [narrow_dot(whitened[g], factor_ref[g], 0) for g in group]
    for g in group:
        projected = narrow_dot(smoothed[g], panel_ref[g])
        for k in range(plan.links):
            leaving[spots[g][k]] = projected[:, k * rows : (k + 1) * rows]

    @pl.when(arc == pl.num_programs(0) - 1)
    def _():
        for s in range(count):
            outward(s).start()
        for s in range(count):
            outward(s).wait()


def run_arcs(plan, tab, arrived, coupling_panel, inv_factor):
    arcs, arc_rows, width = coupling_panel.shape
    block = arrived[0].shape[1:]
    total = plan.rings * plan.slots
    group = GROUP if arcs % GROUP == 0 else 1
    anywhere = pl.BlockSpec(memory_space=pl.ANY)
    return pl.pallas_call(
        functools.partial(arcs_kernel, plan),
        grid_spec=pltpu.PrefetchScalarGridSpec(
            num_scalar_prefetch=1,
            grid=(arcs // group,),
            in_specs=[anywhere] * (plan.rings * plan.plane)
            + [
                pl.BlockSpec((group, arc_rows, width), lambda i, t: (i, 0, 0)),
                pl.BlockSpec((group, arc_rows, arc_rows), lambda i, t: (i, 0, 0)),
            ],
            out_specs=[anywhere] * (plan.rings * plan.plane),
            scratch_shapes=[
                pltpu.VMEM((total,) + block, jnp.bfloat16),
                pltpu.VMEM((total,) + block, jnp.bfloat16),
                pltpu.VMEM((group, width, block[1]), jnp.bfloat16),
                pltpu.SemaphoreType.DMA((plan.rings * plan.plane,)),
            ],
        ),
        out_shape=[jax.ShapeDtypeStruct((plan.cap,) + block, jnp.bfloat16)]
        * (plan.rings * plan.plane),
        name="arcs",
    )(tab, *arrived, coupling_panel, inv_factor)


def add_up(plan, step, me_ref, tab_ref, got_refs, part_refs, acc):
    me = me_ref[0]
    here = lax.rem(me, plan.plane)
    column = plan.source_plane(me, step) * plan.plane + here
    start = jnp.zeros(acc.shape, jnp.float32)
    for part_ref in part_refs:
        start = start + part_ref[...].astype(jnp.float32)
    acc[...] = start
    for offset, got_ref in enumerate(got_refs):
        q = plan.source_traced(here, offset)
        for r in range(plan.cap):
            held = tab_ref[r * plan.plane + q, column]

            @pl.when(held > 0)
            def _():
                acc[held - 1] += got_ref[r].astype(jnp.float32)


def fold_kernel(plan, step, me_ref, tab_ref, *refs):
    got_refs, part_refs = refs[: plan.plane], refs[plan.plane : -2]
    out_ref, acc = refs[-2], refs[-1]
    add_up(plan, step, me_ref, tab_ref, got_refs, part_refs, acc)
    out_ref[...] = acc[...].astype(out_ref.dtype)


def image_kernel(plan, both, me_ref, tab_ref, field_ref, prior_ref, *refs):
    got_refs, part_refs = refs[: plan.plane], refs[plan.plane : -3]
    image_ref, gram_ref, acc = refs[-3:]
    add_up(plan, 0, me_ref, tab_ref, got_refs, part_refs, acc)
    rows = acc.shape[1]
    for b in range(plan.blocks):
        image_ref[b] = acc[b].T + prior_ref[:, b : b + 1] * field_ref[b]
    gram_ref[...] = jnp.zeros_like(gram_ref)
    batch = max(n for n in range(1, 6) if plan.blocks % n == 0)

    @pl.loop(0, plan.blocks, step=batch)
    def _(b):
        field = field_ref[pl.ds(b, batch)].reshape(batch * rows, -1)
        image = image_ref[pl.ds(b, batch)].reshape(batch * rows, -1)
        gram_ref[0] += gram_of(field, image)
        if both:
            gram_ref[1] += gram_of(image, image)


def gram_of(left, right):
    return lax.dot_general(
        left,
        right,
        (((0,), (0,)), ((), ())),
        precision=lax.Precision.HIGHEST,
        preferred_element_type=jnp.float32,
    )


def fold_specs(args):
    return [pl.BlockSpec(memory_space=SMEM)] * 2 + [pl.BlockSpec(memory_space=VMEM)] * (
        len(args) - 2
    )


def fold(plan, step, me, tab, got, parts):
    shape = (plan.blocks,) + got[0].shape[1:]
    args = (me, tab, *got, *parts)
    return pl.pallas_call(
        functools.partial(fold_kernel, plan, step),
        out_shape=jax.ShapeDtypeStruct(shape, jnp.bfloat16),
        in_specs=fold_specs(args),
        out_specs=pl.BlockSpec(memory_space=VMEM),
        scratch_shapes=[pltpu.VMEM(shape, jnp.float32)],
        name="fold",
    )(*args)


def fold_image(plan, me, tab, got, parts, field, prior_cols, both):
    shape, cols = field.shape, field.shape[2]
    args = (me, tab, field, prior_cols, *got, *parts)
    return pl.pallas_call(
        functools.partial(image_kernel, plan, both),
        out_shape=[
            jax.ShapeDtypeStruct(shape, jnp.float32),
            jax.ShapeDtypeStruct((2 if both else 1, cols, cols), jnp.float32),
        ],
        in_specs=fold_specs(args),
        out_specs=[pl.BlockSpec(memory_space=VMEM)] * 2,
        scratch_shapes=[pltpu.VMEM(shape, jnp.float32)],
        name="image",
    )(*args)


def update_kernel(field_ref, image_ref, sol_ref, res_ref, step_ref, sol_out, res_out):
    blocks, rows, cols = field_ref.shape
    step = step_ref[...]
    size = (blocks * rows, cols)
    moved = times_high(field_ref[...].reshape(size), step).reshape(field_ref.shape)
    sol_out[...] = sol_ref[...] + moved
    moved = times_high(image_ref[...].reshape(size), step).reshape(field_ref.shape)
    res_out[...] = res_ref[...] - moved


def update(field, image, solution_field, residual, step_mat):
    blocks, rows, cols = field.shape
    batch = max(n for n in range(1, 5) if blocks % n == 0)
    spec = pl.BlockSpec((batch, rows, cols), lambda i: (i, 0, 0))
    return pl.pallas_call(
        update_kernel,
        grid=(blocks // batch,),
        out_shape=[jax.ShapeDtypeStruct(field.shape, jnp.float32)] * 2,
        in_specs=[spec] * 4 + [pl.BlockSpec((cols, cols), lambda i: (0, 0))],
        out_specs=[spec] * 2,
        name="update",
    )(field, image, solution_field, residual, step_mat)


def identity(size):
    rows = lax.broadcasted_iota(jnp.int32, (size, size), 0)
    lanes = lax.broadcasted_iota(jnp.int32, (size, size), 1)
    return jnp.where(rows == lanes, 1.0, 0.0)


def eliminate(matrix):
    size = matrix.shape[0]
    rows = lax.broadcasted_iota(jnp.int32, (size, size), 0)
    lanes = lax.broadcasted_iota(jnp.int32, (size, size), 1)

    def pivot(k, matrix):
        on_row, on_lane = rows == k, lanes == k
        column = jnp.sum(jnp.where(on_lane, matrix, 0.0), axis=1, keepdims=True)
        row = jnp.sum(jnp.where(on_row, matrix, 0.0), axis=0, keepdims=True)
        scale = 1.0 / jnp.sum(jnp.where(on_lane[:1], row, 0.0), axis=1, keepdims=True)
        row = jnp.where(on_lane[:1], 1.0, row) * scale
        rest = jnp.where(on_lane, 0.0, matrix) - column * row
        return jnp.where(on_row, row, rest)

    return lax.fori_loop(0, size, pivot, matrix)


def invert_into(out_refs, matrices):
    size = matrices[0].shape[0]
    eye = identity(size)
    scales, scaled = [], []
    for matrix in matrices:
        diagonal = eye * matrix
        down = lax.rsqrt(jnp.sum(diagonal, axis=1, keepdims=True))
        along = lax.rsqrt(jnp.sum(diagonal, axis=0, keepdims=True))
        scales.append((down, along))
        scaled.append(matrix * down * along)
    off = [matrix - eye for matrix in scaled]
    second = [times_high(e, e) for e in off]
    fourth = [times_high(e, e) for e in second]
    third = [times_high(e, f) for e, f in zip(off, second)]
    guess = [eye - e + f - g for e, f, g in zip(off, second, third)]
    guess = [x + times_high(x, e) for x, e in zip(guess, fourth)]
    left = [eye - times_high(a, x) for a, x in zip(scaled, guess)]
    guess = [x + times_high(x, r) for x, r in zip(guess, left)]
    for out_ref, x, r, a, (down, along) in zip(out_refs, guess, left, scaled, scales):
        out_ref[...] = x * down * along
        worst = jnp.max(jnp.sum(jnp.abs(r), axis=1, keepdims=True))

        @pl.when(jnp.logical_not(worst < 1e-3))
        def _():
            y = eliminate(a)
            y = y + times_high(y, eye - times_high(a, y))
            out_ref[...] = y * down * along


def step_kernel(grams_ref, step_ref, beta_ref, new_ref, first_inv, second_inv):
    res, cross, image = grams_ref[0], grams_ref[1], grams_ref[2]
    invert_into([first_inv, second_inv], [0.5 * (cross + cross.T), 0.5 * (res + res.T)])
    step = times_high(first_inv[...], res)
    step_ref[...] = step
    moved = times_high(cross, step)
    new = res - moved.T - moved + times_high(step.T, times_high(image, step))
    new_ref[...] = new
    beta_ref[...] = times_high(second_inv[...], new)


def last_kernel(grams_ref, res_ref, step_ref, first_inv):
    curv = grams_ref[0]
    invert_into([first_inv], [0.5 * (curv + curv.T)])
    step_ref[...] = times_high(first_inv[...], res_ref[...])


def small_solve(kernel, args, outputs, scratch):
    shape = args[0].shape[1:]
    return pl.pallas_call(
        kernel,
        out_shape=[jax.ShapeDtypeStruct(shape, jnp.float32)] * outputs,
        scratch_shapes=[pltpu.VMEM(shape, jnp.float32)] * scratch,
        name="solve",
    )(*args)


def trade_plane(plan, buffers):
    moved = [None] * plan.plane
    moved[0] = buffers[0]
    for offset in range(plan.plane - 1, 0, -1):
        moved[offset] = lax.ppermute(buffers[offset], AXES, plan.shift_plane(offset))
    return moved


def gate_kernel(in_ref, out_ref):
    out_ref[0] = in_ref[0]


def gate(me):
    return pl.pallas_call(
        gate_kernel,
        out_shape=jax.ShapeDtypeStruct(me.shape, me.dtype),
        in_specs=[pl.BlockSpec(memory_space=SMEM)],
        out_specs=pl.BlockSpec(memory_space=SMEM),
        name="gate",
    )(me)


def apply_schur(plan, me, tab, field, prior_cols, coupling_panel, inv_factor, both):
    chunk, arrived = field.astype(jnp.bfloat16), []
    for s in range(plan.rings):
        following = None
        if s + 1 < plan.rings:
            following = lax.ppermute(chunk, AXES, plan.ring)
        chosen = pick(plan, s, me, tab, chunk)
        arrived += trade_plane(plan, chosen)
        if s + 1 < plan.rings:
            me = gate(me)
        chunk = following
    leaving = run_arcs(plan, tab, arrived, coupling_panel, inv_factor)
    moved, folded = {}, []
    for j, s in enumerate(plan.back):
        buffers = leaving[s * plan.plane : (s + 1) * plan.plane]
        if j >= 2:
            *buffers, _ = lax.optimization_barrier((*buffers, folded[j - 2]))
        got = trade_plane(plan, buffers)
        sources = [moved[source] for source in plan.follows(s)]
        if s:
            me = gate(me)
        if s == 0:
            image, grams = fold_image(plan, me, tab, got, sources, field, prior_cols, both)
            return image, grams, me
        folded.append(fold(plan, s, me, tab, got, sources))
        moved[s] = lax.ppermute(folded[j], AXES, plan.shift_back(s))


def per_device(
    mesh, right_side, prior_diag, inv_factor, coupling_panel, coupling_owner, coupling_block
):
    plan = Plan(mesh, coupling_panel.shape[0], coupling_owner.shape[1], right_side.shape[0])
    me = lax.axis_index(AXES).astype(jnp.int32).reshape(1)
    tab = make_tables(plan, me, coupling_owner, coupling_block)
    prior_cols = prior_diag.T
    solution_field = None
    residual = right_side
    direction = right_side
    start_gram = inner_gram(residual, residual)
    for sweep_index in range(ITERS):
        last = sweep_index + 1 == ITERS
        image_vec, grams, me = apply_schur(
            plan, me, tab, direction, prior_cols, coupling_panel, inv_factor, not last
        )
        if last:
            (step_mat,) = small_solve(last_kernel, (sum_all(grams), res_gram), 1, 1)
            return tuple(update(direction, image_vec, solution_field, residual, step_mat))
        grams = jnp.concatenate([start_gram[None], grams], axis=0)
        step_mat, beta_mat, res_gram = small_solve(step_kernel, (sum_all(grams),), 3, 2)
        solution_field = combine_cols(direction, step_mat)
        residual = residual - combine_cols(image_vec, step_mat)
        direction = residual + combine_cols(direction, beta_mat)


def solution(mesh):
    in_specs = (
        P(AXES, None, None),
        P(AXES, None),
        P(AXES, None, None),
        P(AXES, None, None),
        P(),
        P(),
    )
    out_specs = (P(AXES, None, None), P(AXES, None, None))
    return jax.shard_map(
        functools.partial(per_device, mesh),
        mesh=mesh,
        in_specs=in_specs,
        out_specs=out_specs,
        check_vma=False,
    )
```

```python
import functools

import jax
import jax.numpy as jnp
from jax import lax
from jax.experimental import pallas as pl
from jax.experimental.pallas import tpu as pltpu
from jax.sharding import PartitionSpec as P


ITERS = 2
GROUP = 4
AXES = ("arc", "vec")
SMEM = pltpu.MemorySpace.SMEM
VMEM = pltpu.MemorySpace.VMEM


SMALL = pltpu.CompilerParams(vmem_limit_bytes=16 << 20)


def in_vmem(*arrays):
    placed = [pltpu.with_memory_space_constraint(array, pltpu.VMEM) for array in arrays]
    return placed if len(placed) > 1 else placed[0]


def inner_gram(left, right):
    return jnp.einsum("grc,grd->cd", left, right, precision=lax.Precision.HIGHEST)


def combine_cols(field, weights):
    return jnp.einsum("grc,cd->grd", field, weights, precision=lax.Precision.HIGHEST)


def times_high(left, right):
    return jnp.dot(left, right, precision=lax.Precision.HIGHEST)


def trade(buffer):
    return lax.all_to_all(buffer, AXES, split_axis=0, concat_axis=0, tiled=True)


def sum_all(grams):
    device_count = lax.axis_size(AXES)
    count, rows, cols = grams.shape
    pieces = grams.reshape(device_count, count * rows // device_count, cols)
    mine = jnp.sum(trade(pieces), axis=0)
    shared = jnp.broadcast_to(mine[None], pieces.shape)
    return trade(shared).reshape(grams.shape)


class Plan:
    def __init__(self, mesh, arcs_here, links, blocks_here):
        arc, vec = mesh.shape["arc"], mesh.shape["vec"]
        half = max(1, vec // 2)
        self.rings = arc // half if arc % half == 0 else arc
        self.devices = arc * vec
        self.plane = self.devices // self.rings
        self.arcs, self.links, self.blocks = arcs_here, links, blocks_here
        entries = arcs_here * links
        self.cap = (entries + self.devices - 1) // self.devices + 1
        self.slots = self.plane * self.cap
        self.own_row = arcs_here
        self.padded = -(-self.slots // 128) * 128
        self.order = [self.plane_at(i) for i in range(self.rings)]
        self.ring = [
            (self.order[i] * self.plane + p, self.order[(i + 1) % self.rings] * self.plane + p)
            for i in range(self.rings)
            for p in range(self.plane)
        ]
        self.paired = self.plane & (self.plane - 1) == 0
        half = self.rings // 2
        onward, reverse = list(range(half, 0, -1)), list(range(half + 1, self.rings))
        self.back = []
        while onward or reverse:
            self.back += onward[:1] + reverse[:1]
            onward, reverse = onward[1:], reverse[1:]
        self.back.append(0)

    def follows(self, step):
        half = self.rings // 2
        sources = [step + 1] if step < half else []
        if step > half + 1 or (step == 0 and self.rings > half + 1):
            sources.append((step - 1) % self.rings)
        return sources

    def shift_back(self, step):
        move = 1 if step <= self.rings // 2 else -1
        return [
            (self.order[i] * self.plane + p, self.order[(i - move) % self.rings] * self.plane + p)
            for i in range(self.rings)
            for p in range(self.plane)
        ]

    def target(self, p, offset):
        return p ^ offset if self.paired else (p + offset) % self.plane

    def target_traced(self, p, offset):
        return p ^ offset if self.paired else lax.rem(p + offset, self.plane)

    def source_traced(self, p, offset):
        return p ^ offset if self.paired else lax.rem(p - offset + self.plane, self.plane)

    def shift_plane(self, offset):
        return [
            (z * self.plane + p, z * self.plane + self.target(p, offset))
            for z in range(self.rings)
            for p in range(self.plane)
        ]

    def plane_at(self, place):
        return 2 * place if 2 * place < self.rings else 2 * self.rings - 1 - 2 * place

    def place_of(self, z):
        half = lax.div(z, 2)
        return jnp.where(lax.rem(z, 2) == 0, half, self.rings - 1 - half)

    def source_plane(self, me, step):
        place = self.place_of(lax.div(me, self.plane))
        place = lax.rem(place - step + self.rings, self.rings)
        doubled = 2 * place
        return jnp.where(doubled < self.rings, doubled, 2 * self.rings - 1 - doubled)


def tables_kernel(
    plan, me_ref, owner_cols, block_cols, tab_ref, held_ref, owner_ref, block_ref, all_ref
):
    me = me_ref[0]
    arcs, links, lanes = plan.arcs, plan.links, tab_ref.shape[1]
    z = lax.div(me, plan.plane)
    span = plan.plane * arcs
    first = pl.multiple_of(z * span, span)
    owner_ref[...] = owner_cols[:, pl.ds(first, span)].T
    block_ref[...] = block_cols[:, pl.ds(first, span)].T
    owners = lax.broadcasted_iota(jnp.int32, (arcs, lanes), 1)
    low = lax.broadcasted_iota(jnp.int32, (arcs, arcs), 0)
    high = lax.broadcasted_iota(jnp.int32, (arcs, arcs), 1)
    before = (high < low).astype(jnp.float32)

    def incidence(row):
        owner = owner_ref[pl.ds(row, arcs), :]
        block = block_ref[pl.ds(row, arcs), :]
        named = jnp.zeros((arcs, lanes), jnp.float32)
        held = jnp.zeros((arcs, lanes), jnp.int32)
        for k in range(links):
            same = owner[:, k : k + 1] == owners
            named = jnp.where(same, 1.0, named)
            held = jnp.where(same, block[:, k : k + 1] + 1, held)
        rank = jnp.dot(before, named, preferred_element_type=jnp.float32).astype(jnp.int32)
        return held, rank

    all_ref[...] = jnp.zeros_like(all_ref)
    for q in range(plan.plane):
        held, rank = incidence(q * arcs)
        for r in range(plan.cap):
            at_rank = jnp.where(rank == r, held, 0)
            all_ref[r * plan.plane + q : r * plan.plane + q + 1, :] = jnp.sum(
                at_rank, axis=0, keepdims=True
            )
    columns = jnp.zeros((held_ref.shape[1], 128), jnp.int32)
    wide = lax.broadcasted_iota(jnp.int32, columns.shape, 1)
    across = lax.broadcasted_iota(jnp.int32, all_ref.shape, 1)
    for s in range(plan.rings):
        column = plan.source_plane(me, s) * plan.plane + lax.rem(me, plan.plane)
        picked = jnp.sum(jnp.where(across == column, all_ref[...], 0), axis=1, keepdims=True)
        columns = jnp.where(wide == s, picked, columns)
    held_ref[...] = columns.T[: held_ref.shape[0]]
    row = pl.multiple_of(lax.rem(me, plan.plane) * arcs, arcs)
    held, rank = incidence(row)
    place = plan.place_of(z)
    other = plan.place_of(lax.div(owners, plan.plane))
    step = lax.rem(place - other + plan.rings, plan.rings)
    here, there = lax.rem(me, plan.plane), lax.rem(owners, plan.plane)
    offset = here ^ there if plan.paired else lax.rem(here - there + plan.plane, plan.plane)
    slot = step * plan.slots + offset * plan.cap + rank
    tab_ref[:arcs, :] = slot
    mine = jnp.zeros((arcs, lanes), jnp.int32)
    owner = owner_ref[pl.ds(row, arcs), :]
    for k in range(links):
        mine = jnp.where(owners == k, owner[:, k : k + 1], mine)
    tab_ref[plan.own_row : plan.own_row + arcs, :] = mine


def make_tables(plan, me, coupling_owner, coupling_block):
    lanes = -(-plan.devices // 128) * 128
    return pl.pallas_call(
        functools.partial(tables_kernel, plan),
        out_shape=[
            jax.ShapeDtypeStruct((2 * plan.arcs, lanes), jnp.int32),
            jax.ShapeDtypeStruct((-(-plan.rings // 8) * 8, plan.padded), jnp.int32),
        ],
        in_specs=[
            pl.BlockSpec(memory_space=SMEM),
            pl.BlockSpec(memory_space=VMEM),
            pl.BlockSpec(memory_space=VMEM),
        ],
        out_specs=[pl.BlockSpec(memory_space=VMEM)] * 2,
        scratch_shapes=[pltpu.VMEM((plan.plane * plan.arcs, plan.links), jnp.int32)] * 2
        + [pltpu.VMEM((plan.padded, lanes), jnp.int32)],
        compiler_params=SMALL,
        name="tables",
    )(me, coupling_owner.T, coupling_block.T)


def pick_kernel(plan, step, me_ref, held_ref, chunk_ref, *out_refs):
    here = lax.rem(me_ref[0], plan.plane)
    for offset, out_ref in enumerate(out_refs):
        q = plan.target_traced(here, offset)
        for r in range(plan.cap):
            block = jnp.maximum(held_ref[step, r * plan.plane + q] - 1, 0)
            out_ref[r] = chunk_ref[block]


def pick(plan, step, me, held, chunk):
    shape = (plan.cap,) + chunk.shape[1:]
    return pl.pallas_call(
        functools.partial(pick_kernel, plan, step),
        out_shape=[pltpu.VMEM(shape, chunk.dtype)] * plan.plane,
        in_specs=[
            pl.BlockSpec(memory_space=SMEM),
            pl.BlockSpec(memory_space=SMEM),
            pl.BlockSpec(memory_space=VMEM),
        ],
        out_specs=[pl.BlockSpec(memory_space=VMEM)] * plan.plane,
        compiler_params=SMALL,
        name="pick",
    )(me, held, in_vmem(chunk))


def narrow_dot(left, right, contract=1):
    product = lax.dot_general(
        left, right, (((contract,), (0,)), ((), ())), preferred_element_type=jnp.float32
    )
    return product.astype(jnp.bfloat16)


def arcs_kernel(plan, tab_ref, *refs):
    count, cap = plan.rings * plan.plane, plan.cap
    arrived_refs = refs[:count]
    panel_ref, factor_ref = refs[count], refs[count + 1]
    out_refs = refs[count + 2 : 2 * count + 2]
    arrived, leaving, fetched, sems = refs[2 * count + 2 :]
    arc = pl.program_id(0)
    rows = arrived.shape[1]

    def inward(s):
        return pltpu.make_async_copy(
            arrived_refs[s], arrived.at[pl.ds(s * cap, cap)], sems.at[s]
        )

    def outward(s):
        return pltpu.make_async_copy(
            leaving.at[pl.ds(s * cap, cap)], out_refs[s], sems.at[s]
        )

    @pl.when(arc == 0)
    def _():
        for s in range(count):
            inward(s).start()
        for s in range(count):
            inward(s).wait()

    group = range(panel_ref.shape[0])
    spots = [[] for _ in group]
    for g in group:
        row = arc * len(group) + g
        for k in range(plan.links):
            spot = tab_ref[row, tab_ref[plan.own_row + row, k]]
            spots[g].append(spot)
            fetched[g, k * rows : (k + 1) * rows, :] = arrived[spot]
    coupled = [narrow_dot(panel_ref[g], fetched[g]) for g in group]
    whitened = [narrow_dot(factor_ref[g], coupled[g]) for g in group]
    smoothed = [narrow_dot(whitened[g], factor_ref[g], 0) for g in group]
    for g in group:
        projected = narrow_dot(smoothed[g], panel_ref[g])
        for k in range(plan.links):
            leaving[spots[g][k]] = projected[:, k * rows : (k + 1) * rows]

    @pl.when(arc == pl.num_programs(0) - 1)
    def _():
        for s in range(count):
            outward(s).start()
        for s in range(count):
            outward(s).wait()


def run_arcs(plan, tab, arrived, coupling_panel, inv_factor):
    arcs, arc_rows, width = coupling_panel.shape
    block = arrived[0].shape[1:]
    total = plan.rings * plan.slots
    group = GROUP if arcs % GROUP == 0 else 1
    anywhere = pl.BlockSpec(memory_space=pl.ANY)
    return pl.pallas_call(
        functools.partial(arcs_kernel, plan),
        grid_spec=pltpu.PrefetchScalarGridSpec(
            num_scalar_prefetch=1,
            grid=(arcs // group,),
            in_specs=[anywhere] * (plan.rings * plan.plane)
            + [
                pl.BlockSpec((group, arc_rows, width), lambda i, t: (i, 0, 0)),
                pl.BlockSpec((group, arc_rows, arc_rows), lambda i, t: (i, 0, 0)),
            ],
            out_specs=[pl.BlockSpec(memory_space=VMEM)] * (plan.rings * plan.plane),
            scratch_shapes=[
                pltpu.VMEM((total,) + block, jnp.bfloat16),
                pltpu.VMEM((total,) + block, jnp.bfloat16),
                pltpu.VMEM((group, width, block[1]), jnp.bfloat16),
                pltpu.SemaphoreType.DMA((plan.rings * plan.plane,)),
            ],
        ),
        out_shape=[pltpu.VMEM((plan.cap,) + block, jnp.bfloat16)] * (plan.rings * plan.plane),
        compiler_params=pltpu.CompilerParams(vmem_limit_bytes=32 << 20),
        name="arcs",
    )(tab, *arrived, coupling_panel, inv_factor)


def add_up(plan, step, me_ref, held_ref, got_refs, part_refs, acc):
    here = lax.rem(me_ref[0], plan.plane)
    start = jnp.zeros(acc.shape, jnp.float32)
    for part_ref in part_refs:
        start = start + part_ref[...].astype(jnp.float32)
    acc[...] = start
    for offset, got_ref in enumerate(got_refs):
        q = plan.source_traced(here, offset)
        for r in range(plan.cap):
            held = held_ref[step, r * plan.plane + q]

            @pl.when(held > 0)
            def _():
                acc[held - 1] += got_ref[r].astype(jnp.float32)


def fold_kernel(plan, step, me_ref, held_ref, *refs):
    got_refs, part_refs = refs[: plan.plane], refs[plan.plane : -2]
    out_ref, acc = refs[-2], refs[-1]
    add_up(plan, step, me_ref, held_ref, got_refs, part_refs, acc)
    out_ref[...] = acc[...].astype(out_ref.dtype)


def image_kernel(plan, both, me_ref, held_ref, field_ref, prior_ref, *refs):
    got_refs, part_refs = refs[: plan.plane], refs[plan.plane : -3]
    image_ref, gram_ref, acc = refs[-3:]
    add_up(plan, 0, me_ref, held_ref, got_refs, part_refs, acc)
    rows = acc.shape[1]
    for b in range(plan.blocks):
        image_ref[b] = acc[b].T + prior_ref[:, b : b + 1] * field_ref[b]
    gram_ref[...] = jnp.zeros_like(gram_ref)
    batch = max(n for n in range(1, 6) if plan.blocks % n == 0)

    @pl.loop(0, plan.blocks, step=batch)
    def _(b):
        field = field_ref[pl.ds(b, batch)].reshape(batch * rows, -1)
        image = image_ref[pl.ds(b, batch)].reshape(batch * rows, -1)
        gram_ref[0] += gram_of(field, image)
        if both:
            gram_ref[1] += gram_of(image, image)


def gram_of(left, right):
    return lax.dot_general(
        left,
        right,
        (((0,), (0,)), ((), ())),
        precision=lax.Precision.HIGHEST,
        preferred_element_type=jnp.float32,
    )


def fold_specs(args):
    return [pl.BlockSpec(memory_space=SMEM)] * 2 + [pl.BlockSpec(memory_space=VMEM)] * (
        len(args) - 2
    )


def fold(plan, step, me, held, got, parts):
    shape = (plan.blocks,) + got[0].shape[1:]
    args = (me, held, *in_vmem(*got, *parts))
    return pl.pallas_call(
        functools.partial(fold_kernel, plan, step),
        out_shape=pltpu.VMEM(shape, jnp.bfloat16),
        in_specs=fold_specs(args),
        out_specs=pl.BlockSpec(memory_space=VMEM),
        scratch_shapes=[pltpu.VMEM(shape, jnp.float32)],
        compiler_params=SMALL,
        name="fold",
    )(*args)


def fold_image(plan, me, held, got, parts, field, prior_cols, both):
    shape, cols = field.shape, field.shape[2]
    args = (me, held, field, prior_cols, *in_vmem(*got, *parts))
    return pl.pallas_call(
        functools.partial(image_kernel, plan, both),
        out_shape=[
            jax.ShapeDtypeStruct(shape, jnp.float32),
            jax.ShapeDtypeStruct((2 if both else 1, cols, cols), jnp.float32),
        ],
        in_specs=fold_specs(args),
        out_specs=[pl.BlockSpec(memory_space=VMEM)] * 2,
        scratch_shapes=[pltpu.VMEM(shape, jnp.float32)],
        compiler_params=SMALL,
        name="image",
    )(*args)


def update_kernel(field_ref, image_ref, sol_ref, res_ref, step_ref, sol_out, res_out):
    blocks, rows, cols = field_ref.shape
    step = step_ref[...]
    size = (blocks * rows, cols)
    moved = times_high(field_ref[...].reshape(size), step).reshape(field_ref.shape)
    sol_out[...] = sol_ref[...] + moved
    moved = times_high(image_ref[...].reshape(size), step).reshape(field_ref.shape)
    res_out[...] = res_ref[...] - moved


def update(field, image, solution_field, residual, step_mat):
    blocks, rows, cols = field.shape
    batch = max(n for n in range(1, 5) if blocks % n == 0)
    spec = pl.BlockSpec((batch, rows, cols), lambda i: (i, 0, 0))
    return pl.pallas_call(
        update_kernel,
        grid=(blocks // batch,),
        out_shape=[jax.ShapeDtypeStruct(field.shape, jnp.float32)] * 2,
        in_specs=[spec] * 4 + [pl.BlockSpec((cols, cols), lambda i: (0, 0))],
        out_specs=[spec] * 2,
        compiler_params=SMALL,
        name="update",
    )(field, image, solution_field, residual, step_mat)


def identity(size):
    rows = lax.broadcasted_iota(jnp.int32, (size, size), 0)
    lanes = lax.broadcasted_iota(jnp.int32, (size, size), 1)
    return jnp.where(rows == lanes, 1.0, 0.0)


def eliminate(matrix):
    size = matrix.shape[0]
    rows = lax.broadcasted_iota(jnp.int32, (size, size), 0)
    lanes = lax.broadcasted_iota(jnp.int32, (size, size), 1)

    def pivot(k, matrix):
        on_row, on_lane = rows == k, lanes == k
        column = jnp.sum(jnp.where(on_lane, matrix, 0.0), axis=1, keepdims=True)
        row = jnp.sum(jnp.where(on_row, matrix, 0.0), axis=0, keepdims=True)
        scale = 1.0 / jnp.sum(jnp.where(on_lane[:1], row, 0.0), axis=1, keepdims=True)
        row = jnp.where(on_lane[:1], 1.0, row) * scale
        rest = jnp.where(on_lane, 0.0, matrix) - column * row
        return jnp.where(on_row, row, rest)

    return lax.fori_loop(0, size, pivot, matrix)


def invert_into(out_refs, matrices):
    size = matrices[0].shape[0]
    eye = identity(size)
    scales, scaled = [], []
    for matrix in matrices:
        diagonal = eye * matrix
        down = lax.rsqrt(jnp.sum(diagonal, axis=1, keepdims=True))
        along = lax.rsqrt(jnp.sum(diagonal, axis=0, keepdims=True))
        scales.append((down, along))
        scaled.append(matrix * down * along)
    off = [matrix - eye for matrix in scaled]
    second = [times_high(e, e) for e in off]
    fourth = [times_high(e, e) for e in second]
    third = [times_high(e, f) for e, f in zip(off, second)]
    guess = [eye - e + f - g for e, f, g in zip(off, second, third)]
    guess = [x + times_high(x, e) for x, e in zip(guess, fourth)]
    left = [eye - times_high(a, x) for a, x in zip(scaled, guess)]
    guess = [x + times_high(x, r) for x, r in zip(guess, left)]
    for out_ref, x, r, a, (down, along) in zip(out_refs, guess, left, scaled, scales):
        out_ref[...] = x * down * along
        worst = jnp.max(jnp.sum(jnp.abs(r), axis=1, keepdims=True))

        @pl.when(jnp.logical_not(worst < 1e-3))
        def _():
            y = eliminate(a)
            y = y + times_high(y, eye - times_high(a, y))
            out_ref[...] = y * down * along


def step_kernel(grams_ref, step_ref, beta_ref, new_ref, first_inv, second_inv):
    res, cross, image = grams_ref[0], grams_ref[1], grams_ref[2]
    invert_into([first_inv, second_inv], [0.5 * (cross + cross.T), 0.5 * (res + res.T)])
    step = times_high(first_inv[...], res)
    step_ref[...] = step
    moved = times_high(cross, step)
    new = res - moved.T - moved + times_high(step.T, times_high(image, step))
    new_ref[...] = new
    beta_ref[...] = times_high(second_inv[...], new)


def last_kernel(grams_ref, res_ref, step_ref, first_inv):
    curv = grams_ref[0]
    invert_into([first_inv], [0.5 * (curv + curv.T)])
    step_ref[...] = times_high(first_inv[...], res_ref[...])


def small_solve(kernel, args, outputs, scratch):
    shape = args[0].shape[1:]
    return pl.pallas_call(
        kernel,
        out_shape=[jax.ShapeDtypeStruct(shape, jnp.float32)] * outputs,
        scratch_shapes=[pltpu.VMEM(shape, jnp.float32)] * scratch,
        compiler_params=SMALL,
        name="solve",
    )(*args)


def trade_plane(plan, buffers):
    moved = [None] * plan.plane
    moved[0] = buffers[0]
    for offset in range(plan.plane - 1, 0, -1):
        moved[offset] = lax.ppermute(buffers[offset], AXES, plan.shift_plane(offset))
    return moved


def gate_kernel(in_ref, out_ref):
    out_ref[0] = in_ref[0]


def gate(me):
    return pl.pallas_call(
        gate_kernel,
        out_shape=jax.ShapeDtypeStruct(me.shape, me.dtype),
        in_specs=[pl.BlockSpec(memory_space=SMEM)],
        out_specs=pl.BlockSpec(memory_space=SMEM),
        compiler_params=SMALL,
        name="gate",
    )(me)


def apply_schur(plan, me, tab, held, field, prior_cols, coupling_panel, inv_factor, both):
    chunk, arrived = field.astype(jnp.bfloat16), []
    for s in range(plan.rings):
        following = None
        if s + 1 < plan.rings:
            following = lax.ppermute(chunk, AXES, plan.ring)
        chosen = pick(plan, s, me, held, chunk)
        arrived += trade_plane(plan, chosen)
        if s + 1 < plan.rings:
            me = gate(me)
        chunk = following
    leaving = run_arcs(plan, tab, arrived, coupling_panel, inv_factor)
    moved, folded = {}, []
    for j, s in enumerate(plan.back):
        buffers = leaving[s * plan.plane : (s + 1) * plan.plane]
        if j >= 2:
            *buffers, _ = lax.optimization_barrier((*buffers, folded[j - 2]))
        got = trade_plane(plan, buffers)
        sources = [moved[source] for source in plan.follows(s)]
        if s:
            me = gate(me)
        if s == 0:
            image, grams = fold_image(plan, me, held, got, sources, field, prior_cols, both)
            return image, grams, me
        folded.append(fold(plan, s, me, held, got, sources))
        moved[s] = lax.ppermute(folded[j], AXES, plan.shift_back(s))


def per_device(
    mesh, right_side, prior_diag, inv_factor, coupling_panel, coupling_owner, coupling_block
):
    plan = Plan(mesh, coupling_panel.shape[0], coupling_owner.shape[1], right_side.shape[0])
    me = lax.axis_index(AXES).astype(jnp.int32).reshape(1)
    tab, held = make_tables(plan, me, coupling_owner, coupling_block)
    prior_cols = prior_diag.T
    solution_field = None
    residual = right_side
    direction = right_side
    start_gram = inner_gram(residual, residual)
    for sweep_index in range(ITERS):
        last = sweep_index + 1 == ITERS
        image_vec, grams, me = apply_schur(
            plan, me, tab, held, direction, prior_cols, coupling_panel, inv_factor, not last
        )
        if last:
            (step_mat,) = small_solve(last_kernel, (sum_all(grams), res_gram), 1, 1)
            return tuple(update(direction, image_vec, solution_field, residual, step_mat))
        grams = jnp.concatenate([start_gram[None], grams], axis=0)
        step_mat, beta_mat, res_gram = small_solve(step_kernel, (sum_all(grams),), 3, 2)
        solution_field = combine_cols(direction, step_mat)
        residual = residual - combine_cols(image_vec, step_mat)
        direction = residual + combine_cols(direction, beta_mat)


def solution(mesh):
    in_specs = (
        P(AXES, None, None),
        P(AXES, None),
        P(AXES, None, None),
        P(AXES, None, None),
        P(),
        P(),
    )
    out_specs = (P(AXES, None, None), P(AXES, None, None))
    return jax.shard_map(
        functools.partial(per_device, mesh),
        mesh=mesh,
        in_specs=in_specs,
        out_specs=out_specs,
        check_vma=False,
    )
```

```python
import functools

import jax
import jax.numpy as jnp
from jax import lax
from jax.experimental import pallas as pl
from jax.experimental.pallas import tpu as pltpu
from jax.sharding import PartitionSpec as P


ITERS = 2
GROUP = 4
AXES = ("arc", "vec")
SMEM = pltpu.MemorySpace.SMEM
VMEM = pltpu.MemorySpace.VMEM


SMALL = pltpu.CompilerParams(vmem_limit_bytes=16 << 20)


def in_vmem(*arrays):
    placed = [pltpu.with_memory_space_constraint(array, pltpu.VMEM) for array in arrays]
    return placed if len(placed) > 1 else placed[0]


def inner_gram(left, right):
    return jnp.einsum("grc,grd->cd", left, right, precision=lax.Precision.HIGHEST)


def combine_cols(field, weights):
    return jnp.einsum("grc,cd->grd", field, weights, precision=lax.Precision.HIGHEST)


def times_high(left, right):
    return jnp.dot(left, right, precision=lax.Precision.HIGHEST)


def trade(buffer):
    return lax.all_to_all(buffer, AXES, split_axis=0, concat_axis=0, tiled=True)


def sum_all(grams):
    device_count = lax.axis_size(AXES)
    count, rows, cols = grams.shape
    pieces = grams.reshape(device_count, count * rows // device_count, cols)
    pieces = trade(pieces)
    shared = jnp.broadcast_to(jnp.sum(pieces, axis=0)[None], pieces.shape)
    return trade(shared).reshape(grams.shape)


class Plan:
    def __init__(self, mesh, arcs_here, links, blocks_here):
        arc, vec = mesh.shape["arc"], mesh.shape["vec"]
        half = max(1, vec // 2)
        self.rings = arc // half if arc % half == 0 else arc
        self.devices = arc * vec
        self.plane = self.devices // self.rings
        self.arcs, self.links, self.blocks = arcs_here, links, blocks_here
        entries = arcs_here * links
        self.cap = (entries + self.devices - 1) // self.devices + 1
        self.slots = self.plane * self.cap
        self.own_row = arcs_here
        self.padded = -(-self.slots // 128) * 128
        self.order = [self.plane_at(i) for i in range(self.rings)]
        self.ring = [
            (self.order[i] * self.plane + p, self.order[(i + 1) % self.rings] * self.plane + p)
            for i in range(self.rings)
            for p in range(self.plane)
        ]
        self.paired = self.plane & (self.plane - 1) == 0
        half = self.rings // 2
        onward, reverse = list(range(half, 0, -1)), list(range(half + 1, self.rings))
        self.back = []
        while onward or reverse:
            self.back += onward[:1] + reverse[:1]
            onward, reverse = onward[1:], reverse[1:]
        self.back.append(0)

    def follows(self, step):
        half = self.rings // 2
        sources = [step + 1] if step < half else []
        if step > half + 1 or (step == 0 and self.rings > half + 1):
            sources.append((step - 1) % self.rings)
        return sources

    def shift_back(self, step):
        move = 1 if step <= self.rings // 2 else -1
        return [
            (self.order[i] * self.plane + p, self.order[(i - move) % self.rings] * self.plane + p)
            for i in range(self.rings)
            for p in range(self.plane)
        ]

    def target(self, p, offset):
        return p ^ offset if self.paired else (p + offset) % self.plane

    def target_traced(self, p, offset):
        return p ^ offset if self.paired else lax.rem(p + offset, self.plane)

    def source_traced(self, p, offset):
        return p ^ offset if self.paired else lax.rem(p - offset + self.plane, self.plane)

    def shift_plane(self, offset):
        return [
            (z * self.plane + p, z * self.plane + self.target(p, offset))
            for z in range(self.rings)
            for p in range(self.plane)
        ]

    def plane_at(self, place):
        return 2 * place if 2 * place < self.rings else 2 * self.rings - 1 - 2 * place

    def place_of(self, z):
        half = lax.div(z, 2)
        return jnp.where(lax.rem(z, 2) == 0, half, self.rings - 1 - half)

    def source_plane(self, me, step):
        place = self.place_of(lax.div(me, self.plane))
        place = lax.rem(place - step + self.rings, self.rings)
        doubled = 2 * place
        return jnp.where(doubled < self.rings, doubled, 2 * self.rings - 1 - doubled)


def tables_kernel(
    plan, me_ref, owner_cols, block_cols, tab_ref, held_ref, owner_ref, block_ref, all_ref
):
    me = me_ref[0]
    arcs, links, lanes = plan.arcs, plan.links, tab_ref.shape[1]
    z = lax.div(me, plan.plane)
    span = plan.plane * arcs
    first = pl.multiple_of(z * span, span)
    owner_ref[...] = owner_cols[:, pl.ds(first, span)].T
    block_ref[...] = block_cols[:, pl.ds(first, span)].T
    owners = lax.broadcasted_iota(jnp.int32, (arcs, lanes), 1)
    low = lax.broadcasted_iota(jnp.int32, (arcs, arcs), 0)
    high = lax.broadcasted_iota(jnp.int32, (arcs, arcs), 1)
    before = (high < low).astype(jnp.float32)

    def incidence(row):
        owner = owner_ref[pl.ds(row, arcs), :]
        block = block_ref[pl.ds(row, arcs), :]
        named = jnp.zeros((arcs, lanes), jnp.float32)
        held = jnp.zeros((arcs, lanes), jnp.int32)
        for k in range(links):
            same = owner[:, k : k + 1] == owners
            named = jnp.where(same, 1.0, named)
            held = jnp.where(same, block[:, k : k + 1] + 1, held)
        rank = jnp.dot(before, named, preferred_element_type=jnp.float32).astype(jnp.int32)
        return held, rank

    all_ref[...] = jnp.zeros_like(all_ref)
    for q in range(plan.plane):
        held, rank = incidence(q * arcs)
        for r in range(plan.cap):
            at_rank = jnp.where(rank == r, held, 0)
            all_ref[r * plan.plane + q : r * plan.plane + q + 1, :] = jnp.sum(
                at_rank, axis=0, keepdims=True
            )
    columns = jnp.zeros((held_ref.shape[1], 128), jnp.int32)
    wide = lax.broadcasted_iota(jnp.int32, columns.shape, 1)
    across = lax.broadcasted_iota(jnp.int32, all_ref.shape, 1)
    for s in range(plan.rings):
        column = plan.source_plane(me, s) * plan.plane + lax.rem(me, plan.plane)
        picked = jnp.sum(jnp.where(across == column, all_ref[...], 0), axis=1, keepdims=True)
        columns = jnp.where(wide == s, picked, columns)
    held_ref[...] = columns.T[: held_ref.shape[0]]
    row = pl.multiple_of(lax.rem(me, plan.plane) * arcs, arcs)
    held, rank = incidence(row)
    place = plan.place_of(z)
    other = plan.place_of(lax.div(owners, plan.plane))
    step = lax.rem(place - other + plan.rings, plan.rings)
    here, there = lax.rem(me, plan.plane), lax.rem(owners, plan.plane)
    offset = here ^ there if plan.paired else lax.rem(here - there + plan.plane, plan.plane)
    slot = step * plan.slots + offset * plan.cap + rank
    tab_ref[:arcs, :] = slot
    mine = jnp.zeros((arcs, lanes), jnp.int32)
    owner = owner_ref[pl.ds(row, arcs), :]
    for k in range(links):
        mine = jnp.where(owners == k, owner[:, k : k + 1], mine)
    tab_ref[plan.own_row : plan.own_row + arcs, :] = mine


def make_tables(plan, me, coupling_owner, coupling_block):
    lanes = -(-plan.devices // 128) * 128
    return pl.pallas_call(
        functools.partial(tables_kernel, plan),
        out_shape=[
            jax.ShapeDtypeStruct((2 * plan.arcs, lanes), jnp.int32),
            jax.ShapeDtypeStruct((-(-plan.rings // 8) * 8, plan.padded), jnp.int32),
        ],
        in_specs=[
            pl.BlockSpec(memory_space=SMEM),
            pl.BlockSpec(memory_space=VMEM),
            pl.BlockSpec(memory_space=VMEM),
        ],
        out_specs=[pl.BlockSpec(memory_space=VMEM)] * 2,
        scratch_shapes=[pltpu.VMEM((plan.plane * plan.arcs, plan.links), jnp.int32)] * 2
        + [pltpu.VMEM((plan.padded, lanes), jnp.int32)],
        compiler_params=SMALL,
        name="tables",
    )(me, coupling_owner.T, coupling_block.T)


def pick_kernel(plan, step, me_ref, held_ref, chunk_ref, *out_refs):
    here = lax.rem(me_ref[0], plan.plane)
    for offset, out_ref in enumerate(out_refs):
        q = plan.target_traced(here, offset)
        for r in range(plan.cap):
            block = jnp.maximum(held_ref[step, r * plan.plane + q] - 1, 0)
            out_ref[r] = chunk_ref[block]


def pick(plan, step, me, held, chunk):
    shape = (plan.cap,) + chunk.shape[1:]
    return pl.pallas_call(
        functools.partial(pick_kernel, plan, step),
        out_shape=[pltpu.VMEM(shape, chunk.dtype)] * plan.plane,
        in_specs=[
            pl.BlockSpec(memory_space=SMEM),
            pl.BlockSpec(memory_space=SMEM),
            pl.BlockSpec(memory_space=VMEM),
        ],
        out_specs=[pl.BlockSpec(memory_space=VMEM)] * plan.plane,
        compiler_params=SMALL,
        name="pick",
    )(me, held, in_vmem(chunk))


def narrow_dot(left, right, contract=1):
    product = lax.dot_general(
        left, right, (((contract,), (0,)), ((), ())), preferred_element_type=jnp.float32
    )
    return product.astype(jnp.bfloat16)


def arcs_kernel(plan, tab_ref, *refs):
    count, cap = plan.rings * plan.plane, plan.cap
    arrived_refs = refs[:count]
    panel_ref, factor_ref = refs[count], refs[count + 1]
    out_refs = refs[count + 2 : 2 * count + 2]
    arrived, leaving, fetched, sems = refs[2 * count + 2 :]
    arc = pl.program_id(0)
    rows = arrived.shape[1]

    def inward(s):
        return pltpu.make_async_copy(
            arrived_refs[s], arrived.at[pl.ds(s * cap, cap)], sems.at[s]
        )

    def outward(s):
        return pltpu.make_async_copy(
            leaving.at[pl.ds(s * cap, cap)], out_refs[s], sems.at[s]
        )

    @pl.when(arc == 0)
    def _():
        for s in range(count):
            inward(s).start()
        for s in range(count):
            inward(s).wait()

    group = range(panel_ref.shape[0])
    spots = [[] for _ in group]
    for g in group:
        row = arc * len(group) + g
        for k in range(plan.links):
            spot = tab_ref[row, tab_ref[plan.own_row + row, k]]
            spots[g].append(spot)
            fetched[g, k * rows : (k + 1) * rows, :] = arrived[spot]
    coupled = [narrow_dot(panel_ref[g], fetched[g]) for g in group]
    whitened = [narrow_dot(factor_ref[g], coupled[g]) for g in group]
    smoothed = [narrow_dot(whitened[g], factor_ref[g], 0) for g in group]
    for g in group:
        projected = narrow_dot(smoothed[g], panel_ref[g])
        for k in range(plan.links):
            leaving[spots[g][k]] = projected[:, k * rows : (k + 1) * rows]

    @pl.when(arc == pl.num_programs(0) - 1)
    def _():
        for s in range(count):
            outward(s).start()
        for s in range(count):
            outward(s).wait()


def run_arcs(plan, tab, arrived, coupling_panel, inv_factor):
    arcs, arc_rows, width = coupling_panel.shape
    block = arrived[0].shape[1:]
    total = plan.rings * plan.slots
    group = GROUP if arcs % GROUP == 0 else 1
    anywhere = pl.BlockSpec(memory_space=pl.ANY)
    return pl.pallas_call(
        functools.partial(arcs_kernel, plan),
        grid_spec=pltpu.PrefetchScalarGridSpec(
            num_scalar_prefetch=1,
            grid=(arcs // group,),
            in_specs=[anywhere] * (plan.rings * plan.plane)
            + [
                pl.BlockSpec((group, arc_rows, width), lambda i, t: (i, 0, 0)),
                pl.BlockSpec((group, arc_rows, arc_rows), lambda i, t: (i, 0, 0)),
            ],
            out_specs=[anywhere] * (plan.rings * plan.plane),
            scratch_shapes=[
                pltpu.VMEM((total,) + block, jnp.bfloat16),
                pltpu.VMEM((total,) + block, jnp.bfloat16),
                pltpu.VMEM((group, width, block[1]), jnp.bfloat16),
                pltpu.SemaphoreType.DMA((plan.rings * plan.plane,)),
            ],
        ),
        out_shape=[jax.ShapeDtypeStruct((plan.cap,) + block, jnp.bfloat16)]
        * (plan.rings * plan.plane),
        name="arcs",
    )(tab, *arrived, coupling_panel, inv_factor)


def add_up(plan, step, me_ref, held_ref, got_refs, part_refs, acc):
    here = lax.rem(me_ref[0], plan.plane)
    start = jnp.zeros(acc.shape, jnp.float32)
    for part_ref in part_refs:
        start = start + part_ref[...].astype(jnp.float32)
    acc[...] = start
    for offset, got_ref in enumerate(got_refs):
        q = plan.source_traced(here, offset)
        for r in range(plan.cap):
            held = held_ref[step, r * plan.plane + q]

            @pl.when(held > 0)
            def _():
                acc[held - 1] += got_ref[r].astype(jnp.float32)


def fold_kernel(plan, step, me_ref, held_ref, *refs):
    got_refs, part_refs = refs[: plan.plane], refs[plan.plane : -2]
    out_ref, acc = refs[-2], refs[-1]
    add_up(plan, step, me_ref, held_ref, got_refs, part_refs, acc)
    out_ref[...] = acc[...].astype(out_ref.dtype)


def image_kernel(plan, both, me_ref, held_ref, field_ref, prior_ref, *refs):
    got_refs, part_refs = refs[: plan.plane], refs[plan.plane : -3]
    image_ref, gram_ref, acc = refs[-3:]
    add_up(plan, 0, me_ref, held_ref, got_refs, part_refs, acc)
    rows = acc.shape[1]
    for b in range(plan.blocks):
        image_ref[b] = acc[b].T + prior_ref[:, b : b + 1] * field_ref[b]
    gram_ref[...] = jnp.zeros_like(gram_ref)
    batch = max(n for n in range(1, 6) if plan.blocks % n == 0)

    @pl.loop(0, plan.blocks, step=batch)
    def _(b):
        field = field_ref[pl.ds(b, batch)].reshape(batch * rows, -1)
        image = image_ref[pl.ds(b, batch)].reshape(batch * rows, -1)
        gram_ref[0] += gram_of(field, image)
        if both:
            gram_ref[1] += gram_of(image, image)


def gram_of(left, right):
    return lax.dot_general(
        left,
        right,
        (((0,), (0,)), ((), ())),
        precision=lax.Precision.HIGHEST,
        preferred_element_type=jnp.float32,
    )


def fold_specs(args):
    return [pl.BlockSpec(memory_space=SMEM)] * 2 + [pl.BlockSpec(memory_space=VMEM)] * (
        len(args) - 2
    )


def fold(plan, step, me, held, got, parts):
    shape = (plan.blocks,) + got[0].shape[1:]
    args = (me, held, *in_vmem(*got, *parts))
    return pl.pallas_call(
        functools.partial(fold_kernel, plan, step),
        out_shape=pltpu.VMEM(shape, jnp.bfloat16),
        in_specs=fold_specs(args),
        out_specs=pl.BlockSpec(memory_space=VMEM),
        scratch_shapes=[pltpu.VMEM(shape, jnp.float32)],
        compiler_params=SMALL,
        name="fold",
    )(*args)


def fold_image(plan, me, held, got, parts, field, prior_cols, both):
    shape, cols = field.shape, field.shape[2]
    args = (me, held, field, prior_cols, *in_vmem(*got, *parts))
    return pl.pallas_call(
        functools.partial(image_kernel, plan, both),
        out_shape=[
            jax.ShapeDtypeStruct(shape, jnp.float32),
            jax.ShapeDtypeStruct((2 if both else 1, cols, cols), jnp.float32),
        ],
        in_specs=fold_specs(args),
        out_specs=[pl.BlockSpec(memory_space=VMEM)] * 2,
        scratch_shapes=[pltpu.VMEM(shape, jnp.float32)],
        compiler_params=SMALL,
        name="image",
    )(*args)


def update_kernel(field_ref, image_ref, sol_ref, res_ref, step_ref, sol_out, res_out):
    blocks, rows, cols = field_ref.shape
    step = step_ref[...]
    size = (blocks * rows, cols)
    moved = times_high(field_ref[...].reshape(size), step).reshape(field_ref.shape)
    sol_out[...] = sol_ref[...] + moved
    moved = times_high(image_ref[...].reshape(size), step).reshape(field_ref.shape)
    res_out[...] = res_ref[...] - moved


def update(field, image, solution_field, residual, step_mat):
    blocks, rows, cols = field.shape
    batch = max(n for n in range(1, 5) if blocks % n == 0)
    spec = pl.BlockSpec((batch, rows, cols), lambda i: (i, 0, 0))
    return pl.pallas_call(
        update_kernel,
        grid=(blocks // batch,),
        out_shape=[jax.ShapeDtypeStruct(field.shape, jnp.float32)] * 2,
        in_specs=[spec] * 4 + [pl.BlockSpec((cols, cols), lambda i: (0, 0))],
        out_specs=[spec] * 2,
        name="update",
    )(field, image, solution_field, residual, step_mat)


def identity(size):
    rows = lax.broadcasted_iota(jnp.int32, (size, size), 0)
    lanes = lax.broadcasted_iota(jnp.int32, (size, size), 1)
    return jnp.where(rows == lanes, 1.0, 0.0)


def eliminate(matrix):
    size = matrix.shape[0]
    rows = lax.broadcasted_iota(jnp.int32, (size, size), 0)
    lanes = lax.broadcasted_iota(jnp.int32, (size, size), 1)

    def pivot(k, matrix):
        on_row, on_lane = rows == k, lanes == k
        column = jnp.sum(jnp.where(on_lane, matrix, 0.0), axis=1, keepdims=True)
        row = jnp.sum(jnp.where(on_row, matrix, 0.0), axis=0, keepdims=True)
        scale = 1.0 / jnp.sum(jnp.where(on_lane[:1], row, 0.0), axis=1, keepdims=True)
        row = jnp.where(on_lane[:1], 1.0, row) * scale
        rest = jnp.where(on_lane, 0.0, matrix) - column * row
        return jnp.where(on_row, row, rest)

    return lax.fori_loop(0, size, pivot, matrix)


def invert_into(out_refs, matrices):
    size = matrices[0].shape[0]
    eye = identity(size)
    scales, scaled = [], []
    for matrix in matrices:
        diagonal = eye * matrix
        down = lax.rsqrt(jnp.sum(diagonal, axis=1, keepdims=True))
        along = lax.rsqrt(jnp.sum(diagonal, axis=0, keepdims=True))
        scales.append((down, along))
        scaled.append(matrix * down * along)
    off = [matrix - eye for matrix in scaled]
    second = [times_high(e, e) for e in off]
    fourth = [times_high(e, e) for e in second]
    third = [times_high(e, f) for e, f in zip(off, second)]
    guess = [eye - e + f - g for e, f, g in zip(off, second, third)]
    guess = [x + times_high(x, e) for x, e in zip(guess, fourth)]
    left = [eye - times_high(a, x) for a, x in zip(scaled, guess)]
    guess = [x + times_high(x, r) for x, r in zip(guess, left)]
    for out_ref, x, r, a, (down, along) in zip(out_refs, guess, left, scaled, scales):
        out_ref[...] = x * down * along
        worst = jnp.max(jnp.sum(jnp.abs(r), axis=1, keepdims=True))

        @pl.when(jnp.logical_not(worst < 1e-3))
        def _():
            y = eliminate(a)
            y = y + times_high(y, eye - times_high(a, y))
            out_ref[...] = y * down * along


def step_kernel(grams_ref, res_ref, step_ref, beta_ref, new_ref, first_inv, second_inv):
    res, cross, image = res_ref[...], grams_ref[0], grams_ref[1]
    invert_into([first_inv, second_inv], [0.5 * (cross + cross.T), 0.5 * (res + res.T)])
    step = times_high(first_inv[...], res)
    step_ref[...] = step
    moved = times_high(cross, step)
    new = res - moved.T - moved + times_high(step.T, times_high(image, step))
    new_ref[...] = new
    beta_ref[...] = times_high(second_inv[...], new)


def last_kernel(grams_ref, res_ref, step_ref, first_inv):
    curv = grams_ref[0]
    invert_into([first_inv], [0.5 * (curv + curv.T)])
    step_ref[...] = times_high(first_inv[...], res_ref[...])


def small_solve(kernel, args, outputs, scratch):
    shape = args[0].shape[1:]
    return pl.pallas_call(
        kernel,
        out_shape=[jax.ShapeDtypeStruct(shape, jnp.float32)] * outputs,
        scratch_shapes=[pltpu.VMEM(shape, jnp.float32)] * scratch,
        compiler_params=SMALL,
        name="solve",
    )(*args)


def trade_plane(plan, buffers):
    moved = [None] * plan.plane
    moved[0] = buffers[0]
    for offset in range(plan.plane - 1, 0, -1):
        moved[offset] = lax.ppermute(buffers[offset], AXES, plan.shift_plane(offset))
    return moved


def gate_kernel(in_ref, out_ref):
    out_ref[0] = in_ref[0]


def gate(me):
    return pl.pallas_call(
        gate_kernel,
        out_shape=jax.ShapeDtypeStruct(me.shape, me.dtype),
        in_specs=[pl.BlockSpec(memory_space=SMEM)],
        out_specs=pl.BlockSpec(memory_space=SMEM),
        compiler_params=SMALL,
        name="gate",
    )(me)


def apply_schur(plan, me, tab, held, field, prior_cols, coupling_panel, inv_factor, both):
    chunk, arrived = field.astype(jnp.bfloat16), []
    for s in range(plan.rings):
        following = None
        if s + 1 < plan.rings:
            following = lax.ppermute(chunk, AXES, plan.ring)
        chosen = pick(plan, s, me, held, chunk)
        arrived += trade_plane(plan, chosen)
        if s + 1 < plan.rings:
            me = gate(me)
        chunk = following
    leaving = run_arcs(plan, tab, arrived, coupling_panel, inv_factor)
    moved, folded = {}, []
    for j, s in enumerate(plan.back):
        buffers = leaving[s * plan.plane : (s + 1) * plan.plane]
        if j >= 2:
            *buffers, _ = lax.optimization_barrier((*buffers, folded[j - 2]))
        got = trade_plane(plan, buffers)
        sources = [moved[source] for source in plan.follows(s)]
        if s:
            me = gate(me)
        if s == 0:
            image, grams = fold_image(plan, me, held, got, sources, field, prior_cols, both)
            return image, grams, me
        folded.append(fold(plan, s, me, held, got, sources))
        moved[s] = lax.ppermute(folded[j], AXES, plan.shift_back(s))


def per_device(
    mesh, right_side, prior_diag, inv_factor, coupling_panel, coupling_owner, coupling_block
):
    plan = Plan(mesh, coupling_panel.shape[0], coupling_owner.shape[1], right_side.shape[0])
    me = lax.axis_index(AXES).astype(jnp.int32).reshape(1)
    tab, held = make_tables(plan, me, coupling_owner, coupling_block)
    prior_cols = prior_diag.T
    solution_field = None
    residual = right_side
    direction = right_side
    res_gram = sum_all(inner_gram(residual, residual)[None])[0]
    for sweep_index in range(ITERS):
        last = sweep_index + 1 == ITERS
        image_vec, grams, me = apply_schur(
            plan, me, tab, held, direction, prior_cols, coupling_panel, inv_factor, not last
        )
        if last:
            (step_mat,) = small_solve(last_kernel, (sum_all(grams), res_gram), 1, 1)
            return tuple(update(direction, image_vec, solution_field, residual, step_mat))
        grams = sum_all(grams)
        step_mat, beta_mat, res_gram = small_solve(step_kernel, (grams, res_gram), 3, 2)
        solution_field = combine_cols(direction, step_mat)
        residual = residual - combine_cols(image_vec, step_mat)
        direction = residual + combine_cols(direction, beta_mat)


def solution(mesh):
    in_specs = (
        P(AXES, None, None),
        P(AXES, None),
        P(AXES, None, None),
        P(AXES, None, None),
        P(),
        P(),
    )
    out_specs = (P(AXES, None, None), P(AXES, None, None))
    return jax.shard_map(
        functools.partial(per_device, mesh),
        mesh=mesh,
        in_specs=in_specs,
        out_specs=out_specs,
        check_vma=False,
    )
```

```python
import functools

import jax
import jax.numpy as jnp
from jax import lax
from jax.experimental import pallas as pl
from jax.experimental.pallas import tpu as pltpu
from jax.sharding import PartitionSpec as P


BLEND = 0.5
GROUP = 4
AXES = ("arc", "vec")
SMEM = pltpu.MemorySpace.SMEM
VMEM = pltpu.MemorySpace.VMEM


SMALL = pltpu.CompilerParams(vmem_limit_bytes=16 << 20)


def in_vmem(*arrays):
    placed = [pltpu.with_memory_space_constraint(array, pltpu.VMEM) for array in arrays]
    return placed if len(placed) > 1 else placed[0]


def inner_gram(left, right):
    return jnp.einsum("grc,grd->cd", left, right, precision=lax.Precision.HIGHEST)


def combine_cols(field, weights):
    return jnp.einsum("grc,cd->grd", field, weights, precision=lax.Precision.HIGHEST)


def times_high(left, right):
    return jnp.dot(left, right, precision=lax.Precision.HIGHEST)


def trade(buffer):
    return lax.all_to_all(buffer, AXES, split_axis=0, concat_axis=0, tiled=True)


def sum_all(grams):
    device_count = lax.axis_size(AXES)
    count, rows, cols = grams.shape
    pieces = grams.reshape(device_count, count * rows // device_count, cols)
    pieces = trade(pieces)
    shared = jnp.broadcast_to(jnp.sum(pieces, axis=0)[None], pieces.shape)
    return trade(shared).reshape(grams.shape)


class Plan:
    def __init__(self, mesh, arcs_here, links, blocks_here):
        arc, vec = mesh.shape["arc"], mesh.shape["vec"]
        half = max(1, vec // 2)
        self.rings = arc // half if arc % half == 0 else arc
        self.devices = arc * vec
        self.plane = self.devices // self.rings
        self.arcs, self.links, self.blocks = arcs_here, links, blocks_here
        entries = arcs_here * links
        self.cap = (entries + self.devices - 1) // self.devices + 1
        self.slots = self.plane * self.cap
        self.own_row = arcs_here
        self.padded = -(-self.slots // 128) * 128
        self.order = [self.plane_at(i) for i in range(self.rings)]
        self.ring = [
            (self.order[i] * self.plane + p, self.order[(i + 1) % self.rings] * self.plane + p)
            for i in range(self.rings)
            for p in range(self.plane)
        ]
        self.paired = self.plane & (self.plane - 1) == 0
        half = self.rings // 2
        onward, reverse = list(range(half, 0, -1)), list(range(half + 1, self.rings))
        self.back = []
        while onward or reverse:
            self.back += onward[:1] + reverse[:1]
            onward, reverse = onward[1:], reverse[1:]
        self.back.append(0)

    def follows(self, step):
        half = self.rings // 2
        sources = [step + 1] if step < half else []
        if step > half + 1 or (step == 0 and self.rings > half + 1):
            sources.append((step - 1) % self.rings)
        return sources

    def shift_back(self, step):
        move = 1 if step <= self.rings // 2 else -1
        return [
            (self.order[i] * self.plane + p, self.order[(i - move) % self.rings] * self.plane + p)
            for i in range(self.rings)
            for p in range(self.plane)
        ]

    def target(self, p, offset):
        return p ^ offset if self.paired else (p + offset) % self.plane

    def target_traced(self, p, offset):
        return p ^ offset if self.paired else lax.rem(p + offset, self.plane)

    def source_traced(self, p, offset):
        return p ^ offset if self.paired else lax.rem(p - offset + self.plane, self.plane)

    def shift_plane(self, offset):
        return [
            (z * self.plane + p, z * self.plane + self.target(p, offset))
            for z in range(self.rings)
            for p in range(self.plane)
        ]

    def plane_at(self, place):
        return 2 * place if 2 * place < self.rings else 2 * self.rings - 1 - 2 * place

    def place_of(self, z):
        half = lax.div(z, 2)
        return jnp.where(lax.rem(z, 2) == 0, half, self.rings - 1 - half)

    def source_plane(self, me, step):
        place = self.place_of(lax.div(me, self.plane))
        place = lax.rem(place - step + self.rings, self.rings)
        doubled = 2 * place
        return jnp.where(doubled < self.rings, doubled, 2 * self.rings - 1 - doubled)


def tables_kernel(
    plan, me_ref, owner_cols, block_cols, tab_ref, held_ref, owner_ref, block_ref, all_ref
):
    me = me_ref[0]
    arcs, links, lanes = plan.arcs, plan.links, tab_ref.shape[1]
    z = lax.div(me, plan.plane)
    span = plan.plane * arcs
    first = pl.multiple_of(z * span, span)
    owner_ref[...] = owner_cols[:, pl.ds(first, span)].T
    block_ref[...] = block_cols[:, pl.ds(first, span)].T
    owners = lax.broadcasted_iota(jnp.int32, (arcs, lanes), 1)
    low = lax.broadcasted_iota(jnp.int32, (arcs, arcs), 0)
    high = lax.broadcasted_iota(jnp.int32, (arcs, arcs), 1)
    before = (high < low).astype(jnp.float32)

    def incidence(row):
        owner = owner_ref[pl.ds(row, arcs), :]
        block = block_ref[pl.ds(row, arcs), :]
        named = jnp.zeros((arcs, lanes), jnp.float32)
        held = jnp.zeros((arcs, lanes), jnp.int32)
        for k in range(links):
            same = owner[:, k : k + 1] == owners
            named = jnp.where(same, 1.0, named)
            held = jnp.where(same, block[:, k : k + 1] + 1, held)
        rank = jnp.dot(before, named, preferred_element_type=jnp.float32).astype(jnp.int32)
        return held, rank

    all_ref[...] = jnp.zeros_like(all_ref)
    for q in range(plan.plane):
        held, rank = incidence(q * arcs)
        for r in range(plan.cap):
            at_rank = jnp.where(rank == r, held, 0)
            all_ref[r * plan.plane + q : r * plan.plane + q + 1, :] = jnp.sum(
                at_rank, axis=0, keepdims=True
            )
    columns = jnp.zeros((held_ref.shape[1], 128), jnp.int32)
    wide = lax.broadcasted_iota(jnp.int32, columns.shape, 1)
    across = lax.broadcasted_iota(jnp.int32, all_ref.shape, 1)
    for s in range(plan.rings):
        column = plan.source_plane(me, s) * plan.plane + lax.rem(me, plan.plane)
        picked = jnp.sum(jnp.where(across == column, all_ref[...], 0), axis=1, keepdims=True)
        columns = jnp.where(wide == s, picked, columns)
    held_ref[...] = columns.T[: held_ref.shape[0]]
    row = pl.multiple_of(lax.rem(me, plan.plane) * arcs, arcs)
    held, rank = incidence(row)
    place = plan.place_of(z)
    other = plan.place_of(lax.div(owners, plan.plane))
    step = lax.rem(place - other + plan.rings, plan.rings)
    here, there = lax.rem(me, plan.plane), lax.rem(owners, plan.plane)
    offset = here ^ there if plan.paired else lax.rem(here - there + plan.plane, plan.plane)
    slot = step * plan.slots + offset * plan.cap + rank
    tab_ref[:arcs, :] = slot
    mine = jnp.zeros((arcs, lanes), jnp.int32)
    owner = owner_ref[pl.ds(row, arcs), :]
    for k in range(links):
        mine = jnp.where(owners == k, owner[:, k : k + 1], mine)
    tab_ref[plan.own_row : plan.own_row + arcs, :] = mine


def make_tables(plan, me, coupling_owner, coupling_block):
    lanes = -(-plan.devices // 128) * 128
    return pl.pallas_call(
        functools.partial(tables_kernel, plan),
        out_shape=[
            jax.ShapeDtypeStruct((2 * plan.arcs, lanes), jnp.int32),
            jax.ShapeDtypeStruct((-(-plan.rings // 8) * 8, plan.padded), jnp.int32),
        ],
        in_specs=[
            pl.BlockSpec(memory_space=SMEM),
            pl.BlockSpec(memory_space=VMEM),
            pl.BlockSpec(memory_space=VMEM),
        ],
        out_specs=[pl.BlockSpec(memory_space=VMEM)] * 2,
        scratch_shapes=[pltpu.VMEM((plan.plane * plan.arcs, plan.links), jnp.int32)] * 2
        + [pltpu.VMEM((plan.padded, lanes), jnp.int32)],
        compiler_params=SMALL,
        name="tables",
    )(me, coupling_owner.T, coupling_block.T)


def pick_kernel(plan, step, me_ref, held_ref, chunk_ref, *out_refs):
    here = lax.rem(me_ref[0], plan.plane)
    for offset, out_ref in enumerate(out_refs):
        q = plan.target_traced(here, offset)
        for r in range(plan.cap):
            block = jnp.maximum(held_ref[step, r * plan.plane + q] - 1, 0)
            out_ref[r] = chunk_ref[block]


def pick(plan, step, me, held, chunk):
    shape = (plan.cap,) + chunk.shape[1:]
    return pl.pallas_call(
        functools.partial(pick_kernel, plan, step),
        out_shape=[pltpu.VMEM(shape, chunk.dtype)] * plan.plane,
        in_specs=[
            pl.BlockSpec(memory_space=SMEM),
            pl.BlockSpec(memory_space=SMEM),
            pl.BlockSpec(memory_space=VMEM),
        ],
        out_specs=[pl.BlockSpec(memory_space=VMEM)] * plan.plane,
        compiler_params=SMALL,
        name="pick",
    )(me, held, in_vmem(chunk))


def narrow_dot(left, right, contract=1):
    product = lax.dot_general(
        left, right, (((contract,), (0,)), ((), ())), preferred_element_type=jnp.float32
    )
    return product.astype(jnp.bfloat16)


def mix_in(earlier, fresh, mix):
    def halves(wide):
        high = wide.astype(jnp.bfloat16)
        return high, (wide - high.astype(jnp.float32)).astype(jnp.bfloat16)

    def product(left, right):
        return jnp.dot(left, right, preferred_element_type=jnp.float32)

    high, low = halves(jnp.concatenate([earlier, fresh], axis=1))
    mix_high, mix_low = halves(mix)
    return product(high, mix_high) + (product(high, mix_low) + product(low, mix_high))


def arcs_kernel(plan, mixed, tab_ref, *refs):
    count, cap = plan.rings * plan.plane, plan.cap
    arrived_refs = refs[:count]
    panel_ref, factor_ref = refs[count], refs[count + 1]
    extra = refs[count + 2 : -4 - count] if mixed else ()
    out_refs = refs[-4 - count : -4] if mixed else refs[count + 2 : -5]
    arrived, leaving, fetched, sems = refs[-4:]
    arc = pl.program_id(0)
    rows = arrived.shape[1]

    def inward(s):
        return pltpu.make_async_copy(
            arrived_refs[s], arrived.at[pl.ds(s * cap, cap)], sems.at[s]
        )

    def outward(s):
        return pltpu.make_async_copy(
            leaving.at[pl.ds(s * cap, cap)], out_refs[s], sems.at[s]
        )

    @pl.when(arc == 0)
    def _():
        for s in range(count):
            inward(s).start()
        for s in range(count):
            inward(s).wait()

    group = range(panel_ref.shape[0])
    spots = [[] for _ in group]
    for g in group:
        row = arc * len(group) + g
        for k in range(plan.links):
            spot = tab_ref[row, tab_ref[plan.own_row + row, k]]
            spots[g].append(spot)
            fetched[g, k * rows : (k + 1) * rows, :] = arrived[spot]
    coupled = []
    for g in group:
        wide = jnp.dot(panel_ref[g], fetched[g], preferred_element_type=jnp.float32)
        if mixed:
            wide = mix_in(extra[0][g], wide, extra[1][...])
        else:
            refs[-5][g] = wide
        coupled.append(wide.astype(jnp.bfloat16))
    whitened = [narrow_dot(factor_ref[g], coupled[g]) for g in group]
    smoothed = [narrow_dot(whitened[g], factor_ref[g], 0) for g in group]
    for g in group:
        projected = narrow_dot(smoothed[g], panel_ref[g])
        for k in range(plan.links):
            leaving[spots[g][k]] = projected[:, k * rows : (k + 1) * rows]

    @pl.when(arc == pl.num_programs(0) - 1)
    def _():
        for s in range(count):
            outward(s).start()
        for s in range(count):
            outward(s).wait()


def run_arcs(plan, tab, arrived, coupling_panel, inv_factor, extra):
    arcs, arc_rows, width = coupling_panel.shape
    block = arrived[0].shape[1:]
    total = plan.rings * plan.slots
    group = GROUP if arcs % GROUP == 0 else 1
    anywhere = pl.BlockSpec(memory_space=pl.ANY)
    wide = pl.BlockSpec((group, arc_rows, block[1]), lambda i, t: (i, 0, 0))
    return pl.pallas_call(
        functools.partial(arcs_kernel, plan, bool(extra)),
        grid_spec=pltpu.PrefetchScalarGridSpec(
            num_scalar_prefetch=1,
            grid=(arcs // group,),
            in_specs=[anywhere] * (plan.rings * plan.plane)
            + [
                pl.BlockSpec((group, arc_rows, width), lambda i, t: (i, 0, 0)),
                pl.BlockSpec((group, arc_rows, arc_rows), lambda i, t: (i, 0, 0)),
            ]
            + ([wide, pl.BlockSpec(extra[1].shape, lambda i, t: (0, 0))] if extra else []),
            out_specs=[anywhere] * (plan.rings * plan.plane) + ([] if extra else [wide]),
            scratch_shapes=[
                pltpu.VMEM((total,) + block, jnp.bfloat16),
                pltpu.VMEM((total,) + block, jnp.bfloat16),
                pltpu.VMEM((group, width, block[1]), jnp.bfloat16),
                pltpu.SemaphoreType.DMA((plan.rings * plan.plane,)),
            ],
        ),
        out_shape=[jax.ShapeDtypeStruct((plan.cap,) + block, jnp.bfloat16)]
        * (plan.rings * plan.plane)
        + ([] if extra else [jax.ShapeDtypeStruct((arcs, arc_rows, block[1]), jnp.float32)]),
        name="arcs",
    )(tab, *arrived, coupling_panel, inv_factor, *extra)


def add_up(plan, step, me_ref, held_ref, got_refs, part_refs, acc):
    here = lax.rem(me_ref[0], plan.plane)
    start = jnp.zeros(acc.shape, jnp.float32)
    for part_ref in part_refs:
        start = start + part_ref[...].astype(jnp.float32)
    acc[...] = start
    for offset, got_ref in enumerate(got_refs):
        q = plan.source_traced(here, offset)
        for r in range(plan.cap):
            held = held_ref[step, r * plan.plane + q]

            @pl.when(held > 0)
            def _():
                acc[held - 1] += got_ref[r].astype(jnp.float32)


def fold_kernel(plan, step, me_ref, held_ref, *refs):
    got_refs, part_refs = refs[: plan.plane], refs[plan.plane : -2]
    out_ref, acc = refs[-2], refs[-1]
    add_up(plan, step, me_ref, held_ref, got_refs, part_refs, acc)
    out_ref[...] = acc[...].astype(out_ref.dtype)


def image_kernel(plan, both, me_ref, held_ref, field_ref, prior_ref, *refs):
    outputs = 4 if both else 3
    got_refs, part_refs = refs[: plan.plane], refs[plan.plane : -outputs]
    image_ref, gram_ref, acc = refs[-outputs], refs[1 - outputs], refs[-1]
    add_up(plan, 0, me_ref, held_ref, got_refs, part_refs, acc)
    rows = acc.shape[1]
    for b in range(plan.blocks):
        image = acc[b].T + prior_ref[:, b : b + 1] * field_ref[b]
        image_ref[b] = image
        if both:
            refs[-2][b] = (field_ref[b] - BLEND * image).astype(jnp.bfloat16)
    gram_ref[...] = jnp.zeros_like(gram_ref)
    batch = max(n for n in range(1, 6) if plan.blocks % n == 0)

    @pl.loop(0, plan.blocks, step=batch)
    def _(b):
        field = field_ref[pl.ds(b, batch)].reshape(batch * rows, -1)
        image = image_ref[pl.ds(b, batch)].reshape(batch * rows, -1)
        gram_ref[0] += gram_of(field, image)
        if both:
            gram_ref[1] += gram_of(image, image)


def gram_of(left, right):
    return lax.dot_general(
        left,
        right,
        (((0,), (0,)), ((), ())),
        precision=lax.Precision.HIGHEST,
        preferred_element_type=jnp.float32,
    )


def fold_specs(args):
    return [pl.BlockSpec(memory_space=SMEM)] * 2 + [pl.BlockSpec(memory_space=VMEM)] * (
        len(args) - 2
    )


def fold(plan, step, me, held, got, parts):
    shape = (plan.blocks,) + got[0].shape[1:]
    args = (me, held, *in_vmem(*got, *parts))
    return pl.pallas_call(
        functools.partial(fold_kernel, plan, step),
        out_shape=pltpu.VMEM(shape, jnp.bfloat16),
        in_specs=fold_specs(args),
        out_specs=pl.BlockSpec(memory_space=VMEM),
        scratch_shapes=[pltpu.VMEM(shape, jnp.float32)],
        compiler_params=SMALL,
        name="fold",
    )(*args)


def fold_image(plan, me, held, got, parts, field, prior_cols, both):
    shape, cols = field.shape, field.shape[2]
    args = (me, held, field, prior_cols, *in_vmem(*got, *parts))
    return pl.pallas_call(
        functools.partial(image_kernel, plan, both),
        out_shape=[
            jax.ShapeDtypeStruct(shape, jnp.float32),
            jax.ShapeDtypeStruct((2 if both else 1, cols, cols), jnp.float32),
        ]
        + ([pltpu.VMEM(shape, jnp.bfloat16)] if both else []),
        in_specs=fold_specs(args),
        out_specs=[pl.BlockSpec(memory_space=VMEM)] * (3 if both else 2),
        scratch_shapes=[pltpu.VMEM(shape, jnp.float32)],
        compiler_params=SMALL,
        name="image",
    )(*args)


def update_kernel(field_ref, image_ref, sol_ref, res_ref, step_ref, sol_out, res_out):
    blocks, rows, cols = field_ref.shape
    step = step_ref[...]
    size = (blocks * rows, cols)
    moved = times_high(field_ref[...].reshape(size), step).reshape(field_ref.shape)
    sol_out[...] = sol_ref[...] + moved
    moved = times_high(image_ref[...].reshape(size), step).reshape(field_ref.shape)
    res_out[...] = res_ref[...] - moved


def update(field, image, solution_field, residual, step_mat):
    blocks, rows, cols = field.shape
    batch = max(n for n in range(1, 5) if blocks % n == 0)
    spec = pl.BlockSpec((batch, rows, cols), lambda i: (i, 0, 0))
    return pl.pallas_call(
        update_kernel,
        grid=(blocks // batch,),
        out_shape=[jax.ShapeDtypeStruct(field.shape, jnp.float32)] * 2,
        in_specs=[spec] * 4 + [pl.BlockSpec((cols, cols), lambda i: (0, 0))],
        out_specs=[spec] * 2,
        name="update",
    )(field, image, solution_field, residual, step_mat)


def identity(size):
    rows = lax.broadcasted_iota(jnp.int32, (size, size), 0)
    lanes = lax.broadcasted_iota(jnp.int32, (size, size), 1)
    return jnp.where(rows == lanes, 1.0, 0.0)


def eliminate(matrix):
    size = matrix.shape[0]
    rows = lax.broadcasted_iota(jnp.int32, (size, size), 0)
    lanes = lax.broadcasted_iota(jnp.int32, (size, size), 1)

    def pivot(k, matrix):
        on_row, on_lane = rows == k, lanes == k
        column = jnp.sum(jnp.where(on_lane, matrix, 0.0), axis=1, keepdims=True)
        row = jnp.sum(jnp.where(on_row, matrix, 0.0), axis=0, keepdims=True)
        scale = 1.0 / jnp.sum(jnp.where(on_lane[:1], row, 0.0), axis=1, keepdims=True)
        row = jnp.where(on_lane[:1], 1.0, row) * scale
        rest = jnp.where(on_lane, 0.0, matrix) - column * row
        return jnp.where(on_row, row, rest)

    return lax.fori_loop(0, size, pivot, matrix)


def invert_into(out_refs, matrices):
    size = matrices[0].shape[0]
    eye = identity(size)
    scales, scaled = [], []
    for matrix in matrices:
        diagonal = eye * matrix
        down = lax.rsqrt(jnp.sum(diagonal, axis=1, keepdims=True))
        along = lax.rsqrt(jnp.sum(diagonal, axis=0, keepdims=True))
        scales.append((down, along))
        scaled.append(matrix * down * along)
    off = [matrix - eye for matrix in scaled]
    second = [times_high(e, e) for e in off]
    fourth = [times_high(e, e) for e in second]
    third = [times_high(e, f) for e, f in zip(off, second)]
    guess = [eye - e + f - g for e, f, g in zip(off, second, third)]
    guess = [x + times_high(x, e) for x, e in zip(guess, fourth)]
    left = [eye - times_high(a, x) for a, x in zip(scaled, guess)]
    guess = [x + times_high(x, r) for x, r in zip(guess, left)]
    for out_ref, x, r, a, (down, along) in zip(out_refs, guess, left, scaled, scales):
        out_ref[...] = x * down * along
        worst = jnp.max(jnp.sum(jnp.abs(r), axis=1, keepdims=True))

        @pl.when(jnp.logical_not(worst < 1e-3))
        def _():
            y = eliminate(a)
            y = y + times_high(y, eye - times_high(a, y))
            out_ref[...] = y * down * along


def step_kernel(
    grams_ref, res_ref, step_ref, beta_ref, new_ref, mix_ref, first_inv, second_inv
):
    res, cross, image = res_ref[...], grams_ref[0], grams_ref[1]
    invert_into([first_inv, second_inv], [0.5 * (cross + cross.T), 0.5 * (res + res.T)])
    step = times_high(first_inv[...], res)
    step_ref[...] = step
    moved = times_high(cross, step)
    new = res - moved.T - moved + times_high(step.T, times_high(image, step))
    new_ref[...] = new
    beta = times_high(second_inv[...], new)
    beta_ref[...] = beta
    size = beta.shape[0]
    mix_ref[size:, :] = step * (1.0 / BLEND)
    mix_ref[:size, :] = identity(size) + beta - step * (1.0 / BLEND)


def last_kernel(grams_ref, res_ref, step_ref, first_inv):
    curv = grams_ref[0]
    invert_into([first_inv], [0.5 * (curv + curv.T)])
    step_ref[...] = times_high(first_inv[...], res_ref[...])


def small_solve(kernel, args, outputs, scratch, tall=0):
    shape = args[0].shape[1:]
    double = (2 * shape[0], shape[1])
    return pl.pallas_call(
        kernel,
        out_shape=[jax.ShapeDtypeStruct(shape, jnp.float32)] * outputs
        + [jax.ShapeDtypeStruct(double, jnp.float32)] * tall,
        scratch_shapes=[pltpu.VMEM(shape, jnp.float32)] * scratch,
        compiler_params=SMALL,
        name="solve",
    )(*args)


def trade_plane(plan, buffers):
    moved = [None] * plan.plane
    moved[0] = buffers[0]
    for offset in range(plan.plane - 1, 0, -1):
        moved[offset] = lax.ppermute(buffers[offset], AXES, plan.shift_plane(offset))
    return moved


def gate_kernel(in_ref, out_ref):
    out_ref[0] = in_ref[0]


def gate(me):
    return pl.pallas_call(
        gate_kernel,
        out_shape=jax.ShapeDtypeStruct(me.shape, me.dtype),
        in_specs=[pl.BlockSpec(memory_space=SMEM)],
        out_specs=pl.BlockSpec(memory_space=SMEM),
        compiler_params=SMALL,
        name="gate",
    )(me)


def apply_schur(
    plan, me, tab, held, chunk, field, prior_cols, coupling_panel, inv_factor, extra=()
):
    arrived, both = [], not extra
    for s in range(plan.rings):
        following = None
        if s + 1 < plan.rings:
            following = lax.ppermute(chunk, AXES, plan.ring)
        chosen = pick(plan, s, me, held, chunk)
        arrived += trade_plane(plan, chosen)
        if s + 1 < plan.rings:
            me = gate(me)
        chunk = following
    leaving = run_arcs(plan, tab, arrived, coupling_panel, inv_factor, extra)
    moved, folded = {}, []
    for j, s in enumerate(plan.back):
        buffers = leaving[s * plan.plane : (s + 1) * plan.plane]
        if j >= 2:
            *buffers, _ = lax.optimization_barrier((*buffers, folded[j - 2]))
        got = trade_plane(plan, buffers)
        sources = [moved[source] for source in plan.follows(s)]
        if s:
            me = gate(me)
        if s == 0:
            made = fold_image(plan, me, held, got, sources, field, prior_cols, both)
            return (*made, leaving[-1], me)
        folded.append(fold(plan, s, me, held, got, sources))
        moved[s] = lax.ppermute(folded[j], AXES, plan.shift_back(s))


def per_device(
    mesh, right_side, prior_diag, inv_factor, coupling_panel, coupling_owner, coupling_block
):
    plan = Plan(mesh, coupling_panel.shape[0], coupling_owner.shape[1], right_side.shape[0])
    me = lax.axis_index(AXES).astype(jnp.int32).reshape(1)
    tab, held = make_tables(plan, me, coupling_owner, coupling_block)
    prior_cols = prior_diag.T
    common = (prior_cols, coupling_panel, inv_factor)
    rounded = right_side.astype(jnp.bfloat16)
    res_gram = sum_all(inner_gram(right_side, right_side)[None])[0]
    image_vec, grams, blend, coupled, me = apply_schur(
        plan, me, tab, held, rounded, right_side, *common
    )
    grams, res_gram = lax.optimization_barrier((grams, res_gram))
    grams = sum_all(grams)
    step_mat, beta_mat, res_gram, mix = small_solve(
        step_kernel, (grams, res_gram), 3, 2, 1
    )
    solution_field = combine_cols(right_side, step_mat)
    residual = right_side - combine_cols(image_vec, step_mat)
    direction = residual + combine_cols(right_side, beta_mat)
    image_vec, grams, _, _ = apply_schur(
        plan, me, tab, held, blend, direction, *common, extra=(coupled, mix)
    )
    (step_mat,) = small_solve(last_kernel, (sum_all(grams), res_gram), 1, 1)
    return tuple(update(direction, image_vec, solution_field, residual, step_mat))


def solution(mesh):
    in_specs = (
        P(AXES, None, None),
        P(AXES, None),
        P(AXES, None, None),
        P(AXES, None, None),
        P(),
        P(),
    )
    out_specs = (P(AXES, None, None), P(AXES, None, None))
    return jax.shard_map(
        functools.partial(per_device, mesh),
        mesh=mesh,
        in_specs=in_specs,
        out_specs=out_specs,
        check_vma=False,
    )
```

```python
import functools

import jax
import jax.numpy as jnp
from jax import lax
from jax.experimental import pallas as pl
from jax.experimental.pallas import tpu as pltpu
from jax.sharding import PartitionSpec as P


BLEND = 0.5
GROUP = 4
AXES = ("arc", "vec")
SMEM = pltpu.MemorySpace.SMEM
VMEM = pltpu.MemorySpace.VMEM


SMALL = pltpu.CompilerParams(vmem_limit_bytes=16 << 20)


def in_vmem(*arrays):
    placed = [pltpu.with_memory_space_constraint(array, pltpu.VMEM) for array in arrays]
    return placed


def inner_gram(left, right):
    return jnp.einsum("grc,grd->cd", left, right, precision=lax.Precision.HIGHEST)


def combine_cols(field, weights):
    return jnp.einsum("grc,cd->grd", field, weights, precision=lax.Precision.HIGHEST)


def times_high(left, right):
    return jnp.dot(left, right, precision=lax.Precision.HIGHEST)


def trade(buffer):
    return lax.all_to_all(buffer, AXES, split_axis=0, concat_axis=0, tiled=True)


def sum_all(grams):
    device_count = lax.axis_size(AXES)
    count, rows, cols = grams.shape
    pieces = grams.reshape(device_count, count * rows // device_count, cols)
    pieces = trade(pieces)
    shared = jnp.broadcast_to(jnp.sum(pieces, axis=0)[None], pieces.shape)
    return trade(shared).reshape(grams.shape)


class Plan:
    def __init__(self, mesh, arcs_here, links, blocks_here):
        arc, vec = mesh.shape["arc"], mesh.shape["vec"]
        half = max(1, vec // 2)
        self.rings = arc // half if arc % half == 0 else arc
        self.devices = arc * vec
        self.plane = self.devices // self.rings
        self.arcs, self.links, self.blocks = arcs_here, links, blocks_here
        entries = arcs_here * links
        self.cap = (entries + self.devices - 1) // self.devices + 1
        self.slots = self.plane * self.cap
        self.own_row = arcs_here
        self.padded = -(-self.slots // 128) * 128
        self.order = [self.plane_at(i) for i in range(self.rings)]
        self.ring = [
            (self.order[i] * self.plane + p, self.order[(i + 1) % self.rings] * self.plane + p)
            for i in range(self.rings)
            for p in range(self.plane)
        ]
        self.paired = self.plane & (self.plane - 1) == 0
        half = self.rings // 2
        onward, reverse = list(range(half, 0, -1)), list(range(half + 1, self.rings))
        self.back = []
        while onward or reverse:
            self.back += onward[:1] + reverse[:1]
            onward, reverse = onward[1:], reverse[1:]
        self.back.append(0)

    def follows(self, step):
        half = self.rings // 2
        sources = [step + 1] if step < half else []
        if step > half + 1 or (step == 0 and self.rings > half + 1):
            sources.append((step - 1) % self.rings)
        return sources

    def shift_back(self, step):
        move = 1 if step <= self.rings // 2 else -1
        return [
            (self.order[i] * self.plane + p, self.order[(i - move) % self.rings] * self.plane + p)
            for i in range(self.rings)
            for p in range(self.plane)
        ]

    def target(self, p, offset):
        return p ^ offset if self.paired else (p + offset) % self.plane

    def target_traced(self, p, offset):
        return p ^ offset if self.paired else lax.rem(p + offset, self.plane)

    def source_traced(self, p, offset):
        return p ^ offset if self.paired else lax.rem(p - offset + self.plane, self.plane)

    def shift_plane(self, offset):
        return [
            (z * self.plane + p, z * self.plane + self.target(p, offset))
            for z in range(self.rings)
            for p in range(self.plane)
        ]

    def plane_at(self, place):
        return 2 * place if 2 * place < self.rings else 2 * self.rings - 1 - 2 * place

    def place_of(self, z):
        half = lax.div(z, 2)
        return jnp.where(lax.rem(z, 2) == 0, half, self.rings - 1 - half)

    def source_plane(self, me, step):
        place = self.place_of(lax.div(me, self.plane))
        place = lax.rem(place - step + self.rings, self.rings)
        doubled = 2 * place
        return jnp.where(doubled < self.rings, doubled, 2 * self.rings - 1 - doubled)


def tables_kernel(
    plan, me_ref, owner_cols, block_cols, tab_ref, held_ref, owner_ref, block_ref, all_ref
):
    me = me_ref[0]
    arcs, links, lanes = plan.arcs, plan.links, tab_ref.shape[1]
    z = lax.div(me, plan.plane)
    span = plan.plane * arcs
    first = pl.multiple_of(z * span, span)
    owner_ref[...] = owner_cols[:, pl.ds(first, span)].T
    block_ref[...] = block_cols[:, pl.ds(first, span)].T
    owners = lax.broadcasted_iota(jnp.int32, (arcs, lanes), 1)
    low = lax.broadcasted_iota(jnp.int32, (arcs, arcs), 0)
    high = lax.broadcasted_iota(jnp.int32, (arcs, arcs), 1)
    before = (high < low).astype(jnp.float32)

    def incidence(row):
        owner = owner_ref[pl.ds(row, arcs), :]
        block = block_ref[pl.ds(row, arcs), :]
        named = jnp.zeros((arcs, lanes), jnp.float32)
        held = jnp.zeros((arcs, lanes), jnp.int32)
        for k in range(links):
            same = owner[:, k : k + 1] == owners
            named = jnp.where(same, 1.0, named)
            held = jnp.where(same, block[:, k : k + 1] + 1, held)
        rank = jnp.dot(before, named, preferred_element_type=jnp.float32).astype(jnp.int32)
        return held, rank

    all_ref[...] = jnp.zeros_like(all_ref)
    for q in range(plan.plane):
        held, rank = incidence(q * arcs)
        for r in range(plan.cap):
            at_rank = jnp.where(rank == r, held, 0)
            all_ref[r * plan.plane + q : r * plan.plane + q + 1, :] = jnp.sum(
                at_rank, axis=0, keepdims=True
            )
    columns = jnp.zeros((held_ref.shape[1], 128), jnp.int32)
    wide = lax.broadcasted_iota(jnp.int32, columns.shape, 1)
    across = lax.broadcasted_iota(jnp.int32, all_ref.shape, 1)
    for s in range(plan.rings):
        column = plan.source_plane(me, s) * plan.plane + lax.rem(me, plan.plane)
        picked = jnp.sum(jnp.where(across == column, all_ref[...], 0), axis=1, keepdims=True)
        columns = jnp.where(wide == s, picked, columns)
    held_ref[...] = columns.T[: held_ref.shape[0]]
    row = pl.multiple_of(lax.rem(me, plan.plane) * arcs, arcs)
    held, rank = incidence(row)
    place = plan.place_of(z)
    other = plan.place_of(lax.div(owners, plan.plane))
    step = lax.rem(place - other + plan.rings, plan.rings)
    here, there = lax.rem(me, plan.plane), lax.rem(owners, plan.plane)
    offset = here ^ there if plan.paired else lax.rem(here - there + plan.plane, plan.plane)
    slot = step * plan.slots + offset * plan.cap + rank
    tab_ref[:arcs, :] = slot
    mine = jnp.zeros((arcs, lanes), jnp.int32)
    owner = owner_ref[pl.ds(row, arcs), :]
    for k in range(links):
        mine = jnp.where(owners == k, owner[:, k : k + 1], mine)
    tab_ref[plan.own_row : plan.own_row + arcs, :] = mine


def make_tables(plan, me, coupling_owner, coupling_block):
    lanes = -(-plan.devices // 128) * 128
    return pl.pallas_call(
        functools.partial(tables_kernel, plan),
        out_shape=[
            jax.ShapeDtypeStruct((2 * plan.arcs, lanes), jnp.int32),
            jax.ShapeDtypeStruct((-(-plan.rings // 8) * 8, plan.padded), jnp.int32),
        ],
        in_specs=[
            pl.BlockSpec(memory_space=SMEM),
            pl.BlockSpec(memory_space=VMEM),
            pl.BlockSpec(memory_space=VMEM),
        ],
        out_specs=[pl.BlockSpec(memory_space=VMEM)] * 2,
        scratch_shapes=[pltpu.VMEM((plan.plane * plan.arcs, plan.links), jnp.int32)] * 2
        + [pltpu.VMEM((plan.padded, lanes), jnp.int32)],
        compiler_params=SMALL,
        name="tables",
    )(me, coupling_owner.T, coupling_block.T)


def pick_kernel(plan, step, me_ref, held_ref, chunk_ref, *out_refs):
    here = lax.rem(me_ref[0], plan.plane)
    for offset, out_ref in enumerate(out_refs):
        q = plan.target_traced(here, offset)
        for r in range(plan.cap):
            block = jnp.maximum(held_ref[step, r * plan.plane + q] - 1, 0)
            out_ref[r] = chunk_ref[block]


def pick(plan, step, me, held, chunk):
    shape = (plan.cap,) + chunk.shape[1:]
    return pl.pallas_call(
        functools.partial(pick_kernel, plan, step),
        out_shape=[jax.ShapeDtypeStruct(shape, chunk.dtype)]
        + [pltpu.VMEM(shape, chunk.dtype)] * (plan.plane - 1),
        in_specs=[
            pl.BlockSpec(memory_space=SMEM),
            pl.BlockSpec(memory_space=SMEM),
            pl.BlockSpec(memory_space=VMEM),
        ],
        out_specs=[pl.BlockSpec(memory_space=VMEM)] * plan.plane,
        compiler_params=SMALL,
        name="pick",
    )(me, held, *in_vmem(chunk))


def narrow_dot(left, right, contract=1):
    product = lax.dot_general(
        left, right, (((contract,), (0,)), ((), ())), preferred_element_type=jnp.float32
    )
    return product.astype(jnp.bfloat16)


def mix_in(earlier, fresh, mix):
    def halves(wide):
        high = wide.astype(jnp.bfloat16)
        return high, (wide - high.astype(jnp.float32)).astype(jnp.bfloat16)

    def product(left, right):
        return jnp.dot(left, right, preferred_element_type=jnp.float32)

    high, low = halves(jnp.concatenate([earlier, fresh], axis=1))
    mix_high, mix_low = halves(mix)
    return product(high, mix_high) + (product(high, mix_low) + product(low, mix_high))


def arcs_kernel(plan, mixed, tab_ref, *refs):
    count, cap = plan.rings * plan.plane, plan.cap
    arrived_refs = refs[:count]
    panel_ref, factor_ref = refs[count], refs[count + 1]
    extra = refs[count + 2 : -4 - count] if mixed else ()
    out_refs = refs[-4 - count : -4] if mixed else refs[count + 2 : -5]
    arrived, leaving, fetched, sems = refs[-4:]
    arc = pl.program_id(0)
    rows = arrived.shape[1]

    def inward(s):
        return pltpu.make_async_copy(
            arrived_refs[s], arrived.at[pl.ds(s * cap, cap)], sems.at[s]
        )

    def outward(s):
        return pltpu.make_async_copy(
            leaving.at[pl.ds(s * cap, cap)], out_refs[s], sems.at[s]
        )

    @pl.when(arc == 0)
    def _():
        for s in range(count):
            inward(s).start()
        for s in range(count):
            inward(s).wait()

    group = range(panel_ref.shape[0])
    spots = [[] for _ in group]
    for g in group:
        row = arc * len(group) + g
        for k in range(plan.links):
            spot = tab_ref[row, tab_ref[plan.own_row + row, k]]
            spots[g].append(spot)
            fetched[g, k * rows : (k + 1) * rows, :] = arrived[spot]
    coupled = []
    for g in group:
        wide = jnp.dot(panel_ref[g], fetched[g], preferred_element_type=jnp.float32)
        if mixed:
            wide = mix_in(extra[0][g], wide, extra[1][...])
        else:
            refs[-5][g] = wide
        coupled.append(wide.astype(jnp.bfloat16))
    whitened = [narrow_dot(factor_ref[g], coupled[g]) for g in group]
    smoothed = [narrow_dot(whitened[g], factor_ref[g], 0) for g in group]
    for g in group:
        projected = narrow_dot(smoothed[g], panel_ref[g])
        for k in range(plan.links):
            leaving[spots[g][k]] = projected[:, k * rows : (k + 1) * rows]

    @pl.when(arc == pl.num_programs(0) - 1)
    def _():
        for s in range(count):
            outward(s).start()
        for s in range(count):
            outward(s).wait()


def run_arcs(plan, tab, arrived, coupling_panel, inv_factor, extra):
    arcs, arc_rows, width = coupling_panel.shape
    block = arrived[0].shape[1:]
    total = plan.rings * plan.slots
    group = GROUP if arcs % GROUP == 0 else 1
    anywhere = pl.BlockSpec(memory_space=pl.ANY)
    wide = pl.BlockSpec((group, arc_rows, block[1]), lambda i, t: (i, 0, 0))
    return pl.pallas_call(
        functools.partial(arcs_kernel, plan, bool(extra)),
        grid_spec=pltpu.PrefetchScalarGridSpec(
            num_scalar_prefetch=1,
            grid=(arcs // group,),
            in_specs=[anywhere] * (plan.rings * plan.plane)
            + [
                pl.BlockSpec((group, arc_rows, width), lambda i, t: (i, 0, 0)),
                pl.BlockSpec((group, arc_rows, arc_rows), lambda i, t: (i, 0, 0)),
            ]
            + ([wide, pl.BlockSpec(extra[1].shape, lambda i, t: (0, 0))] if extra else []),
            out_specs=[anywhere] * (plan.rings * plan.plane) + ([] if extra else [wide]),
            scratch_shapes=[
                pltpu.VMEM((total,) + block, jnp.bfloat16),
                pltpu.VMEM((total,) + block, jnp.bfloat16),
                pltpu.VMEM((group, width, block[1]), jnp.bfloat16),
                pltpu.SemaphoreType.DMA((plan.rings * plan.plane,)),
            ],
        ),
        out_shape=[jax.ShapeDtypeStruct((plan.cap,) + block, jnp.bfloat16)]
        * (plan.rings * plan.plane)
        + ([] if extra else [jax.ShapeDtypeStruct((arcs, arc_rows, block[1]), jnp.float32)]),
        name="arcs",
    )(tab, *arrived, coupling_panel, inv_factor, *extra)


def add_up(plan, step, me_ref, held_ref, got_refs, part_refs, acc):
    here = lax.rem(me_ref[0], plan.plane)
    start = jnp.zeros(acc.shape, jnp.float32)
    for part_ref in part_refs:
        start = start + part_ref[...].astype(jnp.float32)
    acc[...] = start
    for offset, got_ref in enumerate(got_refs):
        q = plan.source_traced(here, offset)
        for r in range(plan.cap):
            held = held_ref[step, r * plan.plane + q]

            @pl.when(held > 0)
            def _():
                acc[held - 1] += got_ref[r].astype(jnp.float32)


def fold_kernel(plan, step, me_ref, held_ref, *refs):
    got_refs, part_refs = refs[: plan.plane], refs[plan.plane : -2]
    out_ref, acc = refs[-2], refs[-1]
    add_up(plan, step, me_ref, held_ref, got_refs, part_refs, acc)
    out_ref[...] = acc[...].astype(out_ref.dtype)


def image_kernel(plan, both, me_ref, held_ref, field_ref, prior_ref, *refs):
    outputs = 4 if both else 3
    got_refs, part_refs = refs[: plan.plane], refs[plan.plane : -outputs]
    image_ref, gram_ref, acc = refs[-outputs], refs[1 - outputs], refs[-1]
    add_up(plan, 0, me_ref, held_ref, got_refs, part_refs, acc)
    rows = acc.shape[1]
    for b in range(plan.blocks):
        image = acc[b].T + prior_ref[:, b : b + 1] * field_ref[b]
        image_ref[b] = image
        if both:
            refs[-2][b] = (field_ref[b] - BLEND * image).astype(jnp.bfloat16)
    gram_ref[...] = jnp.zeros_like(gram_ref)
    batch = max(n for n in range(1, 6) if plan.blocks % n == 0)

    @pl.loop(0, plan.blocks, step=batch)
    def _(b):
        field = field_ref[pl.ds(b, batch)].reshape(batch * rows, -1)
        image = image_ref[pl.ds(b, batch)].reshape(batch * rows, -1)
        gram_ref[0] += gram_of(field, image)
        if both:
            gram_ref[1] += gram_of(image, image)


def gram_of(left, right):
    return lax.dot_general(
        left,
        right,
        (((0,), (0,)), ((), ())),
        precision=lax.Precision.HIGHEST,
        preferred_element_type=jnp.float32,
    )


def fold_specs(args):
    return [pl.BlockSpec(memory_space=SMEM)] * 2 + [pl.BlockSpec(memory_space=VMEM)] * (
        len(args) - 2
    )


def fold(plan, step, me, held, got, parts):
    shape = (plan.blocks,) + got[0].shape[1:]
    args = (me, held, got[0], *in_vmem(*got[1:], *parts))
    return pl.pallas_call(
        functools.partial(fold_kernel, plan, step),
        out_shape=pltpu.VMEM(shape, jnp.bfloat16),
        in_specs=fold_specs(args),
        out_specs=pl.BlockSpec(memory_space=VMEM),
        scratch_shapes=[pltpu.VMEM(shape, jnp.float32)],
        compiler_params=SMALL,
        name="fold",
    )(*args)


def fold_image(plan, me, held, got, parts, field, prior_cols, both):
    shape, cols = field.shape, field.shape[2]
    args = (me, held, field, prior_cols, got[0], *in_vmem(*got[1:], *parts))
    return pl.pallas_call(
        functools.partial(image_kernel, plan, both),
        out_shape=[
            jax.ShapeDtypeStruct(shape, jnp.float32),
            jax.ShapeDtypeStruct((2 if both else 1, cols, cols), jnp.float32),
        ]
        + ([pltpu.VMEM(shape, jnp.bfloat16)] if both else []),
        in_specs=fold_specs(args),
        out_specs=[pl.BlockSpec(memory_space=VMEM)] * (3 if both else 2),
        scratch_shapes=[pltpu.VMEM(shape, jnp.float32)],
        compiler_params=SMALL,
        name="image",
    )(*args)


def update_kernel(field_ref, image_ref, sol_ref, res_ref, step_ref, sol_out, res_out):
    blocks, rows, cols = field_ref.shape
    step = step_ref[...]
    size = (blocks * rows, cols)
    moved = times_high(field_ref[...].reshape(size), step).reshape(field_ref.shape)
    sol_out[...] = sol_ref[...] + moved
    moved = times_high(image_ref[...].reshape(size), step).reshape(field_ref.shape)
    res_out[...] = res_ref[...] - moved


def update(field, image, solution_field, residual, step_mat):
    blocks, rows, cols = field.shape
    batch = max(n for n in range(1, 5) if blocks % n == 0)
    spec = pl.BlockSpec((batch, rows, cols), lambda i: (i, 0, 0))
    return pl.pallas_call(
        update_kernel,
        grid=(blocks // batch,),
        out_shape=[jax.ShapeDtypeStruct(field.shape, jnp.float32)] * 2,
        in_specs=[spec] * 4 + [pl.BlockSpec((cols, cols), lambda i: (0, 0))],
        out_specs=[spec] * 2,
        name="update",
    )(field, image, solution_field, residual, step_mat)


def identity(size):
    rows = lax.broadcasted_iota(jnp.int32, (size, size), 0)
    lanes = lax.broadcasted_iota(jnp.int32, (size, size), 1)
    return jnp.where(rows == lanes, 1.0, 0.0)


def eliminate(matrix):
    size = matrix.shape[0]
    rows = lax.broadcasted_iota(jnp.int32, (size, size), 0)
    lanes = lax.broadcasted_iota(jnp.int32, (size, size), 1)

    def pivot(k, matrix):
        on_row, on_lane = rows == k, lanes == k
        column = jnp.sum(jnp.where(on_lane, matrix, 0.0), axis=1, keepdims=True)
        row = jnp.sum(jnp.where(on_row, matrix, 0.0), axis=0, keepdims=True)
        scale = 1.0 / jnp.sum(jnp.where(on_lane[:1], row, 0.0), axis=1, keepdims=True)
        row = jnp.where(on_lane[:1], 1.0, row) * scale
        rest = jnp.where(on_lane, 0.0, matrix) - column * row
        return jnp.where(on_row, row, rest)

    return lax.fori_loop(0, size, pivot, matrix)


def invert_into(out_refs, matrices):
    size = matrices[0].shape[0]
    eye = identity(size)
    scales, scaled = [], []
    for matrix in matrices:
        diagonal = eye * matrix
        down = lax.rsqrt(jnp.sum(diagonal, axis=1, keepdims=True))
        along = lax.rsqrt(jnp.sum(diagonal, axis=0, keepdims=True))
        scales.append((down, along))
        scaled.append(matrix * down * along)
    off = [matrix - eye for matrix in scaled]
    second = [times_high(e, e) for e in off]
    fourth = [times_high(e, e) for e in second]
    third = [times_high(e, f) for e, f in zip(off, second)]
    guess = [eye - e + f - g for e, f, g in zip(off, second, third)]
    guess = [x + times_high(x, e) for x, e in zip(guess, fourth)]
    left = [eye - times_high(a, x) for a, x in zip(scaled, guess)]
    guess = [x + times_high(x, r) for x, r in zip(guess, left)]
    for out_ref, x, r, a, (down, along) in zip(out_refs, guess, left, scaled, scales):
        out_ref[...] = x * down * along
        worst = jnp.max(jnp.sum(jnp.abs(r), axis=1, keepdims=True))

        @pl.when(jnp.logical_not(worst < 1e-3))
        def _():
            y = eliminate(a)
            y = y + times_high(y, eye - times_high(a, y))
            out_ref[...] = y * down * along


def step_kernel(
    grams_ref, res_ref, step_ref, beta_ref, new_ref, mix_ref, first_inv, second_inv
):
    res, cross, image = res_ref[...], grams_ref[0], grams_ref[1]
    invert_into([first_inv, second_inv], [0.5 * (cross + cross.T), 0.5 * (res + res.T)])
    step = times_high(first_inv[...], res)
    step_ref[...] = step
    moved = times_high(cross, step)
    new = res - moved.T - moved + times_high(step.T, times_high(image, step))
    new_ref[...] = new
    beta = times_high(second_inv[...], new)
    beta_ref[...] = beta
    size = beta.shape[0]
    mix_ref[size:, :] = step * (1.0 / BLEND)
    mix_ref[:size, :] = identity(size) + beta - step * (1.0 / BLEND)


def last_kernel(grams_ref, res_ref, step_ref, first_inv):
    curv = grams_ref[0]
    invert_into([first_inv], [0.5 * (curv + curv.T)])
    step_ref[...] = times_high(first_inv[...], res_ref[...])


def small_solve(kernel, args, outputs, scratch, tall=0):
    shape = args[0].shape[1:]
    double = (2 * shape[0], shape[1])
    return pl.pallas_call(
        kernel,
        out_shape=[jax.ShapeDtypeStruct(shape, jnp.float32)] * outputs
        + [jax.ShapeDtypeStruct(double, jnp.float32)] * tall,
        scratch_shapes=[pltpu.VMEM(shape, jnp.float32)] * scratch,
        compiler_params=SMALL,
        name="solve",
    )(*args)


def trade_plane(plan, buffers):
    moved = [None] * plan.plane
    moved[0] = buffers[0]
    for offset in range(plan.plane - 1, 0, -1):
        moved[offset] = lax.ppermute(buffers[offset], AXES, plan.shift_plane(offset))
    return moved


def gate_kernel(in_ref, out_ref):
    out_ref[0] = in_ref[0]


def gate(me):
    return pl.pallas_call(
        gate_kernel,
        out_shape=jax.ShapeDtypeStruct(me.shape, me.dtype),
        in_specs=[pl.BlockSpec(memory_space=SMEM)],
        out_specs=pl.BlockSpec(memory_space=SMEM),
        compiler_params=SMALL,
        name="gate",
    )(me)


def apply_schur(
    plan, me, tab, held, chunk, field, prior_cols, coupling_panel, inv_factor, extra=()
):
    arrived, both = [], not extra
    for s in range(plan.rings):
        following = None
        if s + 1 < plan.rings:
            following = lax.ppermute(chunk, AXES, plan.ring)
        chosen = pick(plan, s, me, held, chunk)
        arrived += trade_plane(plan, chosen)
        if s + 1 < plan.rings:
            me = gate(me)
        chunk = following
    leaving = run_arcs(plan, tab, arrived, coupling_panel, inv_factor, extra)
    moved, folded = {}, []
    for j, s in enumerate(plan.back):
        buffers = leaving[s * plan.plane : (s + 1) * plan.plane]
        if j >= 2:
            *buffers, _ = lax.optimization_barrier((*buffers, folded[j - 2]))
        got = trade_plane(plan, buffers)
        sources = [moved[source] for source in plan.follows(s)]
        if s:
            me = gate(me)
        if s == 0:
            made = fold_image(plan, me, held, got, sources, field, prior_cols, both)
            return (*made, leaving[-1], me)
        folded.append(fold(plan, s, me, held, got, sources))
        moved[s] = lax.ppermute(folded[j], AXES, plan.shift_back(s))


def per_device(
    mesh, right_side, prior_diag, inv_factor, coupling_panel, coupling_owner, coupling_block
):
    plan = Plan(mesh, coupling_panel.shape[0], coupling_owner.shape[1], right_side.shape[0])
    me = lax.axis_index(AXES).astype(jnp.int32).reshape(1)
    tab, held = make_tables(plan, me, coupling_owner, coupling_block)
    prior_cols = prior_diag.T
    common = (prior_cols, coupling_panel, inv_factor)
    rounded = right_side.astype(jnp.bfloat16)
    res_gram = sum_all(inner_gram(right_side, right_side)[None])[0]
    image_vec, grams, blend, coupled, me = apply_schur(
        plan, me, tab, held, rounded, right_side, *common
    )
    grams, res_gram = lax.optimization_barrier((grams, res_gram))
    grams = sum_all(grams)
    step_mat, beta_mat, res_gram, mix = small_solve(
        step_kernel, (grams, res_gram), 3, 2, 1
    )
    solution_field = combine_cols(right_side, step_mat)
    residual = right_side - combine_cols(image_vec, step_mat)
    direction = residual + combine_cols(right_side, beta_mat)
    image_vec, grams, _, _ = apply_schur(
        plan, me, tab, held, blend, direction, *common, extra=(coupled, mix)
    )
    (step_mat,) = small_solve(last_kernel, (sum_all(grams), res_gram), 1, 1)
    return tuple(update(direction, image_vec, solution_field, residual, step_mat))


def solution(mesh):
    in_specs = (
        P(AXES, None, None),
        P(AXES, None),
        P(AXES, None, None),
        P(AXES, None, None),
        P(),
        P(),
    )
    out_specs = (P(AXES, None, None), P(AXES, None, None))
    return jax.shard_map(
        functools.partial(per_device, mesh),
        mesh=mesh,
        in_specs=in_specs,
        out_specs=out_specs,
        check_vma=False,
    )
```

```python
import functools

import jax
import jax.numpy as jnp
from jax import lax
from jax.experimental import pallas as pl
from jax.experimental.pallas import tpu as pltpu
from jax.sharding import PartitionSpec as P


BLEND = 0.5
GROUP = 4
AXES = ("arc", "vec")
SMEM = pltpu.MemorySpace.SMEM
VMEM = pltpu.MemorySpace.VMEM


SMALL = pltpu.CompilerParams(vmem_limit_bytes=16 << 20)


def in_vmem(*arrays):
    placed = [pltpu.with_memory_space_constraint(array, pltpu.VMEM) for array in arrays]
    return placed


def inner_gram(left, right):
    return jnp.einsum("grc,grd->cd", left, right, precision=lax.Precision.HIGHEST)


def combine_cols(field, weights):
    return jnp.einsum("grc,cd->grd", field, weights, precision=lax.Precision.HIGHEST)


def times_high(left, right):
    return jnp.dot(left, right, precision=lax.Precision.HIGHEST)


def trade(buffer):
    return lax.all_to_all(buffer, AXES, split_axis=0, concat_axis=0, tiled=True)


def sum_all(grams):
    device_count = lax.axis_size(AXES)
    count, rows, cols = grams.shape
    pieces = grams.reshape(device_count, count * rows // device_count, cols)
    pieces = trade(pieces)
    shared = jnp.broadcast_to(jnp.sum(pieces, axis=0)[None], pieces.shape)
    return trade(shared).reshape(grams.shape)


class Plan:
    def __init__(self, mesh, arcs_here, links, blocks_here):
        arc, vec = mesh.shape["arc"], mesh.shape["vec"]
        half = max(1, vec // 2)
        self.rings = arc // half if arc % half == 0 else arc
        self.devices = arc * vec
        self.plane = self.devices // self.rings
        self.arcs, self.links, self.blocks = arcs_here, links, blocks_here
        entries = arcs_here * links
        self.cap = (entries + self.devices - 1) // self.devices + 1
        self.slots = self.plane * self.cap
        self.own_row = arcs_here
        self.padded = -(-self.slots // 128) * 128
        self.order = [self.plane_at(i) for i in range(self.rings)]
        self.ring = [
            (self.order[i] * self.plane + p, self.order[(i + 1) % self.rings] * self.plane + p)
            for i in range(self.rings)
            for p in range(self.plane)
        ]
        self.paired = self.plane & (self.plane - 1) == 0
        half = self.rings // 2
        onward, reverse = list(range(half, 0, -1)), list(range(half + 1, self.rings))
        self.back = []
        while onward or reverse:
            self.back += onward[:1] + reverse[:1]
            onward, reverse = onward[1:], reverse[1:]
        self.back.append(0)

    def follows(self, step):
        half = self.rings // 2
        sources = [step + 1] if step < half else []
        if step > half + 1 or (step == 0 and self.rings > half + 1):
            sources.append((step - 1) % self.rings)
        return sources

    def shift_back(self, step):
        move = 1 if step <= self.rings // 2 else -1
        return [
            (self.order[i] * self.plane + p, self.order[(i - move) % self.rings] * self.plane + p)
            for i in range(self.rings)
            for p in range(self.plane)
        ]

    def target(self, p, offset):
        return p ^ offset if self.paired else (p + offset) % self.plane

    def target_traced(self, p, offset):
        return p ^ offset if self.paired else lax.rem(p + offset, self.plane)

    def source_traced(self, p, offset):
        return p ^ offset if self.paired else lax.rem(p - offset + self.plane, self.plane)

    def shift_plane(self, offset):
        return [
            (z * self.plane + p, z * self.plane + self.target(p, offset))
            for z in range(self.rings)
            for p in range(self.plane)
        ]

    def plane_at(self, place):
        return 2 * place if 2 * place < self.rings else 2 * self.rings - 1 - 2 * place

    def place_of(self, z):
        half = lax.div(z, 2)
        return jnp.where(lax.rem(z, 2) == 0, half, self.rings - 1 - half)

    def source_plane(self, me, step):
        place = self.place_of(lax.div(me, self.plane))
        place = lax.rem(place - step + self.rings, self.rings)
        doubled = 2 * place
        return jnp.where(doubled < self.rings, doubled, 2 * self.rings - 1 - doubled)


def tables_kernel(
    plan, me_ref, owner_cols, block_cols, tab_ref, held_ref, owner_ref, block_ref, all_ref
):
    me = me_ref[0]
    arcs, links, lanes = plan.arcs, plan.links, tab_ref.shape[1]
    z = lax.div(me, plan.plane)
    span = plan.plane * arcs
    first = pl.multiple_of(z * span, span)
    owner_ref[...] = owner_cols[:, pl.ds(first, span)].T
    block_ref[...] = block_cols[:, pl.ds(first, span)].T
    owners = lax.broadcasted_iota(jnp.int32, (arcs, lanes), 1)
    low = lax.broadcasted_iota(jnp.int32, (arcs, arcs), 0)
    high = lax.broadcasted_iota(jnp.int32, (arcs, arcs), 1)
    before = (high < low).astype(jnp.float32)

    def incidence(row):
        owner = owner_ref[pl.ds(row, arcs), :]
        block = block_ref[pl.ds(row, arcs), :]
        named = jnp.zeros((arcs, lanes), jnp.float32)
        held = jnp.zeros((arcs, lanes), jnp.int32)
        for k in range(links):
            same = owner[:, k : k + 1] == owners
            named = jnp.where(same, 1.0, named)
            held = jnp.where(same, block[:, k : k + 1] + 1, held)
        rank = jnp.dot(before, named, preferred_element_type=jnp.float32).astype(jnp.int32)
        return held, rank

    all_ref[...] = jnp.zeros_like(all_ref)
    for q in range(plan.plane):
        held, rank = incidence(q * arcs)
        for r in range(plan.cap):
            at_rank = jnp.where(rank == r, held, 0)
            all_ref[r * plan.plane + q : r * plan.plane + q + 1, :] = jnp.sum(
                at_rank, axis=0, keepdims=True
            )
    columns = jnp.zeros((held_ref.shape[1], 128), jnp.int32)
    wide = lax.broadcasted_iota(jnp.int32, columns.shape, 1)
    across = lax.broadcasted_iota(jnp.int32, all_ref.shape, 1)
    for s in range(plan.rings):
        column = plan.source_plane(me, s) * plan.plane + lax.rem(me, plan.plane)
        picked = jnp.sum(jnp.where(across == column, all_ref[...], 0), axis=1, keepdims=True)
        columns = jnp.where(wide == s, picked, columns)
    held_ref[...] = columns.T[: held_ref.shape[0]]
    row = pl.multiple_of(lax.rem(me, plan.plane) * arcs, arcs)
    held, rank = incidence(row)
    place = plan.place_of(z)
    other = plan.place_of(lax.div(owners, plan.plane))
    step = lax.rem(place - other + plan.rings, plan.rings)
    here, there = lax.rem(me, plan.plane), lax.rem(owners, plan.plane)
    offset = here ^ there if plan.paired else lax.rem(here - there + plan.plane, plan.plane)
    slot = step * plan.slots + offset * plan.cap + rank
    tab_ref[:arcs, :] = slot
    mine = jnp.zeros((arcs, lanes), jnp.int32)
    owner = owner_ref[pl.ds(row, arcs), :]
    for k in range(links):
        mine = jnp.where(owners == k, owner[:, k : k + 1], mine)
    tab_ref[plan.own_row : plan.own_row + arcs, :] = mine


def make_tables(plan, me, coupling_owner, coupling_block):
    lanes = -(-plan.devices // 128) * 128
    return pl.pallas_call(
        functools.partial(tables_kernel, plan),
        out_shape=[
            jax.ShapeDtypeStruct((2 * plan.arcs, lanes), jnp.int32),
            jax.ShapeDtypeStruct((-(-plan.rings // 8) * 8, plan.padded), jnp.int32),
        ],
        in_specs=[
            pl.BlockSpec(memory_space=SMEM),
            pl.BlockSpec(memory_space=VMEM),
            pl.BlockSpec(memory_space=VMEM),
        ],
        out_specs=[pl.BlockSpec(memory_space=VMEM)] * 2,
        scratch_shapes=[pltpu.VMEM((plan.plane * plan.arcs, plan.links), jnp.int32)] * 2
        + [pltpu.VMEM((plan.padded, lanes), jnp.int32)],
        compiler_params=SMALL,
        name="tables",
    )(me, coupling_owner.T, coupling_block.T)


def pick_kernel(plan, step, me_ref, held_ref, chunk_ref, *out_refs):
    here = lax.rem(me_ref[0], plan.plane)
    for offset, out_ref in enumerate(out_refs):
        q = plan.target_traced(here, offset)

        @pl.loop(0, plan.cap)
        def _(r):
            block = jnp.maximum(held_ref[step, r * plan.plane + q] - 1, 0)
            out_ref[r] = chunk_ref[block]


def pick(plan, step, me, held, chunk):
    shape = (plan.cap,) + chunk.shape[1:]
    return pl.pallas_call(
        functools.partial(pick_kernel, plan, step),
        out_shape=[jax.ShapeDtypeStruct(shape, chunk.dtype)]
        + [pltpu.VMEM(shape, chunk.dtype)] * (plan.plane - 1),
        in_specs=[
            pl.BlockSpec(memory_space=SMEM),
            pl.BlockSpec(memory_space=SMEM),
            pl.BlockSpec(memory_space=VMEM),
        ],
        out_specs=[pl.BlockSpec(memory_space=VMEM)] * plan.plane,
        compiler_params=SMALL,
        name="pick",
    )(me, held, *in_vmem(chunk))


def narrow_dot(left, right, contract=1):
    product = lax.dot_general(
        left, right, (((contract,), (0,)), ((), ())), preferred_element_type=jnp.float32
    )
    return product.astype(jnp.bfloat16)


def mix_in(earlier, fresh, mix):
    def halves(wide):
        high = wide.astype(jnp.bfloat16)
        return high, (wide - high.astype(jnp.float32)).astype(jnp.bfloat16)

    def product(left, right):
        return jnp.dot(left, right, preferred_element_type=jnp.float32)

    high, low = halves(jnp.concatenate([earlier, fresh], axis=1))
    mix_high, mix_low = halves(mix)
    return product(high, mix_high) + (product(high, mix_low) + product(low, mix_high))


def arcs_kernel(plan, mixed, tab_ref, *refs):
    count, cap = plan.rings * plan.plane, plan.cap
    arrived_refs = refs[:count]
    panel_ref, factor_ref = refs[count], refs[count + 1]
    extra = refs[count + 2 : -4 - count] if mixed else ()
    out_refs = refs[-4 - count : -4] if mixed else refs[count + 2 : -5]
    arrived, leaving, fetched, sems = refs[-4:]
    arc = pl.program_id(0)
    rows = arrived.shape[1]

    def inward(s):
        return pltpu.make_async_copy(
            arrived_refs[s], arrived.at[pl.ds(s * cap, cap)], sems.at[s]
        )

    def outward(s):
        return pltpu.make_async_copy(
            leaving.at[pl.ds(s * cap, cap)], out_refs[s], sems.at[s]
        )

    @pl.when(arc == 0)
    def _():
        for s in range(count):
            inward(s).start()
        for s in range(count):
            inward(s).wait()

    group = range(panel_ref.shape[0])
    spots = [[] for _ in group]
    for g in group:
        row = arc * len(group) + g
        for k in range(plan.links):
            spot = tab_ref[row, tab_ref[plan.own_row + row, k]]
            spots[g].append(spot)
            fetched[g, k * rows : (k + 1) * rows, :] = arrived[spot]
    coupled = []
    for g in group:
        wide = jnp.dot(panel_ref[g], fetched[g], preferred_element_type=jnp.float32)
        if mixed:
            wide = mix_in(extra[0][g], wide, extra[1][...])
        else:
            refs[-5][g] = wide
        coupled.append(wide.astype(jnp.bfloat16))
    whitened = [narrow_dot(factor_ref[g], coupled[g]) for g in group]
    smoothed = [narrow_dot(whitened[g], factor_ref[g], 0) for g in group]
    for g in group:
        projected = narrow_dot(smoothed[g], panel_ref[g])
        for k in range(plan.links):
            leaving[spots[g][k]] = projected[:, k * rows : (k + 1) * rows]

    @pl.when(arc == pl.num_programs(0) - 1)
    def _():
        for s in range(count):
            outward(s).start()
        for s in range(count):
            outward(s).wait()


def run_arcs(plan, tab, arrived, coupling_panel, inv_factor, extra):
    arcs, arc_rows, width = coupling_panel.shape
    block = arrived[0].shape[1:]
    total = plan.rings * plan.slots
    group = GROUP if arcs % GROUP == 0 else 1
    anywhere = pl.BlockSpec(memory_space=pl.ANY)
    wide = pl.BlockSpec((group, arc_rows, block[1]), lambda i, t: (i, 0, 0))
    return pl.pallas_call(
        functools.partial(arcs_kernel, plan, bool(extra)),
        grid_spec=pltpu.PrefetchScalarGridSpec(
            num_scalar_prefetch=1,
            grid=(arcs // group,),
            in_specs=[anywhere] * (plan.rings * plan.plane)
            + [
                pl.BlockSpec((group, arc_rows, width), lambda i, t: (i, 0, 0)),
                pl.BlockSpec((group, arc_rows, arc_rows), lambda i, t: (i, 0, 0)),
            ]
            + ([wide, pl.BlockSpec(extra[1].shape, lambda i, t: (0, 0))] if extra else []),
            out_specs=[anywhere] * (plan.rings * plan.plane) + ([] if extra else [wide]),
            scratch_shapes=[
                pltpu.VMEM((total,) + block, jnp.bfloat16),
                pltpu.VMEM((total,) + block, jnp.bfloat16),
                pltpu.VMEM((group, width, block[1]), jnp.bfloat16),
                pltpu.SemaphoreType.DMA((plan.rings * plan.plane,)),
            ],
        ),
        out_shape=[jax.ShapeDtypeStruct((plan.cap,) + block, jnp.bfloat16)]
        * (plan.rings * plan.plane)
        + ([] if extra else [jax.ShapeDtypeStruct((arcs, arc_rows, block[1]), jnp.float32)]),
        name="arcs",
    )(tab, *arrived, coupling_panel, inv_factor, *extra)


def add_up(plan, step, me_ref, held_ref, got_refs, part_refs, acc):
    here = lax.rem(me_ref[0], plan.plane)
    start = jnp.zeros(acc.shape, jnp.float32)
    for part_ref in part_refs:
        start = start + part_ref[...].astype(jnp.float32)
    acc[...] = start
    for offset, got_ref in enumerate(got_refs):
        q = plan.source_traced(here, offset)

        @pl.loop(0, plan.cap)
        def _(r):
            held = held_ref[step, r * plan.plane + q]

            @pl.when(held > 0)
            def _():
                acc[held - 1] += got_ref[r].astype(jnp.float32)


def fold_kernel(plan, step, me_ref, held_ref, *refs):
    got_refs, part_refs = refs[: plan.plane], refs[plan.plane : -2]
    out_ref, acc = refs[-2], refs[-1]
    add_up(plan, step, me_ref, held_ref, got_refs, part_refs, acc)
    out_ref[...] = acc[...].astype(out_ref.dtype)


def image_kernel(plan, both, me_ref, held_ref, field_ref, prior_ref, *refs):
    outputs = 4 if both else 3
    got_refs, part_refs = refs[: plan.plane], refs[plan.plane : -outputs]
    image_ref, gram_ref, acc = refs[-outputs], refs[1 - outputs], refs[-1]
    add_up(plan, 0, me_ref, held_ref, got_refs, part_refs, acc)
    rows = acc.shape[1]
    for b in range(plan.blocks):
        image = acc[b].T + prior_ref[:, b : b + 1] * field_ref[b]
        image_ref[b] = image
        if both:
            refs[-2][b] = (field_ref[b] - BLEND * image).astype(jnp.bfloat16)
    gram_ref[...] = jnp.zeros_like(gram_ref)
    batch = max(n for n in range(1, 6) if plan.blocks % n == 0)

    @pl.loop(0, plan.blocks, step=batch)
    def _(b):
        field = field_ref[pl.ds(b, batch)].reshape(batch * rows, -1)
        image = image_ref[pl.ds(b, batch)].reshape(batch * rows, -1)
        gram_ref[0] += gram_of(field, image)
        if both:
            gram_ref[1] += gram_of(image, image)


def gram_of(left, right):
    return lax.dot_general(
        left,
        right,
        (((0,), (0,)), ((), ())),
        precision=lax.Precision.HIGHEST,
        preferred_element_type=jnp.float32,
    )


def fold_specs(args):
    return [pl.BlockSpec(memory_space=SMEM)] * 2 + [pl.BlockSpec(memory_space=VMEM)] * (
        len(args) - 2
    )


def fold(plan, step, me, held, got, parts):
    shape = (plan.blocks,) + got[0].shape[1:]
    args = (me, held, got[0], *in_vmem(*got[1:], *parts))
    return pl.pallas_call(
        functools.partial(fold_kernel, plan, step),
        out_shape=pltpu.VMEM(shape, jnp.bfloat16),
        in_specs=fold_specs(args),
        out_specs=pl.BlockSpec(memory_space=VMEM),
        scratch_shapes=[pltpu.VMEM(shape, jnp.float32)],
        compiler_params=SMALL,
        name="fold",
    )(*args)


def fold_image(plan, me, held, got, parts, field, prior_cols, both):
    shape, cols = field.shape, field.shape[2]
    args = (me, held, field, prior_cols, got[0], *in_vmem(*got[1:], *parts))
    return pl.pallas_call(
        functools.partial(image_kernel, plan, both),
        out_shape=[
            jax.ShapeDtypeStruct(shape, jnp.float32),
            jax.ShapeDtypeStruct((2 if both else 1, cols, cols), jnp.float32),
        ]
        + ([pltpu.VMEM(shape, jnp.bfloat16)] if both else []),
        in_specs=fold_specs(args),
        out_specs=[pl.BlockSpec(memory_space=VMEM)] * (3 if both else 2),
        scratch_shapes=[pltpu.VMEM(shape, jnp.float32)],
        compiler_params=SMALL,
        name="image",
    )(*args)


def update_kernel(field_ref, image_ref, sol_ref, res_ref, step_ref, sol_out, res_out):
    blocks, rows, cols = field_ref.shape
    step = step_ref[...]
    size = (blocks * rows, cols)
    moved = times_high(field_ref[...].reshape(size), step).reshape(field_ref.shape)
    sol_out[...] = sol_ref[...] + moved
    moved = times_high(image_ref[...].reshape(size), step).reshape(field_ref.shape)
    res_out[...] = res_ref[...] - moved


def update(field, image, solution_field, residual, step_mat):
    blocks, rows, cols = field.shape
    batch = max(n for n in range(1, 5) if blocks % n == 0)
    spec = pl.BlockSpec((batch, rows, cols), lambda i: (i, 0, 0))
    return pl.pallas_call(
        update_kernel,
        grid=(blocks // batch,),
        out_shape=[jax.ShapeDtypeStruct(field.shape, jnp.float32)] * 2,
        in_specs=[spec] * 4 + [pl.BlockSpec((cols, cols), lambda i: (0, 0))],
        out_specs=[spec] * 2,
        name="update",
    )(field, image, solution_field, residual, step_mat)


def identity(size):
    rows = lax.broadcasted_iota(jnp.int32, (size, size), 0)
    lanes = lax.broadcasted_iota(jnp.int32, (size, size), 1)
    return jnp.where(rows == lanes, 1.0, 0.0)


def eliminate(matrix):
    size = matrix.shape[0]
    rows = lax.broadcasted_iota(jnp.int32, (size, size), 0)
    lanes = lax.broadcasted_iota(jnp.int32, (size, size), 1)

    def pivot(k, matrix):
        on_row, on_lane = rows == k, lanes == k
        column = jnp.sum(jnp.where(on_lane, matrix, 0.0), axis=1, keepdims=True)
        row = jnp.sum(jnp.where(on_row, matrix, 0.0), axis=0, keepdims=True)
        scale = 1.0 / jnp.sum(jnp.where(on_lane[:1], row, 0.0), axis=1, keepdims=True)
        row = jnp.where(on_lane[:1], 1.0, row) * scale
        rest = jnp.where(on_lane, 0.0, matrix) - column * row
        return jnp.where(on_row, row, rest)

    return lax.fori_loop(0, size, pivot, matrix)


def invert_into(out_refs, matrices):
    size = matrices[0].shape[0]
    eye = identity(size)
    scales, scaled = [], []
    for matrix in matrices:
        diagonal = eye * matrix
        down = lax.rsqrt(jnp.sum(diagonal, axis=1, keepdims=True))
        along = lax.rsqrt(jnp.sum(diagonal, axis=0, keepdims=True))
        scales.append((down, along))
        scaled.append(matrix * down * along)
    off = [matrix - eye for matrix in scaled]
    second = [times_high(e, e) for e in off]
    fourth = [times_high(e, e) for e in second]
    third = [times_high(e, f) for e, f in zip(off, second)]
    guess = [eye - e + f - g for e, f, g in zip(off, second, third)]
    guess = [x + times_high(x, e) for x, e in zip(guess, fourth)]
    left = [eye - times_high(a, x) for a, x in zip(scaled, guess)]
    guess = [x + times_high(x, r) for x, r in zip(guess, left)]
    for out_ref, x, r, a, (down, along) in zip(out_refs, guess, left, scaled, scales):
        out_ref[...] = x * down * along
        worst = jnp.max(jnp.sum(jnp.abs(r), axis=1, keepdims=True))

        @pl.when(jnp.logical_not(worst < 1e-3))
        def _():
            y = eliminate(a)
            y = y + times_high(y, eye - times_high(a, y))
            out_ref[...] = y * down * along


def step_kernel(
    grams_ref, res_ref, step_ref, beta_ref, new_ref, mix_ref, first_inv, second_inv
):
    res, cross, image = res_ref[...], grams_ref[0], grams_ref[1]
    invert_into([first_inv, second_inv], [0.5 * (cross + cross.T), 0.5 * (res + res.T)])
    step = times_high(first_inv[...], res)
    step_ref[...] = step
    moved = times_high(cross, step)
    new = res - moved.T - moved + times_high(step.T, times_high(image, step))
    new_ref[...] = new
    beta = times_high(second_inv[...], new)
    beta_ref[...] = beta
    size = beta.shape[0]
    mix_ref[size:, :] = step * (1.0 / BLEND)
    mix_ref[:size, :] = identity(size) + beta - step * (1.0 / BLEND)


def last_kernel(grams_ref, res_ref, step_ref, first_inv):
    curv = grams_ref[0]
    invert_into([first_inv], [0.5 * (curv + curv.T)])
    step_ref[...] = times_high(first_inv[...], res_ref[...])


def small_solve(kernel, args, outputs, scratch, tall=0):
    shape = args[0].shape[1:]
    double = (2 * shape[0], shape[1])
    return pl.pallas_call(
        kernel,
        out_shape=[jax.ShapeDtypeStruct(shape, jnp.float32)] * outputs
        + [jax.ShapeDtypeStruct(double, jnp.float32)] * tall,
        scratch_shapes=[pltpu.VMEM(shape, jnp.float32)] * scratch,
        compiler_params=SMALL,
        name="solve",
    )(*args)


def trade_plane(plan, buffers):
    moved = [None] * plan.plane
    moved[0] = buffers[0]
    for offset in range(plan.plane - 1, 0, -1):
        moved[offset] = lax.ppermute(buffers[offset], AXES, plan.shift_plane(offset))
    return moved


def gate_kernel(in_ref, out_ref):
    out_ref[0] = in_ref[0]


def gate(me):
    return pl.pallas_call(
        gate_kernel,
        out_shape=jax.ShapeDtypeStruct(me.shape, me.dtype),
        in_specs=[pl.BlockSpec(memory_space=SMEM)],
        out_specs=pl.BlockSpec(memory_space=SMEM),
        compiler_params=SMALL,
        name="gate",
    )(me)


def apply_schur(
    plan, me, tab, held, chunk, field, prior_cols, coupling_panel, inv_factor, extra=()
):
    arrived, both = [], not extra
    for s in range(plan.rings):
        following = None
        if s + 1 < plan.rings:
            following = lax.ppermute(chunk, AXES, plan.ring)
        chosen = pick(plan, s, me, held, chunk)
        arrived += trade_plane(plan, chosen)
        if s + 1 < plan.rings:
            me = gate(me)
        chunk = following
    leaving = run_arcs(plan, tab, arrived, coupling_panel, inv_factor, extra)
    moved, folded = {}, []
    for j, s in enumerate(plan.back):
        buffers = leaving[s * plan.plane : (s + 1) * plan.plane]
        if j >= 2:
            *buffers, _ = lax.optimization_barrier((*buffers, folded[j - 2]))
        got = trade_plane(plan, buffers)
        sources = [moved[source] for source in plan.follows(s)]
        if s:
            me = gate(me)
        if s == 0:
            made = fold_image(plan, me, held, got, sources, field, prior_cols, both)
            return (*made, leaving[-1], me)
        folded.append(fold(plan, s, me, held, got, sources))
        moved[s] = lax.ppermute(folded[j], AXES, plan.shift_back(s))


def per_device(
    mesh, right_side, prior_diag, inv_factor, coupling_panel, coupling_owner, coupling_block
):
    plan = Plan(mesh, coupling_panel.shape[0], coupling_owner.shape[1], right_side.shape[0])
    me = lax.axis_index(AXES).astype(jnp.int32).reshape(1)
    tab, held = make_tables(plan, me, coupling_owner, coupling_block)
    prior_cols = prior_diag.T
    common = (prior_cols, coupling_panel, inv_factor)
    rounded = right_side.astype(jnp.bfloat16)
    res_gram = sum_all(inner_gram(right_side, right_side)[None])[0]
    image_vec, grams, blend, coupled, me = apply_schur(
        plan, me, tab, held, rounded, right_side, *common
    )
    grams, res_gram = lax.optimization_barrier((grams, res_gram))
    grams = sum_all(grams)
    step_mat, beta_mat, res_gram, mix = small_solve(
        step_kernel, (grams, res_gram), 3, 2, 1
    )
    solution_field = combine_cols(right_side, step_mat)
    residual = right_side - combine_cols(image_vec, step_mat)
    direction = residual + combine_cols(right_side, beta_mat)
    image_vec, grams, _, _ = apply_schur(
        plan, me, tab, held, blend, direction, *common, extra=(coupled, mix)
    )
    (step_mat,) = small_solve(last_kernel, (sum_all(grams), res_gram), 1, 1)
    return tuple(update(direction, image_vec, solution_field, residual, step_mat))


def solution(mesh):
    in_specs = (
        P(AXES, None, None),
        P(AXES, None),
        P(AXES, None, None),
        P(AXES, None, None),
        P(),
        P(),
    )
    out_specs = (P(AXES, None, None), P(AXES, None, None))
    return jax.shard_map(
        functools.partial(per_device, mesh),
        mesh=mesh,
        in_specs=in_specs,
        out_specs=out_specs,
        check_vma=False,
    )
```

```python
import functools

import jax
import jax.numpy as jnp
from jax import lax
from jax.experimental import pallas as pl
from jax.experimental.pallas import tpu as pltpu
from jax.sharding import PartitionSpec as P


BLEND = 0.5
GROUP = 4
AXES = ("arc", "vec")
SMEM = pltpu.MemorySpace.SMEM
VMEM = pltpu.MemorySpace.VMEM


SMALL = pltpu.CompilerParams(vmem_limit_bytes=16 << 20)


def in_vmem(*arrays):
    placed = [pltpu.with_memory_space_constraint(array, pltpu.VMEM) for array in arrays]
    return placed


def inner_gram(left, right):
    return jnp.einsum("grc,grd->cd", left, right, precision=lax.Precision.HIGHEST)


def combine_cols(field, weights):
    return jnp.einsum("grc,cd->grd", field, weights, precision=lax.Precision.HIGHEST)


def times_high(left, right):
    return jnp.dot(left, right, precision=lax.Precision.HIGHEST)


def trade(buffer):
    return lax.all_to_all(buffer, AXES, split_axis=0, concat_axis=0, tiled=True)


def sum_all(grams):
    device_count = lax.axis_size(AXES)
    count, rows, cols = grams.shape
    pieces = grams.reshape(device_count, count * rows // device_count, cols)
    pieces = trade(pieces)
    shared = jnp.broadcast_to(jnp.sum(pieces, axis=0)[None], pieces.shape)
    return trade(shared).reshape(grams.shape)


class Plan:
    def __init__(self, mesh, arcs_here, links, blocks_here):
        arc, vec = mesh.shape["arc"], mesh.shape["vec"]
        half = max(1, vec // 2)
        self.rings = arc // half if arc % half == 0 else arc
        self.devices = arc * vec
        self.plane = self.devices // self.rings
        self.arcs, self.links, self.blocks = arcs_here, links, blocks_here
        entries = arcs_here * links
        self.cap = (entries + self.devices - 1) // self.devices + 1
        self.slots = self.plane * self.cap
        self.own_row = arcs_here
        self.padded = -(-self.slots // 128) * 128
        self.order = [self.plane_at(i) for i in range(self.rings)]
        self.ring = [
            (self.order[i] * self.plane + p, self.order[(i + 1) % self.rings] * self.plane + p)
            for i in range(self.rings)
            for p in range(self.plane)
        ]
        self.paired = self.plane & (self.plane - 1) == 0
        half = self.rings // 2
        onward, reverse = list(range(half, 0, -1)), list(range(half + 1, self.rings))
        self.back = []
        while onward or reverse:
            self.back += onward[:1] + reverse[:1]
            onward, reverse = onward[1:], reverse[1:]
        self.back.append(0)

    def follows(self, step):
        half = self.rings // 2
        sources = [step + 1] if step < half else []
        if step > half + 1 or (step == 0 and self.rings > half + 1):
            sources.append((step - 1) % self.rings)
        return sources

    def shift_back(self, step):
        move = 1 if step <= self.rings // 2 else -1
        return [
            (self.order[i] * self.plane + p, self.order[(i - move) % self.rings] * self.plane + p)
            for i in range(self.rings)
            for p in range(self.plane)
        ]

    def target(self, p, offset):
        return p ^ offset if self.paired else (p + offset) % self.plane

    def target_traced(self, p, offset):
        return p ^ offset if self.paired else lax.rem(p + offset, self.plane)

    def source_traced(self, p, offset):
        return p ^ offset if self.paired else lax.rem(p - offset + self.plane, self.plane)

    def shift_plane(self, offset):
        return [
            (z * self.plane + p, z * self.plane + self.target(p, offset))
            for z in range(self.rings)
            for p in range(self.plane)
        ]

    def plane_at(self, place):
        return 2 * place if 2 * place < self.rings else 2 * self.rings - 1 - 2 * place

    def place_of(self, z):
        half = lax.div(z, 2)
        return jnp.where(lax.rem(z, 2) == 0, half, self.rings - 1 - half)

    def source_plane(self, me, step):
        place = self.place_of(lax.div(me, self.plane))
        place = lax.rem(place - step + self.rings, self.rings)
        doubled = 2 * place
        return jnp.where(doubled < self.rings, doubled, 2 * self.rings - 1 - doubled)


def tables_kernel(
    plan, me_ref, owner_cols, block_cols, tab_ref, held_ref, owner_ref, block_ref, all_ref
):
    me = me_ref[0]
    arcs, links, lanes = plan.arcs, plan.links, tab_ref.shape[1]
    z = lax.div(me, plan.plane)
    span = plan.plane * arcs
    first = pl.multiple_of(z * span, span)
    owner_ref[...] = owner_cols[:, pl.ds(first, span)].T
    block_ref[...] = block_cols[:, pl.ds(first, span)].T
    owners = lax.broadcasted_iota(jnp.int32, (arcs, lanes), 1)
    low = lax.broadcasted_iota(jnp.int32, (arcs, arcs), 0)
    high = lax.broadcasted_iota(jnp.int32, (arcs, arcs), 1)
    before = (high < low).astype(jnp.float32)

    def incidence(row):
        owner = owner_ref[pl.ds(row, arcs), :]
        block = block_ref[pl.ds(row, arcs), :]
        named = jnp.zeros((arcs, lanes), jnp.float32)
        held = jnp.zeros((arcs, lanes), jnp.int32)
        for k in range(links):
            same = owner[:, k : k + 1] == owners
            named = jnp.where(same, 1.0, named)
            held = jnp.where(same, block[:, k : k + 1] + 1, held)
        rank = jnp.dot(before, named, preferred_element_type=jnp.float32).astype(jnp.int32)
        return held, rank

    all_ref[...] = jnp.zeros_like(all_ref)
    for q in range(plan.plane):
        held, rank = incidence(q * arcs)
        for r in range(plan.cap):
            at_rank = jnp.where(rank == r, held, 0)
            all_ref[r * plan.plane + q : r * plan.plane + q + 1, :] = jnp.sum(
                at_rank, axis=0, keepdims=True
            )
    columns = jnp.zeros((held_ref.shape[1], 128), jnp.int32)
    wide = lax.broadcasted_iota(jnp.int32, columns.shape, 1)
    across = lax.broadcasted_iota(jnp.int32, all_ref.shape, 1)
    for s in range(plan.rings):
        column = plan.source_plane(me, s) * plan.plane + lax.rem(me, plan.plane)
        picked = jnp.sum(jnp.where(across == column, all_ref[...], 0), axis=1, keepdims=True)
        columns = jnp.where(wide == s, picked, columns)
    held_ref[...] = columns.T[: held_ref.shape[0]]
    row = pl.multiple_of(lax.rem(me, plan.plane) * arcs, arcs)
    held, rank = incidence(row)
    place = plan.place_of(z)
    other = plan.place_of(lax.div(owners, plan.plane))
    step = lax.rem(place - other + plan.rings, plan.rings)
    here, there = lax.rem(me, plan.plane), lax.rem(owners, plan.plane)
    offset = here ^ there if plan.paired else lax.rem(here - there + plan.plane, plan.plane)
    slot = step * plan.slots + offset * plan.cap + rank
    tab_ref[:arcs, :] = slot
    mine = jnp.zeros((arcs, lanes), jnp.int32)
    owner = owner_ref[pl.ds(row, arcs), :]
    for k in range(links):
        mine = jnp.where(owners == k, owner[:, k : k + 1], mine)
    tab_ref[plan.own_row : plan.own_row + arcs, :] = mine


def make_tables(plan, me, coupling_owner, coupling_block):
    lanes = -(-plan.devices // 128) * 128
    return pl.pallas_call(
        functools.partial(tables_kernel, plan),
        out_shape=[
            jax.ShapeDtypeStruct((2 * plan.arcs, lanes), jnp.int32),
            jax.ShapeDtypeStruct((-(-plan.rings // 8) * 8, plan.padded), jnp.int32),
        ],
        in_specs=[
            pl.BlockSpec(memory_space=SMEM),
            pl.BlockSpec(memory_space=VMEM),
            pl.BlockSpec(memory_space=VMEM),
        ],
        out_specs=[pl.BlockSpec(memory_space=VMEM)] * 2,
        scratch_shapes=[pltpu.VMEM((plan.plane * plan.arcs, plan.links), jnp.int32)] * 2
        + [pltpu.VMEM((plan.padded, lanes), jnp.int32)],
        compiler_params=SMALL,
        name="tables",
    )(me, coupling_owner.T, coupling_block.T)


def pick_kernel(plan, step, me_ref, held_ref, chunk_ref, *out_refs):
    here = lax.rem(me_ref[0], plan.plane)
    for offset, out_ref in enumerate(out_refs):
        q = plan.target_traced(here, offset)
        for r in range(plan.cap):
            block = jnp.maximum(held_ref[step, r * plan.plane + q] - 1, 0)
            out_ref[r] = chunk_ref[block]


def pick(plan, step, me, held, chunk):
    shape = (plan.cap,) + chunk.shape[1:]
    return pl.pallas_call(
        functools.partial(pick_kernel, plan, step),
        out_shape=[jax.ShapeDtypeStruct(shape, chunk.dtype)]
        + [pltpu.VMEM(shape, chunk.dtype)] * (plan.plane - 1),
        in_specs=[
            pl.BlockSpec(memory_space=SMEM),
            pl.BlockSpec(memory_space=SMEM),
            pl.BlockSpec(memory_space=VMEM),
        ],
        out_specs=[pl.BlockSpec(memory_space=VMEM)] * plan.plane,
        compiler_params=SMALL,
        name="pick",
    )(me, held, *in_vmem(chunk))


def narrow_dot(left, right, contract=1):
    product = lax.dot_general(
        left, right, (((contract,), (0,)), ((), ())), preferred_element_type=jnp.float32
    )
    return product.astype(jnp.bfloat16)


def split_dot(left, right):
    def halves(wide):
        high = wide.astype(jnp.bfloat16)
        return high, (wide - high.astype(jnp.float32)).astype(jnp.bfloat16)

    def product(left, right):
        return jnp.dot(left, right, preferred_element_type=jnp.float32)

    high, low = halves(left)
    right_high, right_low = halves(right)
    return product(high, right_high) + (product(high, right_low) + product(low, right_high))


def arcs_kernel(plan, mixed, tab_ref, *refs):
    count, cap = plan.rings * plan.plane, plan.cap
    arrived_refs = refs[:count]
    panel_ref, factor_ref = refs[count], refs[count + 1]
    extra = refs[count + 2 : -4 - count] if mixed else ()
    out_refs = refs[-4 - count : -4] if mixed else refs[count + 2 : -5]
    arrived, leaving, fetched, sems = refs[-4:]
    arc = pl.program_id(0)
    rows = arrived.shape[1]

    def inward(s):
        return pltpu.make_async_copy(
            arrived_refs[s], arrived.at[pl.ds(s * cap, cap)], sems.at[s]
        )

    def outward(s):
        return pltpu.make_async_copy(
            leaving.at[pl.ds(s * cap, cap)], out_refs[s], sems.at[s]
        )

    @pl.when(arc == 0)
    def _():
        for s in range(count):
            inward(s).start()
        for s in range(count):
            inward(s).wait()

    group = range(panel_ref.shape[0])
    spots = [[] for _ in group]
    for g in group:
        row = arc * len(group) + g
        for k in range(plan.links):
            spot = tab_ref[row, tab_ref[plan.own_row + row, k]]
            spots[g].append(spot)
            fetched[g, k * rows : (k + 1) * rows, :] = arrived[spot]
    coupled = []
    for g in group:
        wide = jnp.dot(panel_ref[g], fetched[g], preferred_element_type=jnp.float32)
        if mixed:
            wide = split_dot(jnp.concatenate([extra[0][g], wide], axis=1), extra[1][...])
        else:
            refs[-5][g] = wide
        coupled.append(wide.astype(jnp.bfloat16))
    whitened = [narrow_dot(factor_ref[g], coupled[g]) for g in group]
    smoothed = [narrow_dot(whitened[g], factor_ref[g], 0) for g in group]
    for g in group:
        projected = narrow_dot(smoothed[g], panel_ref[g])
        for k in range(plan.links):
            leaving[spots[g][k]] = projected[:, k * rows : (k + 1) * rows]

    @pl.when(arc == pl.num_programs(0) - 1)
    def _():
        for s in range(count):
            outward(s).start()
        for s in range(count):
            outward(s).wait()


def run_arcs(plan, tab, arrived, coupling_panel, inv_factor, extra):
    arcs, arc_rows, width = coupling_panel.shape
    block = arrived[0].shape[1:]
    total = plan.rings * plan.slots
    group = GROUP if arcs % GROUP == 0 else 1
    anywhere = pl.BlockSpec(memory_space=pl.ANY)
    wide = pl.BlockSpec((group, arc_rows, block[1]), lambda i, t: (i, 0, 0))
    return pl.pallas_call(
        functools.partial(arcs_kernel, plan, bool(extra)),
        grid_spec=pltpu.PrefetchScalarGridSpec(
            num_scalar_prefetch=1,
            grid=(arcs // group,),
            in_specs=[anywhere] * (plan.rings * plan.plane)
            + [
                pl.BlockSpec((group, arc_rows, width), lambda i, t: (i, 0, 0)),
                pl.BlockSpec((group, arc_rows, arc_rows), lambda i, t: (i, 0, 0)),
            ]
            + ([wide, pl.BlockSpec(extra[1].shape, lambda i, t: (0, 0))] if extra else []),
            out_specs=[anywhere] * (plan.rings * plan.plane) + ([] if extra else [wide]),
            scratch_shapes=[
                pltpu.VMEM((total,) + block, jnp.bfloat16),
                pltpu.VMEM((total,) + block, jnp.bfloat16),
                pltpu.VMEM((group, width, block[1]), jnp.bfloat16),
                pltpu.SemaphoreType.DMA((plan.rings * plan.plane,)),
            ],
        ),
        out_shape=[jax.ShapeDtypeStruct((plan.cap,) + block, jnp.bfloat16)]
        * (plan.rings * plan.plane)
        + ([] if extra else [jax.ShapeDtypeStruct((arcs, arc_rows, block[1]), jnp.float32)]),
        name="arcs",
    )(tab, *arrived, coupling_panel, inv_factor, *extra)


def add_up(plan, step, me_ref, held_ref, got_refs, part_refs, acc):
    here = lax.rem(me_ref[0], plan.plane)
    start = jnp.zeros(acc.shape, jnp.float32)
    for part_ref in part_refs:
        start = start + part_ref[...].astype(jnp.float32)
    acc[...] = start
    for offset, got_ref in enumerate(got_refs):
        q = plan.source_traced(here, offset)
        for r in range(plan.cap):
            held = held_ref[step, r * plan.plane + q]

            @pl.when(held > 0)
            def _():
                acc[held - 1] += got_ref[r].astype(jnp.float32)


def fold_kernel(plan, step, me_ref, held_ref, *refs):
    got_refs, part_refs = refs[: plan.plane], refs[plan.plane : -2]
    out_ref, acc = refs[-2], refs[-1]
    add_up(plan, step, me_ref, held_ref, got_refs, part_refs, acc)
    out_ref[...] = acc[...].astype(out_ref.dtype)


def image_kernel(plan, both, me_ref, held_ref, field_ref, prior_ref, *refs):
    outputs = 4 if both else 3
    got_refs, part_refs = refs[: plan.plane], refs[plan.plane : -outputs]
    image_ref, gram_ref, acc = refs[-outputs], refs[1 - outputs], refs[-1]
    add_up(plan, 0, me_ref, held_ref, got_refs, part_refs, acc)
    rows = acc.shape[1]
    for b in range(plan.blocks):
        image = acc[b].T + prior_ref[:, b : b + 1] * field_ref[b]
        image_ref[b] = image
        if both:
            refs[-2][b] = (field_ref[b] - BLEND * image).astype(jnp.bfloat16)
    gram_ref[...] = jnp.zeros_like(gram_ref)
    batch = max(n for n in range(1, 6) if plan.blocks % n == 0)

    @pl.loop(0, plan.blocks, step=batch)
    def _(b):
        field = field_ref[pl.ds(b, batch)].reshape(batch * rows, -1)
        image = image_ref[pl.ds(b, batch)].reshape(batch * rows, -1)
        gram_ref[0] += gram_of(field, image)
        if both:
            gram_ref[1] += gram_of(image, image)


def gram_of(left, right):
    return lax.dot_general(
        left,
        right,
        (((0,), (0,)), ((), ())),
        precision=lax.Precision.HIGHEST,
        preferred_element_type=jnp.float32,
    )


def fold_specs(args):
    return [pl.BlockSpec(memory_space=SMEM)] * 2 + [pl.BlockSpec(memory_space=VMEM)] * (
        len(args) - 2
    )


def fold(plan, step, me, held, got, parts):
    shape = (plan.blocks,) + got[0].shape[1:]
    args = (me, held, got[0], *in_vmem(*got[1:], *parts))
    return pl.pallas_call(
        functools.partial(fold_kernel, plan, step),
        out_shape=pltpu.VMEM(shape, jnp.bfloat16),
        in_specs=fold_specs(args),
        out_specs=pl.BlockSpec(memory_space=VMEM),
        scratch_shapes=[pltpu.VMEM(shape, jnp.float32)],
        compiler_params=SMALL,
        name="fold",
    )(*args)


def fold_image(plan, me, held, got, parts, field, prior_cols, both):
    shape, cols = field.shape, field.shape[2]
    args = (me, held, field, prior_cols, got[0], *in_vmem(*got[1:], *parts))
    return pl.pallas_call(
        functools.partial(image_kernel, plan, both),
        out_shape=[
            jax.ShapeDtypeStruct(shape, jnp.float32),
            jax.ShapeDtypeStruct((2 if both else 1, cols, cols), jnp.float32),
        ]
        + ([pltpu.VMEM(shape, jnp.bfloat16)] if both else []),
        in_specs=fold_specs(args),
        out_specs=[pl.BlockSpec(memory_space=VMEM)] * (3 if both else 2),
        scratch_shapes=[pltpu.VMEM(shape, jnp.float32)],
        compiler_params=SMALL,
        name="image",
    )(*args)


def update_kernel(field_ref, image_ref, sol_ref, res_ref, step_ref, sol_out, res_out):
    blocks, rows, cols = field_ref.shape
    step = step_ref[...]
    size = (blocks * rows, cols)
    moved = split_dot(field_ref[...].reshape(size), step).reshape(field_ref.shape)
    sol_out[...] = sol_ref[...] + moved
    moved = split_dot(image_ref[...].reshape(size), step).reshape(field_ref.shape)
    res_out[...] = res_ref[...] - moved


def update(field, image, solution_field, residual, step_mat):
    blocks, rows, cols = field.shape
    batch = max(n for n in range(1, 5) if blocks % n == 0)
    spec = pl.BlockSpec((batch, rows, cols), lambda i: (i, 0, 0))
    return pl.pallas_call(
        update_kernel,
        grid=(blocks // batch,),
        out_shape=[jax.ShapeDtypeStruct(field.shape, jnp.float32)] * 2,
        in_specs=[spec] * 4 + [pl.BlockSpec((cols, cols), lambda i: (0, 0))],
        out_specs=[spec] * 2,
        name="update",
    )(field, image, solution_field, residual, step_mat)


def identity(size):
    rows = lax.broadcasted_iota(jnp.int32, (size, size), 0)
    lanes = lax.broadcasted_iota(jnp.int32, (size, size), 1)
    return jnp.where(rows == lanes, 1.0, 0.0)


def eliminate(matrix):
    size = matrix.shape[0]
    rows = lax.broadcasted_iota(jnp.int32, (size, size), 0)
    lanes = lax.broadcasted_iota(jnp.int32, (size, size), 1)

    def pivot(k, matrix):
        on_row, on_lane = rows == k, lanes == k
        column = jnp.sum(jnp.where(on_lane, matrix, 0.0), axis=1, keepdims=True)
        row = jnp.sum(jnp.where(on_row, matrix, 0.0), axis=0, keepdims=True)
        scale = 1.0 / jnp.sum(jnp.where(on_lane[:1], row, 0.0), axis=1, keepdims=True)
        row = jnp.where(on_lane[:1], 1.0, row) * scale
        rest = jnp.where(on_lane, 0.0, matrix) - column * row
        return jnp.where(on_row, row, rest)

    return lax.fori_loop(0, size, pivot, matrix)


def invert_into(out_refs, matrices):
    size = matrices[0].shape[0]
    eye = identity(size)
    scales, scaled = [], []
    for matrix in matrices:
        diagonal = eye * matrix
        down = lax.rsqrt(jnp.sum(diagonal, axis=1, keepdims=True))
        along = lax.rsqrt(jnp.sum(diagonal, axis=0, keepdims=True))
        scales.append((down, along))
        scaled.append(matrix * down * along)
    off = [matrix - eye for matrix in scaled]
    second = [times_high(e, e) for e in off]
    fourth = [times_high(e, e) for e in second]
    third = [times_high(e, f) for e, f in zip(off, second)]
    guess = [eye - e + f - g for e, f, g in zip(off, second, third)]
    guess = [x + times_high(x, e) for x, e in zip(guess, fourth)]
    left = [eye - times_high(a, x) for a, x in zip(scaled, guess)]
    guess = [x + times_high(x, r) for x, r in zip(guess, left)]
    for out_ref, x, r, a, (down, along) in zip(out_refs, guess, left, scaled, scales):
        out_ref[...] = x * down * along
        worst = jnp.max(jnp.sum(jnp.abs(r), axis=1, keepdims=True))

        @pl.when(jnp.logical_not(worst < 1e-3))
        def _():
            y = eliminate(a)
            y = y + times_high(y, eye - times_high(a, y))
            out_ref[...] = y * down * along


def step_kernel(
    grams_ref, res_ref, step_ref, beta_ref, new_ref, mix_ref, first_inv, second_inv
):
    res, cross, image = res_ref[...], grams_ref[0], grams_ref[1]
    invert_into([first_inv, second_inv], [0.5 * (cross + cross.T), 0.5 * (res + res.T)])
    step = times_high(first_inv[...], res)
    step_ref[...] = step
    moved = times_high(cross, step)
    new = res - moved.T - moved + times_high(step.T, times_high(image, step))
    new_ref[...] = new
    beta = times_high(second_inv[...], new)
    beta_ref[...] = beta
    size = beta.shape[0]
    mix_ref[size:, :] = step * (1.0 / BLEND)
    mix_ref[:size, :] = identity(size) + beta - step * (1.0 / BLEND)


def last_kernel(grams_ref, res_ref, step_ref, first_inv):
    curv = grams_ref[0]
    invert_into([first_inv], [0.5 * (curv + curv.T)])
    step_ref[...] = times_high(first_inv[...], res_ref[...])


def small_solve(kernel, args, outputs, scratch, tall=0):
    shape = args[0].shape[1:]
    double = (2 * shape[0], shape[1])
    return pl.pallas_call(
        kernel,
        out_shape=[jax.ShapeDtypeStruct(shape, jnp.float32)] * outputs
        + [jax.ShapeDtypeStruct(double, jnp.float32)] * tall,
        scratch_shapes=[pltpu.VMEM(shape, jnp.float32)] * scratch,
        compiler_params=SMALL,
        name="solve",
    )(*args)


def trade_plane(plan, buffers):
    moved = [None] * plan.plane
    moved[0] = buffers[0]
    for offset in range(plan.plane - 1, 0, -1):
        moved[offset] = lax.ppermute(buffers[offset], AXES, plan.shift_plane(offset))
    return moved


def gate_kernel(in_ref, out_ref):
    out_ref[0] = in_ref[0]


def gate(me):
    return pl.pallas_call(
        gate_kernel,
        out_shape=jax.ShapeDtypeStruct(me.shape, me.dtype),
        in_specs=[pl.BlockSpec(memory_space=SMEM)],
        out_specs=pl.BlockSpec(memory_space=SMEM),
        compiler_params=SMALL,
        name="gate",
    )(me)


def apply_schur(
    plan, me, tab, held, chunk, field, prior_cols, coupling_panel, inv_factor, extra=()
):
    arrived, both = [], not extra
    for s in range(plan.rings):
        following = None
        if s + 1 < plan.rings:
            following = lax.ppermute(chunk, AXES, plan.ring)
        chosen = pick(plan, s, me, held, chunk)
        arrived += trade_plane(plan, chosen)
        if s + 1 < plan.rings:
            me = gate(me)
        chunk = following
    leaving = run_arcs(plan, tab, arrived, coupling_panel, inv_factor, extra)
    moved, folded = {}, []
    for j, s in enumerate(plan.back):
        buffers = leaving[s * plan.plane : (s + 1) * plan.plane]
        if j >= 2:
            *buffers, _ = lax.optimization_barrier((*buffers, folded[j - 2]))
        got = trade_plane(plan, buffers)
        sources = [moved[source] for source in plan.follows(s)]
        if s:
            me = gate(me)
        if s == 0:
            made = fold_image(plan, me, held, got, sources, field, prior_cols, both)
            return (*made, leaving[-1], me)
        folded.append(fold(plan, s, me, held, got, sources))
        moved[s] = lax.ppermute(folded[j], AXES, plan.shift_back(s))


def per_device(
    mesh, right_side, prior_diag, inv_factor, coupling_panel, coupling_owner, coupling_block
):
    plan = Plan(mesh, coupling_panel.shape[0], coupling_owner.shape[1], right_side.shape[0])
    me = lax.axis_index(AXES).astype(jnp.int32).reshape(1)
    tab, held = make_tables(plan, me, coupling_owner, coupling_block)
    prior_cols = prior_diag.T
    common = (prior_cols, coupling_panel, inv_factor)
    rounded = right_side.astype(jnp.bfloat16)
    res_gram = sum_all(inner_gram(right_side, right_side)[None])[0]
    image_vec, grams, blend, coupled, me = apply_schur(
        plan, me, tab, held, rounded, right_side, *common
    )
    grams, res_gram = lax.optimization_barrier((grams, res_gram))
    grams = sum_all(grams)
    step_mat, beta_mat, res_gram, mix = small_solve(
        step_kernel, (grams, res_gram), 3, 2, 1
    )
    solution_field = combine_cols(right_side, step_mat)
    residual = right_side - combine_cols(image_vec, step_mat)
    direction = residual + combine_cols(right_side, beta_mat)
    image_vec, grams, _, _ = apply_schur(
        plan, me, tab, held, blend, direction, *common, extra=(coupled, mix)
    )
    (step_mat,) = small_solve(last_kernel, (sum_all(grams), res_gram), 1, 1)
    return tuple(update(direction, image_vec, solution_field, residual, step_mat))


def solution(mesh):
    in_specs = (
        P(AXES, None, None),
        P(AXES, None),
        P(AXES, None, None),
        P(AXES, None, None),
        P(),
        P(),
    )
    out_specs = (P(AXES, None, None), P(AXES, None, None))
    return jax.shard_map(
        functools.partial(per_device, mesh),
        mesh=mesh,
        in_specs=in_specs,
        out_specs=out_specs,
        check_vma=False,
    )
```
